32 devices in a mesh: row: 16 (over z, y, core), col: 2 (over x).
Axes of the slice: x: 2, y: 2, z: 4, core: 2. Of those that a mesh axis runs over, the one named last changes fastest.
Arguments:
- c_matrix: bfloat16 [2, 3072, 6144], P(None, 'row', 'col'), may hold values from -6 to 6
- beta_values: bfloat16 [1, 48, 6, 128, 128], P(None, 'col'), may hold values from -0.21875 to 0.21875
- beta_rows: int32 [1, 48, 6], P(None, 'col'), may hold values from 0 to 47, as said below
- alpha_values: bfloat16 [1, 2, 16, 4, 192, 192], P(None, None, 'row'), may hold values from -0.21875 to 0.21875
- alpha_rows: int32 [1, 2, 16, 4], P(None, None, 'row'), may hold values from 0 to 31, as said below
- gaps: float32 [2, 3072, 6144], P(None, 'row', 'col'), may hold values from 0.5 to 4
Outputs:
- update: float32 [2, 3072, 6144], P(None, 'row', 'col')
The draws below stay inside these ranges and needn't reach their ends.
Inputs may be any that keep to these rules, and one draw needn't show every extreme that they name: For every k and tile column j, beta_rows[k, j] lists 6 distinct tile rows and its first entry is j. For every k, g, r, alpha_rows[k, g, r] lists 4 distinct tile rows and its first entry is the tile column g * 16 + r.
All inputs are finite; a program needn't handle non-finite values.
Results may differ from the reference program's by a relative error of at most 0.0029.
Values may be sent and summed in bfloat16 or wider, within the bound.
A program may use at most 192 MiB of HBM per device.

```python
import math
import jax
import jax.numpy as jnp
from jax import lax

ORDER = 6144
PAIRS = 1
TILE_B = 128
GROUPS = 2
SPAN = 3072
ATILE = 192
ROWTILES = 16
BTILES = 48
BNZ = 6
ATILES = 32
ANZ = 4


def tile_lists(key, operators, tile_total, listed):
    scores = jax.random.randint(key, (operators, tile_total, tile_total), 0, 1 << 20) * tile_total
    scores = scores + jnp.arange(tile_total, dtype=jnp.int32)
    scores = jnp.where(jnp.eye(tile_total, dtype=bool)[None], -1, scores)
    return jnp.argsort(scores, axis=-1)[..., :listed].astype(jnp.int32)


def draw_beta_rows(key, part):
    return tile_lists(jax.random.fold_in(key, 11), PAIRS, BTILES, BNZ)


def draw_alpha_rows(key, part):
    tile_table = tile_lists(jax.random.fold_in(key, 23), PAIRS, ATILES, ANZ)
    return tile_table.reshape(PAIRS, GROUPS, ROWTILES, ANZ)


def shard_levels(own_key, shape, pieces, low, top_value):
    def one(dim, blocks):
        steps = jax.random.uniform(jax.random.fold_in(jax.random.fold_in(own_key, 6), dim), (blocks,), jnp.float32, low / len(pieces), top_value / len(pieces))
        return jnp.repeat(jnp.exp(steps), shape[dim] // blocks).reshape((-1,) + (1,) * (len(shape) - dim - 1))

    level = one(*pieces[0])
    for cut in pieces[1:]:
        level = level * one(*cut)
    return level


def centred(own_key, shape, spread, reach, pieces=(), kind=jnp.bfloat16):
    drawn = jax.random.normal(own_key, shape, jnp.float32) * spread
    if len(pieces) > 0:
        drawn = shard_levels(own_key, shape, pieces, -0.22, 0.18) * drawn
    return jnp.clip(drawn, min=-reach, max=reach).astype(kind)


def setup_inputs(seed: int = 0) -> dict:
    keys = jax.random.split(jax.random.key(seed), 7)
    return {
        "c_matrix": centred(keys[0], (GROUPS, SPAN, ORDER), 1.0, 6.0, ((1, 16), (2, 2))),
        "beta_values": centred(keys[1], (PAIRS, BTILES, BNZ, TILE_B, TILE_B), (BNZ * TILE_B) ** -0.5, 0.21875, ((1, 2),)),
        "beta_rows": draw_beta_rows(jax.random.fold_in(keys[6], 71), 0),
        "alpha_values": centred(keys[3], (PAIRS, GROUPS, ROWTILES, ANZ, ATILE, ATILE), (ANZ * ATILE) ** -0.5, 0.21875, ((2, 16),)),
        "alpha_rows": draw_alpha_rows(jax.random.fold_in(keys[6], 71), 0),
        "gaps": jnp.clip(jnp.exp(math.log(4.0) - 2.0794415 * jax.random.uniform(keys[5], (GROUPS, SPAN, ORDER), jnp.float32) ** shard_levels(keys[5], (GROUPS, SPAN, ORDER), ((1, 16), (2, 2)), -0.2, 0.2)), 0.5, 4.0),
    }


def reference(c_matrix, beta_values, beta_rows, alpha_values, alpha_rows, gaps):
    c_full = c_matrix.reshape(ORDER, ORDER)
    c_tiled = c_full.reshape(ORDER, BTILES, TILE_B)
    alpha_tiles = alpha_values.reshape(PAIRS, ATILES, ANZ, ATILE, ATILE)
    alpha_lists = alpha_rows.reshape(PAIRS, ATILES, ANZ).astype(jnp.int32)

    def one_pair(summed, inputs):
        beta_tiles, beta_lists, pair_tiles, pair_lists = inputs
        picked = c_tiled[:, beta_lists].astype(jnp.float32)
        product = jnp.einsum("ajzt,jzts->ajs", picked, beta_tiles.astype(jnp.float32))
        rounded = lax.optimization_barrier(product.astype(jnp.bfloat16))
        x_matrix = rounded.astype(jnp.float32).reshape(ATILES, ATILE, ORDER)

        def one_slot(partial_value, slot):
            slot_tiles, slot_rows = slot
            contrib = jnp.einsum("quv,qvn->qun", slot_tiles.astype(jnp.float32), x_matrix)
            return partial_value.at[slot_rows].add(contrib), None

        summed, _ = lax.scan(one_slot, summed, (jnp.moveaxis(pair_tiles, 1, 0), jnp.moveaxis(pair_lists, 1, 0)))
        return summed, None

    start_sum = jnp.zeros((ATILES, ATILE, ORDER), jnp.float32)
    summed, _ = lax.scan(one_pair, start_sum, (beta_values, beta_rows.astype(jnp.int32), alpha_tiles, alpha_lists))
    y_matrix = summed.reshape(ORDER, ORDER)
    sigma = y_matrix + y_matrix.T
    return (sigma / gaps.reshape(ORDER, ORDER)).reshape(GROUPS, SPAN, ORDER)
```

```python
import functools

import jax
import jax.numpy as jnp
from jax import lax
from jax.experimental import pallas as pl
from jax.experimental.pallas import tpu as pltpu
from jax.sharding import PartitionSpec as P

CONTRACT_LAST = (((1,), (1,)), ((), ()))


def beta_kernel(listed, held, rows_ref, c_ref, b_ref, xt_ref):
    k, j = pl.program_id(0), pl.program_id(1)
    width = b_ref.shape[-1]
    picked = []
    for z in range(listed):
        tile = rows_ref[k, j, z]
        owner = tile // held
        start = pl.multiple_of((tile - owner * held) * width, width)
        picked.append(c_ref[owner, :, pl.ds(start, width)])
    lhs = b_ref[0, 0].reshape(listed * width, width)
    product = lax.dot_general(
        lhs, jnp.concatenate(picked, axis=1), (((0,), (1,)), ((), ())),
        preferred_element_type=jnp.float32,
    )
    xt_ref[0] = product.astype(xt_ref.dtype)


def beta_products(gathered, beta_values, beta_rows):
    pairs, tiles, listed, width, _ = beta_values.shape
    owners, rows, columns = gathered.shape
    return pl.pallas_call(
        functools.partial(beta_kernel, listed, columns // width),
        grid_spec=pltpu.PrefetchScalarGridSpec(
            num_scalar_prefetch=1,
            grid=(pairs, tiles),
            in_specs=[
                pl.BlockSpec((owners, rows, columns), lambda k, j, s: (0, 0, 0)),
                pl.BlockSpec((1, 1, listed, width, width), lambda k, j, s: (k, j, 0, 0, 0)),
            ],
            out_specs=pl.BlockSpec((1, width, rows), lambda k, j, s: (k, j, 0)),
        ),
        out_shape=jax.ShapeDtypeStruct((pairs, tiles * width, rows), jnp.bfloat16),
        compiler_params=pltpu.CompilerParams(vmem_limit_bytes=56 << 20),
        name="beta_products",
    )(beta_rows, gathered, beta_values)


def alpha_kernel(groups, rows_ref, a_ref, x_ref, own_ref, mirror_ref, acc_ref):
    r = pl.program_id(0)
    row_devices = pl.num_programs(0)
    pairs = x_ref.shape[2]
    listed, tile = rows_ref.shape[2], acc_ref.shape[1]

    @pl.when(r == 0)
    def _():
        acc_ref[...] = jnp.zeros_like(acc_ref)

    for i in range(x_ref.shape[1]):
        at = r * x_ref.shape[1] + i
        for k in range(pairs):
            parts = [x_ref[c, i, k] for c in range(x_ref.shape[0])]
            merged = jnp.concatenate(parts, axis=1) if len(parts) > 1 else parts[0]
            for g in range(groups):
                x = merged[:, g * tile : (g + 1) * tile]
                slot = k * groups + g

                @pl.loop(0, listed)
                def _(z):
                    acc_ref[rows_ref[at, slot, z]] += lax.dot_general(
                        a_ref[i, slot, z], x, CONTRACT_LAST, preferred_element_type=jnp.float32
                    )

    @pl.when(r == row_devices - 1)
    def _():
        count = acc_ref.shape[0] // groups
        for g in range(groups):
            for to in range(count):
                turned = acc_ref[g * count + to].astype(own_ref.dtype).T
                own_ref[to, :, g * tile : (g + 1) * tile] = turned
                mirror_ref[g, :, to * tile : (to + 1) * tile] = turned


def alpha_products(alpha_all, rows_all, x_strip, groups):
    row_devices, rest = alpha_all.shape[0], alpha_all.shape[1:]
    tile = x_strip.shape[0] * x_strip.shape[-1] // groups
    per = 1
    chunks, _, pairs, strip, chunk = x_strip.shape
    return pl.pallas_call(
        functools.partial(alpha_kernel, groups),
        grid_spec=pltpu.PrefetchScalarGridSpec(
            num_scalar_prefetch=1,
            grid=(row_devices // per,),
            in_specs=[
                pl.BlockSpec((per,) + rest, lambda r, s: (r,) + (0,) * len(rest)),
                pl.BlockSpec((chunks, per, pairs, strip, chunk), lambda r, s: (0, r, 0, 0, 0)),
            ],
            out_specs=[
                pl.BlockSpec((row_devices, strip, groups * tile), lambda r, s: (0, 0, 0)),
                pl.BlockSpec((groups, strip, row_devices * tile), lambda r, s: (0, 0, 0)),
            ],
            scratch_shapes=[pltpu.VMEM((groups * row_devices, tile, strip), jnp.float32)],
        ),
        out_shape=[
            jax.ShapeDtypeStruct((row_devices, strip, groups * tile), jnp.bfloat16),
            jax.ShapeDtypeStruct((groups, strip, row_devices * tile), jnp.bfloat16),
        ],
        compiler_params=pltpu.CompilerParams(vmem_limit_bytes=56 << 20),
        name="alpha_products",
    )(rows_all, alpha_all, x_strip)


def final_kernel(own_ref, mirror_ref, gaps_ref, out_ref):
    own = own_ref[...].T.astype(jnp.float32)
    out_ref[...] = (own + mirror_ref[...].astype(jnp.float32)) / gaps_ref[...]


def final(own, mirror, gaps):
    rows, columns = gaps.shape
    block = next(n for n in (384, 256, 128) if columns % n == 0)
    wide = pl.BlockSpec((rows, block), lambda i: (0, i))
    return pl.pallas_call(
        final_kernel,
        grid=(columns // block,),
        in_specs=[pl.BlockSpec((block, rows), lambda i: (i, 0)), wide, wide],
        out_specs=wide,
        out_shape=jax.ShapeDtypeStruct((rows, columns), jnp.float32),
        name="final",
    )(own, mirror, gaps)


def greet(axes):
    barrier = pltpu.get_barrier_semaphore()
    total = 0
    for axis in axes:
        size, me = lax.axis_size(axis), lax.axis_index(axis)
        total += size - 1

        @pl.loop(1, size)
        def _(off):
            pl.semaphore_signal(
                barrier, inc=1, device_id={axis: lax.rem(me + off, size)},
                device_id_type=pl.DeviceIdType.MESH,
            )

    pl.semaphore_wait(barrier, total)


def remote(src, dst, send_sem, recv_sem, axis, peer):
    return pltpu.make_async_remote_copy(
        src_ref=src, dst_ref=dst, send_sem=send_sem, recv_sem=recv_sem,
        device_id={axis: peer}, device_id_type=pl.DeviceIdType.MESH,
    )


def fused_kernel(chunks, subs, rows_ref, lists_ref, c_ref, b_ref, alpha_ref, own_ref, mirror_ref, *scratch):
    held, sent, xt = scratch[:chunks], scratch[chunks : 2 * chunks], scratch[2 * chunks : 2 * chunks + subs]
    (b_own, flat, a_own, a_all, xr, stack, own_out, mirror_out, list_own, list_all, table, picks,
     load_sem, c_own, c_send, c_recv, x_own, x_send, x_recv, l_own, l_send, l_recv, a_sem,
     up_send, up_recv, down_send, down_recv, y_send, y_recv, core_send, core_recv, t_sem,
     o_own, o_send, o_recv, m_own, m_send, m_recv) = scratch[2 * chunks + subs :]
    row_devices, row = lax.axis_size("row"), lax.axis_index("row")
    col_devices, col = lax.axis_size("col"), lax.axis_index("col")
    rows, columns = c_ref.shape
    tiles, depth, width = b_own.shape
    listed_b = depth // width
    slots, tile, _ = flat.shape
    groups = lists_ref.shape[1]
    listed = slots // groups
    chunk, strip = rows // chunks, columns // row_devices
    part = strip // subs
    chips = row_devices // 2
    per = tiles // chips
    stored = a_own.shape[0]
    lines = row_devices // 4
    chip, core = row // 2, lax.rem(row, 2)
    z, y = row // 4, lax.rem(chip, 2)
    units = [(c, 0, strip) for c in range(chunks - 1)]
    units += [(chunks - 1, s * part, part) for s in range(subs)]

    def own_c(c, t):
        return pltpu.make_async_copy(
            c_ref.at[pl.ds(c * chunk, chunk), pl.ds(pl.multiple_of(t * width, width), width)],
            held[c].at[col * tiles + t], c_own.at[c, t],
        )

    def send_c(c, off, t):
        return remote(
            c_ref.at[pl.ds(c * chunk, chunk), pl.ds(pl.multiple_of(t * width, width), width)],
            held[c].at[col * tiles + t], c_send.at[c, off - 1, t], c_recv.at[c, off - 1, t],
            "col", lax.rem(col + off, col_devices),
        )

    def send_x(u, off, peer):
        c, first, size = units[u]
        start = pl.multiple_of(peer * strip + first, 16)
        return remote(
            sent[c].at[pl.ds(start, size), :], xr.at[c, row, pl.ds(first, size), :],
            x_send.at[u, off - 1], x_recv.at[u, off - 1], "row", peer,
        )

    def own_x(u):
        c, first, size = units[u]
        start = pl.multiple_of(row * strip + first, 16)
        return pltpu.make_async_copy(
            sent[c].at[pl.ds(start, size), :], xr.at[c, row, pl.ds(first, size), :], x_own.at[u]
        )

    def send_own(s, off, peer):
        return remote(
            own_out.at[s, peer], own_ref.at[row, pl.ds(s * part, part), :],
            o_send.at[s, off - 1], o_recv.at[s, off - 1], "row", peer,
        )

    def stay_own(s):
        return pltpu.make_async_copy(
            own_out.at[s, row], own_ref.at[row, pl.ds(s * part, part), :], o_own.at[s]
        )

    def send_mirror(s, off):
        peer = lax.rem(col + off, col_devices)
        return remote(
            mirror_out.at[s, peer], mirror_ref.at[col, pl.ds(s * part, part), :],
            m_send.at[s, off - 1], m_recv.at[s, off - 1], "col", peer,
        )

    def stay_mirror(s):
        return pltpu.make_async_copy(
            mirror_out.at[s, col], mirror_ref.at[col, pl.ds(s * part, part), :], m_own.at[s]
        )

    def send_list(off):
        return remote(
            list_own, list_all.at[row], l_send.at[off - 1], l_recv.at[off - 1], "row",
            lax.rem(row + off, row_devices),
        )

    def reach(i):
        odd = lax.rem(i, 2)
        return chips // 2 + (1 - odd) * (i // 2) - odd * ((i + 1) // 2)

    def pair(i):
        return lax.rem(chip + reach(i), chips)

    def send_pair(send, i):
        for e in range(2):
            send(2 * reach(i) + e - core, 2 * pair(i) + e).start()

    partner, partner_off = row + 1 - 2 * core, 1 + core * (row_devices - 2)

    def block(at_z, at_y, at_core):
        return (at_z * 2 + at_y) * 2 + at_core

    def slab(at):
        return a_all.at[pl.ds(at * stored, stored)]

    def hand(source, at, send_sem, recv_sem, peer):
        return remote(source, slab(at), send_sem, recv_sem, "row", peer)

    def up(step, first=False):
        at = block(z - step, y, core)
        source = a_own if first else slab(at)
        return hand(source, at, up_send.at[step], up_recv.at[step], block(z + 1, y, core))

    def down(step, first=False):
        at = block(z + step, y, core)
        source = a_own if first else slab(at)
        return hand(source, at, down_send.at[step], down_recv.at[step], block(z - 1, y, core))

    def over_y(at_z, first=False):
        at = block(at_z, y, core)
        source = a_own if first else slab(at)
        return hand(source, at, y_send.at[at_z], y_recv.at[at_z], block(z, 1 - y, core))

    def over_core(at_z, at_y, first=False):
        at = block(at_z, at_y, core)
        source = a_own if first else slab(at)
        sem = at_z * 2 + at_y
        return hand(source, at, core_send.at[sem], core_recv.at[sem], block(z, y, 1 - core))

    def arrived(at, recv_sem, send_sem):
        hand(slab(at), at, send_sem, recv_sem, block(z, y, 1 - core)).wait_recv()

    def relay(step):
        @pl.when(z - 1 - step >= 0)
        def _():
            arrived(block(z - 1 - step, y, core), up_recv.at[step], up_send.at[step])
            if step + 1 < lines - 1:

                @pl.when(z + 1 < lines)
                def _():
                    up(step + 1).start()

            over_y(z - 1 - step).start()
            over_core(z - 1 - step, y).start()

        @pl.when(z + 1 + step < lines)
        def _():
            arrived(block(z + 1 + step, y, core), down_recv.at[step], down_send.at[step])
            if step + 1 < lines - 1:

                @pl.when(z >= 1)
                def _():
                    down(step + 1).start()

            over_y(z + 1 + step).start()
            over_core(z + 1 + step, y).start()

    def cross(step):
        at_z = lax.rem(z + step, lines)
        arrived(block(at_z, 1 - y, core), y_recv.at[at_z], y_send.at[at_z])
        over_core(at_z, 1 - y).start()

    def multiply(c, group):
        for q in range(per):
            j = group * per + q
            picked = [held[c][rows_ref[s, 0, j]] for s in range(listed_b)]
            product = lax.dot_general(
                b_own[j], jnp.concatenate(picked, axis=1), (((0,), (1,)), ((), ())),
                preferred_element_type=jnp.float32,
            )
            sent[c][pl.ds(pl.multiple_of(j * width, width), width), :] = product.astype(jnp.bfloat16)

    def make_table():
        total = list_all[0]
        for r in range(1, row_devices):
            total = total + list_all[r]
        square = (width, width)
        by_lane = jnp.broadcast_to(total[0:1], square)
        lane = lax.broadcasted_iota(jnp.int32, square, 1)
        sub = lax.broadcasted_iota(jnp.int32, square, 0)
        keys = by_lane * width + lane

        def count(mask):
            return jnp.sum(jnp.where(mask, 1, 0), axis=0, keepdims=True)

        rank = jnp.broadcast_to(count(keys.T < keys), square)
        hit = rank.T == lane
        by_sub = by_lane.T
        order = jnp.sum(jnp.where(hit, sub, 0), axis=0, keepdims=True)
        target = jnp.sum(jnp.where(hit, by_sub, 0), axis=0, keepdims=True)
        began = count(by_sub < target)
        source, slot = order // slots, order % slots
        table[0:1, :] = source * stored + slot
        table[1:2, :] = source * stored + slots + slot % listed
        table[2:3, :] = order // listed
        table[3:4, :] = jnp.where(lane[0:1] > began, 1, 0)
        table[4:5, :] = count(by_sub <= lane) - 1
        table[5:8, :] = jnp.zeros((3, width), jnp.int32)

    def prepare(s):
        lane = lax.broadcasted_iota(jnp.int32, (part, width), 1)
        low = lane < width // 2

        @pl.loop(0, row_devices)
        def _(r):
            cut = pl.ds(s * part, part)
            middle = xr[1, r, cut, :]
            blank = jnp.zeros_like(middle)
            xt[s][r * groups, :, 0:width] = xr[0, r, cut, :]
            xt[s][r * groups, :, width : 2 * width] = jnp.where(low, middle, blank)
            xt[s][r * groups + 1, :, 0:width] = xr[2, r, cut, :]
            xt[s][r * groups + 1, :, width : 2 * width] = jnp.where(low, blank, middle)

    def contract(s):
        def step(p, run):
            weights = jnp.concatenate([a_all[picks[0, p]], a_all[picks[1, p]]], axis=1)
            product = lax.dot_general(
                xt[s][picks[2, p]], weights, CONTRACT_LAST, preferred_element_type=jnp.float32
            )
            run = product + run * picks[3, p].astype(jnp.float32)
            stack[p] = run.astype(stack.dtype)
            return run

        lax.fori_loop(0, width, step, jnp.zeros((part, tile), jnp.float32), unroll=4)

    def assemble(s, k):
        found = [[stack[picks[4, g * row_devices + 2 * k + e]] for e in range(2)] for g in range(groups)]
        for e in range(2):
            own_out[s, 2 * k + e] = jnp.concatenate([found[g][e] for g in range(groups)], axis=1)
        for g in range(groups):
            start = pl.multiple_of(k * 2 * tile, width)
            mirror_out[s, g, :, pl.ds(start, 2 * tile)] = jnp.concatenate(found[g], axis=1)

    load_b = pltpu.make_async_copy(b_ref, b_own, load_sem.at[0])
    load_a = pltpu.make_async_copy(alpha_ref, flat, load_sem.at[1])
    load_a.start()
    for c in range(chunks):

        @pl.loop(0, tiles)
        def _(t):
            own_c(c, t).start()

        if c == 0:
            load_b.start()

    lane = lax.broadcasted_iota(jnp.int32, list_own.shape, 1)
    mine = jnp.zeros(list_own.shape, jnp.int32)
    for g in range(groups):
        for s in range(listed):
            mine = jnp.where(lane == row * slots + g * listed + s, lists_ref[0, g, 0, s], mine)
    list_own[...] = mine
    load_a.wait()
    for s in range(listed):
        first, second = flat[s], flat[listed + s]
        a_own[s] = first[:, :width]
        a_own[listed + s] = second[:, tile - width :]
        a_own[slots + s] = jnp.concatenate([first[:, width:], second[:, : tile - width]], axis=1)
    keep_list = pltpu.make_async_copy(list_own, list_all.at[row], l_own)
    keep_list.start()
    greet(("row", "col"))
    for c in range(chunks):
        for off in range(1, col_devices):

            @pl.loop(0, tiles)
            def _(t):
                send_c(c, off, t).start()

        if c == 0:

            @pl.loop(1, row_devices)
            def _(off):
                send_list(off).start()

            @pl.when(z + 1 < lines)
            def _():
                up(0, True).start()

            @pl.when(z >= 1)
            def _():
                down(0, True).start()

            over_y(z, True).start()
            over_core(z, y, True).start()

    keep_a = pltpu.make_async_copy(a_own, slab(row), a_sem)
    keep_a.start()
    load_b.wait()
    move_table = pltpu.make_async_copy(table, picks, t_sem)
    relayed = 0
    for c in range(chunks):
        if relayed < lines - 1:
            relay(relayed)
            relayed += 1

        @pl.loop(0, tiles)
        def _(t):
            own_c(c, t).wait()
            for off in range(1, col_devices):
                send_c(c, off, t).wait_recv()

        @pl.loop(0, chips)
        def _(i):
            multiply(c, pair(i))

            @pl.when(i > 0)
            def _():
                send_pair(functools.partial(send_x, c), i - 1)

        send_x(c, partner_off, partner).start()
        own_x(c).start()
        if c == chunks - 1:
            for s in range(1, subs):

                @pl.loop(0, chips - 1)
                def _(i):
                    send_pair(functools.partial(send_x, c + s), i)

                send_x(c + s, partner_off, partner).start()
                own_x(c + s).start()
        if c == 0:
            keep_list.wait()

            @pl.loop(1, row_devices)
            def _(off):
                send_list(off).wait_recv()

            make_table()
            move_table.start()
            cross(0)

    for step in range(relayed, lines - 1):
        relay(step)
    for step in range(1, lines):
        cross(step)
    keep_a.wait()
    move_table.wait()
    for at_z in range(lines):
        for at_y in range(2):
            sem = at_z * 2 + at_y
            arrived(block(at_z, at_y, 1 - core), core_recv.at[sem], core_send.at[sem])
    for s in range(subs):
        for u in range(chunks) if s == 0 else [chunks - 1 + s]:
            own_x(u).wait()

            @pl.loop(1, row_devices)
            def _(off):
                send_x(u, off, lax.rem(row + off, row_devices)).wait_recv()

        prepare(s)
        contract(s)

        @pl.loop(0, chips)
        def _(i):
            assemble(s, pair(i))

            @pl.when(i > 0)
            def _():
                send_pair(functools.partial(send_own, s), i - 1)

        send_own(s, partner_off, partner).start()
        for off in range(1, col_devices):
            send_mirror(s, off).start()
        stay_own(s).start()
        stay_mirror(s).start()

    for step in range(lines - 1):

        @pl.when((z - step >= 0) & (z + 1 < lines))
        def _():
            up(step, step == 0).wait_send()

        @pl.when((z + step < lines) & (z >= 1))
        def _():
            down(step, step == 0).wait_send()

    for at_z in range(lines):
        over_y(at_z).wait_send()
        for at_y in range(2):
            over_core(at_z, at_y).wait_send()

    for c in range(chunks):
        for off in range(1, col_devices):

            @pl.loop(0, tiles)
            def _(t):
                send_c(c, off, t).wait_send()

    @pl.loop(1, row_devices)
    def _(off):
        peer = lax.rem(row + off, row_devices)
        send_list(off).wait_send()
        for u in range(len(units)):
            send_x(u, off, peer).wait_send()
        for s in range(subs):
            send_own(s, off, peer).wait()

    for s in range(subs):
        stay_own(s).wait()
        stay_mirror(s).wait()
        for off in range(1, col_devices):
            send_mirror(s, off).wait()


def fused(c_matrix, beta_values, beta_rows, alpha_tiles, alpha_rows, row_devices, col_devices, subs):
    rows, columns = c_matrix.shape
    _, tiles, listed, width, _ = beta_values.shape
    slots, tile, _ = alpha_tiles.shape
    groups = alpha_rows.shape[1]
    chunks, strip = rows // width, columns // row_devices
    part, units, lines = strip // subs, rows // width - 1 + subs, row_devices // 4
    stored = slots * tile // width
    row_peers, col_peers = row_devices - 1, col_devices - 1
    dma, half = pltpu.SemaphoreType.DMA, jnp.bfloat16
    anywhere = pl.BlockSpec(memory_space=pl.ANY)
    scalars = pl.BlockSpec(memory_space=pltpu.SMEM)
    return pl.pallas_call(
        functools.partial(fused_kernel, chunks, subs),
        in_specs=[scalars, scalars, anywhere, anywhere, anywhere],
        out_specs=[anywhere, anywhere],
        out_shape=[
            jax.ShapeDtypeStruct((row_devices, strip, groups * tile), half),
            jax.ShapeDtypeStruct((col_devices, strip, row_devices * tile), half),
        ],
        scratch_shapes=[pltpu.VMEM((col_devices * tiles, width, width), half)] * chunks
        + [pltpu.VMEM((columns, width), half)] * chunks
        + [pltpu.VMEM((row_devices * groups, part, 2 * width), half)] * subs
        + [
            pltpu.VMEM((tiles, listed * width, width), half),
            pltpu.VMEM((slots, tile, tile), half),
            pltpu.VMEM((stored, tile, width), half),
            pltpu.VMEM((row_devices * stored, tile, width), half),
            pltpu.VMEM((chunks, row_devices, strip, width), half),
            pltpu.VMEM((row_devices * slots, part, tile), half),
            pltpu.VMEM((subs, row_devices, part, groups * tile), half),
            pltpu.VMEM((subs, groups, part, row_devices * tile), half),
            pltpu.VMEM((8, width), jnp.int32),
            pltpu.VMEM((row_devices, 8, width), jnp.int32),
            pltpu.VMEM((8, width), jnp.int32),
            pltpu.SMEM((8, width), jnp.int32),
            dma((2,)),
            dma((chunks, tiles)), dma((chunks, col_peers, tiles)), dma((chunks, col_peers, tiles)),
            dma((units,)), dma((units, row_peers)), dma((units, row_peers)),
            dma, dma((row_peers,)), dma((row_peers,)), dma,
        ]
        + [dma((lines - 1,))] * 4
        + [dma((lines,))] * 2
        + [dma((2 * lines,))] * 2
        + [
            dma,
            dma((subs,)), dma((subs, row_peers)), dma((subs, row_peers)),
            dma((subs,)), dma((subs, col_peers)), dma((subs, col_peers)),
        ],
        compiler_params=pltpu.CompilerParams(
            collective_id=0, has_side_effects=True, vmem_limit_bytes=60 << 20
        ),
        cost_estimate=pl.CostEstimate(flops=1 << 37, bytes_accessed=1 << 28, transcendentals=0),
        name="fused",
    )(
        jnp.transpose(beta_rows, (2, 0, 1)), alpha_rows, c_matrix,
        beta_values.reshape(tiles, listed * width, width), alpha_tiles,
    )


def per_device(c_matrix, beta_values, beta_rows, alpha_values, alpha_rows, gaps):
    row_devices, col_devices = lax.axis_size("row"), lax.axis_size("col")
    groups, stretch, columns = c_matrix.shape
    pairs, _, _, listed, tile, _ = alpha_values.shape
    rows, width = groups * stretch, beta_values.shape[-1]
    c_rows = c_matrix.reshape(rows, columns)
    alpha_tiles = alpha_values.reshape(pairs * groups, listed, tile, tile)
    strip, subs = columns // row_devices, 2
    own_kernels = pairs == 1 and groups == 2 and stretch == tile and 2 * tile == 3 * width
    own_kernels = own_kernels and row_devices % 4 == 0 and row_devices * groups * listed == width
    own_kernels = own_kernels and strip % (16 * subs) == 0 and 2 * strip % width == 0
    if own_kernels:
        own, mirror = fused(
            c_rows, beta_values, beta_rows, alpha_tiles.reshape(-1, tile, tile), alpha_rows,
            row_devices, col_devices, subs,
        )
    else:
        rows_all = lax.all_gather(alpha_rows.reshape(pairs * groups, listed), "row")
        alpha_all = lax.all_gather(alpha_tiles, "row")
        xt = beta_products(lax.all_gather(c_rows, "col"), beta_values, beta_rows)
        xt = jnp.moveaxis(xt.reshape(pairs, row_devices, stretch, rows), 1, 0)
        x_strip = lax.all_to_all(xt, "row", 0, 0)[None]
        own, mirror = alpha_products(alpha_all, rows_all, x_strip, groups)
        own = lax.all_to_all(own, "row", 0, 0)
        mirror = lax.all_to_all(mirror, "col", 0, 0)
    out = final(
        own.reshape(columns, groups * stretch),
        mirror.reshape(groups * stretch, columns),
        gaps.reshape(groups * stretch, columns),
    )
    return out.reshape(gaps.shape)


def solution(mesh):
    placed = (
        P(None, "row", "col"),
        P(None, "col", None, None, None),
        P(None, "col", None),
        P(None, None, "row", None, None, None),
        P(None, None, "row", None),
        P(None, "row", "col"),
    )
    return jax.shard_map(
        per_device, mesh=mesh, in_specs=placed, out_specs=P(None, "row", "col"), check_vma=False
    )
```

```python
import functools

import jax
import jax.numpy as jnp
from jax import lax
from jax.experimental import pallas as pl
from jax.experimental.pallas import tpu as pltpu
from jax.sharding import PartitionSpec as P

CONTRACT_LAST = (((1,), (1,)), ((), ()))
SHARE = 2


def beta_kernel(listed, held, rows_ref, c_ref, b_ref, xt_ref):
    k, j = pl.program_id(0), pl.program_id(1)
    width = b_ref.shape[-1]
    picked = []
    for z in range(listed):
        tile = rows_ref[k, j, z]
        owner = tile // held
        start = pl.multiple_of((tile - owner * held) * width, width)
        picked.append(c_ref[owner, :, pl.ds(start, width)])
    lhs = b_ref[0, 0].reshape(listed * width, width)
    product = lax.dot_general(
        lhs, jnp.concatenate(picked, axis=1), (((0,), (1,)), ((), ())),
        preferred_element_type=jnp.float32,
    )
    xt_ref[0] = product.astype(xt_ref.dtype)


def beta_products(gathered, beta_values, beta_rows):
    pairs, tiles, listed, width, _ = beta_values.shape
    owners, rows, columns = gathered.shape
    return pl.pallas_call(
        functools.partial(beta_kernel, listed, columns // width),
        grid_spec=pltpu.PrefetchScalarGridSpec(
            num_scalar_prefetch=1,
            grid=(pairs, tiles),
            in_specs=[
                pl.BlockSpec((owners, rows, columns), lambda k, j, s: (0, 0, 0)),
                pl.BlockSpec((1, 1, listed, width, width), lambda k, j, s: (k, j, 0, 0, 0)),
            ],
            out_specs=pl.BlockSpec((1, width, rows), lambda k, j, s: (k, j, 0)),
        ),
        out_shape=jax.ShapeDtypeStruct((pairs, tiles * width, rows), jnp.bfloat16),
        compiler_params=pltpu.CompilerParams(vmem_limit_bytes=56 << 20),
        name="beta_products",
    )(beta_rows, gathered, beta_values)


def alpha_kernel(groups, rows_ref, a_ref, x_ref, own_ref, mirror_ref, acc_ref):
    r = pl.program_id(0)
    row_devices = pl.num_programs(0)
    pairs = x_ref.shape[2]
    listed, tile = rows_ref.shape[2], acc_ref.shape[1]

    @pl.when(r == 0)
    def _():
        acc_ref[...] = jnp.zeros_like(acc_ref)

    for i in range(x_ref.shape[1]):
        at = r * x_ref.shape[1] + i
        for k in range(pairs):
            parts = [x_ref[c, i, k] for c in range(x_ref.shape[0])]
            merged = jnp.concatenate(parts, axis=1) if len(parts) > 1 else parts[0]
            for g in range(groups):
                x = merged[:, g * tile : (g + 1) * tile]
                slot = k * groups + g

                @pl.loop(0, listed)
                def _(z):
                    acc_ref[rows_ref[at, slot, z]] += lax.dot_general(
                        a_ref[i, slot, z], x, CONTRACT_LAST, preferred_element_type=jnp.float32
                    )

    @pl.when(r == row_devices - 1)
    def _():
        count = acc_ref.shape[0] // groups
        for g in range(groups):
            for to in range(count):
                turned = acc_ref[g * count + to].astype(own_ref.dtype).T
                own_ref[to, :, g * tile : (g + 1) * tile] = turned
                mirror_ref[g, :, to * tile : (to + 1) * tile] = turned


def alpha_products(alpha_all, rows_all, x_strip, groups):
    row_devices, rest = alpha_all.shape[0], alpha_all.shape[1:]
    tile = x_strip.shape[0] * x_strip.shape[-1] // groups
    per = 1
    chunks, _, pairs, strip, chunk = x_strip.shape
    return pl.pallas_call(
        functools.partial(alpha_kernel, groups),
        grid_spec=pltpu.PrefetchScalarGridSpec(
            num_scalar_prefetch=1,
            grid=(row_devices // per,),
            in_specs=[
                pl.BlockSpec((per,) + rest, lambda r, s: (r,) + (0,) * len(rest)),
                pl.BlockSpec((chunks, per, pairs, strip, chunk), lambda r, s: (0, r, 0, 0, 0)),
            ],
            out_specs=[
                pl.BlockSpec((row_devices, strip, groups * tile), lambda r, s: (0, 0, 0)),
                pl.BlockSpec((groups, strip, row_devices * tile), lambda r, s: (0, 0, 0)),
            ],
            scratch_shapes=[pltpu.VMEM((groups * row_devices, tile, strip), jnp.float32)],
        ),
        out_shape=[
            jax.ShapeDtypeStruct((row_devices, strip, groups * tile), jnp.bfloat16),
            jax.ShapeDtypeStruct((groups, strip, row_devices * tile), jnp.bfloat16),
        ],
        compiler_params=pltpu.CompilerParams(vmem_limit_bytes=56 << 20),
        name="alpha_products",
    )(rows_all, alpha_all, x_strip)


def final_kernel(own_ref, mirror_ref, gaps_ref, out_ref):
    own = own_ref[...].T.astype(jnp.float32)
    out_ref[...] = (own + mirror_ref[...].astype(jnp.float32)) / gaps_ref[...]


def final(own, mirror, gaps):
    rows, columns = gaps.shape
    block = next(n for n in (384, 256, 128) if columns % n == 0)
    wide = pl.BlockSpec((rows, block), lambda i: (0, i))
    return pl.pallas_call(
        final_kernel,
        grid=(columns // block,),
        in_specs=[pl.BlockSpec((block, rows), lambda i: (i, 0)), wide, wide],
        out_specs=wide,
        out_shape=jax.ShapeDtypeStruct((rows, columns), jnp.float32),
        name="final",
    )(own, mirror, gaps)


def knock(axes):
    barrier = pltpu.get_barrier_semaphore()
    for axis in axes:
        size, me = lax.axis_size(axis), lax.axis_index(axis)

        @pl.loop(1, size)
        def _(off):
            pl.semaphore_signal(
                barrier, inc=1, device_id={axis: lax.rem(me + off, size)},
                device_id_type=pl.DeviceIdType.MESH,
            )


def enter(axes):
    total = sum(lax.axis_size(axis) - 1 for axis in axes)
    pl.semaphore_wait(pltpu.get_barrier_semaphore(), total)


def remote(src, dst, send_sem, recv_sem, axis, peer):
    return pltpu.make_async_remote_copy(
        src_ref=src, dst_ref=dst, send_sem=send_sem, recv_sem=recv_sem,
        device_id={axis: peer}, device_id_type=pl.DeviceIdType.MESH,
    )


def fused_kernel(chunks, subs, share, rows_ref, lists_ref, c_ref, b_ref, alpha_ref, own_ref, mirror_ref, *scratch):
    held, sent, xt = scratch[:chunks], scratch[chunks : 2 * chunks], scratch[2 * chunks : 2 * chunks + subs]
    (b_own, flat, a_own, a_all, xr, stack, own_out, mirror_out, list_own, list_all, table, picks,
     load_sem, c_own, c_send, c_recv, x_own, x_send, x_recv, l_own, l_send, l_recv, a_sem,
     up_send, up_recv, down_send, down_recv, y_send, y_recv, core_send, core_recv,
     x_side, x_side_recv, core_side, core_side_recv, t_sem,
     o_own, o_send, o_recv, m_own, m_send, m_recv) = scratch[2 * chunks + subs :]
    row_devices, row = lax.axis_size("row"), lax.axis_index("row")
    col_devices, col = lax.axis_size("col"), lax.axis_index("col")
    rows, columns = c_ref.shape
    tiles, depth, width = b_own.shape
    listed_b = depth // width
    slots, tile, _ = flat.shape
    groups = lists_ref.shape[1]
    listed = slots // groups
    chunk, strip = rows // chunks, columns // row_devices
    part = strip // subs
    chips = row_devices // 2
    per = tiles // chips
    stored = a_own.shape[0]
    lines = row_devices // 4
    chip, core = row // 2, lax.rem(row, 2)
    z, y = row // 4, lax.rem(chip, 2)
    units = [(c, 0, strip) for c in range(chunks - 1)]
    units += [(chunks - 1, s * part, part) for s in range(subs)]

    def own_c(c, t):
        return pltpu.make_async_copy(
            c_ref.at[pl.ds(c * chunk, chunk), pl.ds(pl.multiple_of(t * width, width), width)],
            held[c].at[col * tiles + t], c_own.at[c, t],
        )

    def send_c(c, off, t):
        return remote(
            c_ref.at[pl.ds(c * chunk, chunk), pl.ds(pl.multiple_of(t * width, width), width)],
            held[c].at[col * tiles + t], c_send.at[c, off - 1, t], c_recv.at[c, off - 1, t],
            "col", lax.rem(col + off, col_devices),
        )

    def send_x(u, off, peer):
        c, first, size = units[u]
        start = pl.multiple_of(peer * strip + first, 16)
        return remote(
            sent[c].at[pl.ds(start, size), :], xr.at[c, row, pl.ds(first, size), :],
            x_send.at[u, off - 1], x_recv.at[u, off - 1], "row", peer,
        )

    def own_x(u):
        c, first, size = units[u]
        start = pl.multiple_of(row * strip + first, 16)
        return pltpu.make_async_copy(
            sent[c].at[pl.ds(start, size), :], xr.at[c, row, pl.ds(first, size), :], x_own.at[u]
        )

    def send_own(s, off, peer):
        return remote(
            own_out.at[s, peer], own_ref.at[row, pl.ds(s * part, part), :],
            o_send.at[s, off - 1], o_recv.at[s, off - 1], "row", peer,
        )

    def stay_own(s):
        return pltpu.make_async_copy(
            own_out.at[s, row], own_ref.at[row, pl.ds(s * part, part), :], o_own.at[s]
        )

    def send_mirror(s, off):
        peer = lax.rem(col + off, col_devices)
        return remote(
            mirror_out.at[s, peer], mirror_ref.at[col, pl.ds(s * part, part), :],
            m_send.at[s, off - 1], m_recv.at[s, off - 1], "col", peer,
        )

    def stay_mirror(s):
        return pltpu.make_async_copy(
            mirror_out.at[s, col], mirror_ref.at[col, pl.ds(s * part, part), :], m_own.at[s]
        )

    def send_list(off):
        return remote(
            list_own, list_all.at[row], l_send.at[off - 1], l_recv.at[off - 1], "row",
            lax.rem(row + off, row_devices),
        )

    def reach(i):
        odd = lax.rem(i, 2)
        return chips // 2 + (1 - odd) * (i // 2) - odd * ((i + 1) // 2)

    def pair(i):
        return lax.rem(chip + reach(i), chips)

    def send_pair(send, i):
        for e in range(2):
            send(2 * reach(i) + e - core, 2 * pair(i) + e).start()

    partner, partner_off = row + 1 - 2 * core, 1 + core * (row_devices - 2)

    def block(at_z, at_y, at_core):
        return (at_z * 2 + at_y) * 2 + at_core

    def cut(ref, at, first, size):
        return ref.at[pl.ds(at * stored + first, size)]

    def hand(at, first, size, send_sem, recv_sem, peer, axis="row", source=None):
        held_part = cut(a_all, at, first, size)
        if source is not None:
            held_part = source.at[pl.ds(first, size)]
        return remote(held_part, cut(a_all, at, first, size), send_sem, recv_sem, axis, peer)

    main = (col * share, stored - share)
    gives, gets = (col * (stored - share), share), ((1 - col) * (stored - share), share)
    other_core = block(z, y, 1 - core)

    def up(step, source=None):
        at = block(z - step, y, core)
        return hand(at, *main, up_send.at[step], up_recv.at[step], block(z + 1, y, core), source=source)

    def down(step, source=None):
        at = block(z + step, y, core)
        return hand(at, *main, down_send.at[step], down_recv.at[step], block(z - 1, y, core), source=source)

    def over_y(at_z, source=None):
        at = block(at_z, y, core)
        return hand(at, *main, y_send.at[at_z], y_recv.at[at_z], block(z, 1 - y, core), source=source)

    def over_core(at_z, at_y, source=None):
        at, sem = block(at_z, at_y, core), at_z * 2 + at_y
        return hand(at, *main, core_send.at[sem], core_recv.at[sem], other_core, source=source)

    def side_x(at_z, at_y):
        at, sem = block(at_z, at_y, core), at_z * 2 + at_y
        return hand(at, *gives, x_side.at[sem], x_side_recv.at[sem], 1 - col, "col")

    def side_core(at_z, at_y, source=None):
        at, sem = block(at_z, at_y, core), at_z * 2 + at_y
        return hand(at, *gets, core_side.at[sem], core_side_recv.at[sem], other_core, source=source)

    def arrived(at, span, recv_sem, send_sem):
        hand(at, *span, send_sem, recv_sem, other_core).wait_recv()

    def spread(at_z, at_y):
        over_core(at_z, at_y).start()
        if share:
            side_x(at_z, at_y).start()

    def relay(step):
        @pl.when(z - 1 - step >= 0)
        def _():
            arrived(block(z - 1 - step, y, core), main, up_recv.at[step], up_send.at[step])
            if step + 1 < lines - 1:

                @pl.when(z + 1 < lines)
                def _():
                    up(step + 1).start()

            over_y(z - 1 - step).start()
            spread(z - 1 - step, y)

        @pl.when(z + 1 + step < lines)
        def _():
            arrived(block(z + 1 + step, y, core), main, down_recv.at[step], down_send.at[step])
            if step + 1 < lines - 1:

                @pl.when(z >= 1)
                def _():
                    down(step + 1).start()

            over_y(z + 1 + step).start()
            spread(z + 1 + step, y)

    def cross(step):
        at_z = lax.rem(z + step, lines)
        arrived(block(at_z, 1 - y, core), main, y_recv.at[at_z], y_send.at[at_z])
        spread(at_z, 1 - y)

    def others(body):
        for step in range(1, lines):
            body(lax.rem(z + step, lines), y)
        for step in range(lines):
            body(lax.rem(z + step, lines), 1 - y)

    def side_arrived(at_z, at_y):
        sem = at_z * 2 + at_y
        hand(block(at_z, at_y, core), *gets, x_side.at[sem], x_side_recv.at[sem], 1 - col, "col").wait_recv()
        side_core(at_z, at_y).start()

    def multiply(c, group):
        for q in range(per):
            j = group * per + q
            picked = [held[c][rows_ref[s, 0, j]] for s in range(listed_b)]
            product = lax.dot_general(
                b_own[j], jnp.concatenate(picked, axis=1), (((0,), (1,)), ((), ())),
                preferred_element_type=jnp.float32,
            )
            sent[c][pl.ds(pl.multiple_of(j * width, width), width), :] = product.astype(jnp.bfloat16)

    def make_table():
        total = list_all[0]
        for r in range(1, row_devices):
            total = total + list_all[r]
        square = (width, width)
        by_lane = jnp.broadcast_to(total[0:1], square)
        lane = lax.broadcasted_iota(jnp.int32, square, 1)
        sub = lax.broadcasted_iota(jnp.int32, square, 0)
        keys = by_lane * width + lane

        def count(mask):
            return jnp.sum(jnp.where(mask, 1, 0), axis=0, keepdims=True)

        rank = jnp.broadcast_to(count(keys.T < keys), square)
        hit = rank.T == lane
        by_sub = by_lane.T
        order = jnp.sum(jnp.where(hit, sub, 0), axis=0, keepdims=True)
        target = jnp.sum(jnp.where(hit, by_sub, 0), axis=0, keepdims=True)
        began = count(by_sub < target)
        source, slot = order // slots, order % slots
        table[0:1, :] = source * stored + slot
        table[1:2, :] = source * stored + slots + slot % listed
        table[2:3, :] = order // listed
        table[3:4, :] = jnp.where(lane[0:1] > began, 1, 0)
        table[4:5, :] = count(by_sub <= lane) - 1
        table[5:8, :] = jnp.zeros((3, width), jnp.int32)

    def prepare(s):
        lane = lax.broadcasted_iota(jnp.int32, (part, width), 1)
        low = lane < width // 2

        @pl.loop(0, row_devices)
        def _(r):
            cut = pl.ds(s * part, part)
            middle = xr[1, r, cut, :]
            blank = jnp.zeros_like(middle)
            xt[s][r * groups, :, 0:width] = xr[0, r, cut, :]
            xt[s][r * groups, :, width : 2 * width] = jnp.where(low, middle, blank)
            xt[s][r * groups + 1, :, 0:width] = xr[2, r, cut, :]
            xt[s][r * groups + 1, :, width : 2 * width] = jnp.where(low, blank, middle)

    def contract(s):
        def step(p, run):
            weights = jnp.concatenate([a_all[picks[0, p]], a_all[picks[1, p]]], axis=1)
            product = lax.dot_general(
                xt[s][picks[2, p]], weights, CONTRACT_LAST, preferred_element_type=jnp.float32
            )
            run = product + run * picks[3, p].astype(jnp.float32)
            stack[p] = run.astype(stack.dtype)
            return run

        lax.fori_loop(0, width, step, jnp.zeros((part, tile), jnp.float32), unroll=4)

    def assemble(s, k):
        found = [[stack[picks[4, g * row_devices + 2 * k + e]] for e in range(2)] for g in range(groups)]
        for e in range(2):
            own_out[s, 2 * k + e] = jnp.concatenate([found[g][e] for g in range(groups)], axis=1)
        for g in range(groups):
            start = pl.multiple_of(k * 2 * tile, width)
            mirror_out[s, g, :, pl.ds(start, 2 * tile)] = jnp.concatenate(found[g], axis=1)

    load_b = pltpu.make_async_copy(b_ref, b_own, load_sem.at[0])
    load_a = pltpu.make_async_copy(alpha_ref, flat, load_sem.at[1])
    load_a.start()
    knock(("row", "col"))
    lane = lax.broadcasted_iota(jnp.int32, list_own.shape, 1)
    mine = jnp.zeros(list_own.shape, jnp.int32)
    for g in range(groups):
        for s in range(listed):
            mine = jnp.where(lane == row * slots + g * listed + s, lists_ref[0, g, 0, s], mine)
    list_own[...] = mine
    load_a.wait()
    for s in range(listed):
        first, second = flat[s], flat[listed + s]
        a_own[s] = first[:, :width]
        a_own[listed + s] = second[:, tile - width :]
        a_own[slots + s] = jnp.concatenate([first[:, width:], second[:, : tile - width]], axis=1)
    keep_list = pltpu.make_async_copy(list_own, list_all.at[row], l_own)
    keep_a = pltpu.make_async_copy(a_own, cut(a_all, row, 0, stored), a_sem)
    enter(("row", "col"))

    @pl.when(z + 1 < lines)
    def _():
        up(0, a_own).start()

    @pl.when(z >= 1)
    def _():
        down(0, a_own).start()

    over_y(z, a_own).start()
    over_core(z, y, a_own).start()
    if share:
        side_core(z, y, a_own).start()
    for c in range(chunks):
        for off in range(1, col_devices):

            @pl.loop(0, tiles)
            def _(t):
                send_c(c, off, t).start()

        if c == 0:

            @pl.loop(1, row_devices)
            def _(off):
                send_list(off).start()

            keep_list.start()
            keep_a.start()
            load_b.start()

        @pl.loop(0, tiles)
        def _(t):
            own_c(c, t).start()

    load_b.wait()
    move_table = pltpu.make_async_copy(table, picks, t_sem)
    relayed = 0
    for c in range(chunks):
        if relayed < lines - 1:
            relay(relayed)
            relayed += 1

        @pl.loop(0, tiles)
        def _(t):
            own_c(c, t).wait()
            for off in range(1, col_devices):
                send_c(c, off, t).wait_recv()

        @pl.loop(0, chips)
        def _(i):
            multiply(c, pair(i))

            @pl.when(i > 0)
            def _():
                send_pair(functools.partial(send_x, c), i - 1)

        send_x(c, partner_off, partner).start()
        own_x(c).start()
        if c == chunks - 1:
            for s in range(1, subs):

                @pl.loop(0, chips - 1)
                def _(i):
                    send_pair(functools.partial(send_x, c + s), i)

                send_x(c + s, partner_off, partner).start()
                own_x(c + s).start()
        if c == 0:
            keep_list.wait()

            @pl.loop(1, row_devices)
            def _(off):
                send_list(off).wait_recv()

            make_table()
            move_table.start()
            cross(0)

    for step in range(relayed, lines - 1):
        relay(step)
    for step in range(1, lines):
        cross(step)
    if share:
        others(side_arrived)
    keep_a.wait()
    move_table.wait()
    for at_z in range(lines):
        for at_y in range(2):
            at, sem = block(at_z, at_y, 1 - core), at_z * 2 + at_y
            arrived(at, main, core_recv.at[sem], core_send.at[sem])
            if share:
                arrived(at, gets, core_side_recv.at[sem], core_side.at[sem])
    for s in range(subs):
        for u in range(chunks) if s == 0 else [chunks - 1 + s]:
            own_x(u).wait()

            @pl.loop(1, row_devices)
            def _(off):
                send_x(u, off, lax.rem(row + off, row_devices)).wait_recv()

        prepare(s)
        contract(s)

        @pl.loop(0, chips)
        def _(i):
            assemble(s, pair(i))

            @pl.when(i > 0)
            def _():
                send_pair(functools.partial(send_own, s), i - 1)

        send_own(s, partner_off, partner).start()
        for off in range(1, col_devices):
            send_mirror(s, off).start()
        stay_own(s).start()
        stay_mirror(s).start()

    for step in range(lines - 1):

        @pl.when((z - step >= 0) & (z + 1 < lines))
        def _():
            up(step).wait_send()

        @pl.when((z + step < lines) & (z >= 1))
        def _():
            down(step).wait_send()

    for at_z in range(lines):
        over_y(at_z).wait_send()
        for at_y in range(2):
            over_core(at_z, at_y).wait_send()
            if share:
                side_core(at_z, at_y).wait_send()

    if share:
        others(lambda at_z, at_y: side_x(at_z, at_y).wait_send())
    for c in range(chunks):
        for off in range(1, col_devices):

            @pl.loop(0, tiles)
            def _(t):
                send_c(c, off, t).wait_send()

    @pl.loop(1, row_devices)
    def _(off):
        peer = lax.rem(row + off, row_devices)
        send_list(off).wait_send()
        for u in range(len(units)):
            send_x(u, off, peer).wait_send()
        for s in range(subs):
            send_own(s, off, peer).wait()

    for s in range(subs):
        stay_own(s).wait()
        stay_mirror(s).wait()
        for off in range(1, col_devices):
            send_mirror(s, off).wait()


def fused(c_matrix, beta_values, beta_rows, alpha_tiles, alpha_rows, row_devices, col_devices, subs, share):
    rows, columns = c_matrix.shape
    _, tiles, listed, width, _ = beta_values.shape
    slots, tile, _ = alpha_tiles.shape
    groups = alpha_rows.shape[1]
    chunks, strip = rows // width, columns // row_devices
    part, units, lines = strip // subs, rows // width - 1 + subs, row_devices // 4
    stored = slots * tile // width
    row_peers, col_peers = row_devices - 1, col_devices - 1
    dma, half = pltpu.SemaphoreType.DMA, jnp.bfloat16
    anywhere = pl.BlockSpec(memory_space=pl.ANY)
    scalars = pl.BlockSpec(memory_space=pltpu.SMEM)
    return pl.pallas_call(
        functools.partial(fused_kernel, chunks, subs, share),
        in_specs=[scalars, scalars, anywhere, anywhere, anywhere],
        out_specs=[anywhere, anywhere],
        out_shape=[
            jax.ShapeDtypeStruct((row_devices, strip, groups * tile), half),
            jax.ShapeDtypeStruct((col_devices, strip, row_devices * tile), half),
        ],
        scratch_shapes=[pltpu.VMEM((col_devices * tiles, width, width), half)] * chunks
        + [pltpu.VMEM((columns, width), half)] * chunks
        + [pltpu.VMEM((row_devices * groups, part, 2 * width), half)] * subs
        + [
            pltpu.VMEM((tiles, listed * width, width), half),
            pltpu.VMEM((slots, tile, tile), half),
            pltpu.VMEM((stored, tile, width), half),
            pltpu.VMEM((row_devices * stored, tile, width), half),
            pltpu.VMEM((chunks, row_devices, strip, width), half),
            pltpu.VMEM((row_devices * slots, part, tile), half),
            pltpu.VMEM((subs, row_devices, part, groups * tile), half),
            pltpu.VMEM((subs, groups, part, row_devices * tile), half),
            pltpu.VMEM((8, width), jnp.int32),
            pltpu.VMEM((row_devices, 8, width), jnp.int32),
            pltpu.VMEM((8, width), jnp.int32),
            pltpu.SMEM((8, width), jnp.int32),
            dma((2,)),
            dma((chunks, tiles)), dma((chunks, col_peers, tiles)), dma((chunks, col_peers, tiles)),
            dma((units,)), dma((units, row_peers)), dma((units, row_peers)),
            dma, dma((row_peers,)), dma((row_peers,)), dma,
        ]
        + [dma((lines - 1,))] * 4
        + [dma((lines,))] * 2
        + [dma((2 * lines,))] * 6
        + [
            dma,
            dma((subs,)), dma((subs, row_peers)), dma((subs, row_peers)),
            dma((subs,)), dma((subs, col_peers)), dma((subs, col_peers)),
        ],
        compiler_params=pltpu.CompilerParams(
            collective_id=0, has_side_effects=True, vmem_limit_bytes=60 << 20
        ),
        cost_estimate=pl.CostEstimate(flops=1 << 37, bytes_accessed=1 << 28, transcendentals=0),
        name="fused",
    )(
        jnp.transpose(beta_rows, (2, 0, 1)), alpha_rows, c_matrix,
        beta_values.reshape(tiles, listed * width, width), alpha_tiles,
    )


def per_device(c_matrix, beta_values, beta_rows, alpha_values, alpha_rows, gaps):
    row_devices, col_devices = lax.axis_size("row"), lax.axis_size("col")
    groups, stretch, columns = c_matrix.shape
    pairs, _, _, listed, tile, _ = alpha_values.shape
    rows, width = groups * stretch, beta_values.shape[-1]
    c_rows = c_matrix.reshape(rows, columns)
    alpha_tiles = alpha_values.reshape(pairs * groups, listed, tile, tile)
    strip, subs = columns // row_devices, 2
    own_kernels = pairs == 1 and groups == 2 and stretch == tile and 2 * tile == 3 * width
    own_kernels = own_kernels and row_devices % 4 == 0 and row_devices * groups * listed == width
    own_kernels = own_kernels and strip % (16 * subs) == 0 and 2 * strip % width == 0
    if own_kernels:
        own, mirror = fused(
            c_rows, beta_values, beta_rows, alpha_tiles.reshape(-1, tile, tile), alpha_rows,
            row_devices, col_devices, subs, SHARE,
        )
    else:
        rows_all = lax.all_gather(alpha_rows.reshape(pairs * groups, listed), "row")
        alpha_all = lax.all_gather(alpha_tiles, "row")
        xt = beta_products(lax.all_gather(c_rows, "col"), beta_values, beta_rows)
        xt = jnp.moveaxis(xt.reshape(pairs, row_devices, stretch, rows), 1, 0)
        x_strip = lax.all_to_all(xt, "row", 0, 0)[None]
        own, mirror = alpha_products(alpha_all, rows_all, x_strip, groups)
        own = lax.all_to_all(own, "row", 0, 0)
        mirror = lax.all_to_all(mirror, "col", 0, 0)
    out = final(
        own.reshape(columns, groups * stretch),
        mirror.reshape(groups * stretch, columns),
        gaps.reshape(groups * stretch, columns),
    )
    return out.reshape(gaps.shape)


def solution(mesh):
    placed = (
        P(None, "row", "col"),
        P(None, "col", None, None, None),
        P(None, "col", None),
        P(None, None, "row", None, None, None),
        P(None, None, "row", None),
        P(None, "row", "col"),
    )
    return jax.shard_map(
        per_device, mesh=mesh, in_specs=placed, out_specs=P(None, "row", "col"), check_vma=False
    )
```

```python
import functools

import jax
import jax.numpy as jnp
from jax import lax
from jax.experimental import pallas as pl
from jax.experimental.pallas import tpu as pltpu
from jax.sharding import PartitionSpec as P

CONTRACT_LAST = (((1,), (1,)), ((), ()))
SHARE = 2


def beta_kernel(listed, held, rows_ref, c_ref, b_ref, xt_ref):
    k, j = pl.program_id(0), pl.program_id(1)
    width = b_ref.shape[-1]
    picked = []
    for z in range(listed):
        tile = rows_ref[k, j, z]
        owner = tile // held
        start = pl.multiple_of((tile - owner * held) * width, width)
        picked.append(c_ref[owner, :, pl.ds(start, width)])
    lhs = b_ref[0, 0].reshape(listed * width, width)
    product = lax.dot_general(
        lhs, jnp.concatenate(picked, axis=1), (((0,), (1,)), ((), ())),
        preferred_element_type=jnp.float32,
    )
    xt_ref[0] = product.astype(xt_ref.dtype)


def beta_products(gathered, beta_values, beta_rows):
    pairs, tiles, listed, width, _ = beta_values.shape
    owners, rows, columns = gathered.shape
    return pl.pallas_call(
        functools.partial(beta_kernel, listed, columns // width),
        grid_spec=pltpu.PrefetchScalarGridSpec(
            num_scalar_prefetch=1,
            grid=(pairs, tiles),
            in_specs=[
                pl.BlockSpec((owners, rows, columns), lambda k, j, s: (0, 0, 0)),
                pl.BlockSpec((1, 1, listed, width, width), lambda k, j, s: (k, j, 0, 0, 0)),
            ],
            out_specs=pl.BlockSpec((1, width, rows), lambda k, j, s: (k, j, 0)),
        ),
        out_shape=jax.ShapeDtypeStruct((pairs, tiles * width, rows), jnp.bfloat16),
        compiler_params=pltpu.CompilerParams(vmem_limit_bytes=56 << 20),
        name="beta_products",
    )(beta_rows, gathered, beta_values)


def alpha_kernel(groups, rows_ref, a_ref, x_ref, own_ref, mirror_ref, acc_ref):
    r = pl.program_id(0)
    row_devices = pl.num_programs(0)
    pairs = x_ref.shape[2]
    listed, tile = rows_ref.shape[2], acc_ref.shape[1]

    @pl.when(r == 0)
    def _():
        acc_ref[...] = jnp.zeros_like(acc_ref)

    for i in range(x_ref.shape[1]):
        at = r * x_ref.shape[1] + i
        for k in range(pairs):
            parts = [x_ref[c, i, k] for c in range(x_ref.shape[0])]
            merged = jnp.concatenate(parts, axis=1) if len(parts) > 1 else parts[0]
            for g in range(groups):
                x = merged[:, g * tile : (g + 1) * tile]
                slot = k * groups + g

                @pl.loop(0, listed)
                def _(z):
                    acc_ref[rows_ref[at, slot, z]] += lax.dot_general(
                        a_ref[i, slot, z], x, CONTRACT_LAST, preferred_element_type=jnp.float32
                    )

    @pl.when(r == row_devices - 1)
    def _():
        count = acc_ref.shape[0] // groups
        for g in range(groups):
            for to in range(count):
                turned = acc_ref[g * count + to].astype(own_ref.dtype).T
                own_ref[to, :, g * tile : (g + 1) * tile] = turned
                mirror_ref[g, :, to * tile : (to + 1) * tile] = turned


def alpha_products(alpha_all, rows_all, x_strip, groups):
    row_devices, rest = alpha_all.shape[0], alpha_all.shape[1:]
    tile = x_strip.shape[0] * x_strip.shape[-1] // groups
    per = 1
    chunks, _, pairs, strip, chunk = x_strip.shape
    return pl.pallas_call(
        functools.partial(alpha_kernel, groups),
        grid_spec=pltpu.PrefetchScalarGridSpec(
            num_scalar_prefetch=1,
            grid=(row_devices // per,),
            in_specs=[
                pl.BlockSpec((per,) + rest, lambda r, s: (r,) + (0,) * len(rest)),
                pl.BlockSpec((chunks, per, pairs, strip, chunk), lambda r, s: (0, r, 0, 0, 0)),
            ],
            out_specs=[
                pl.BlockSpec((row_devices, strip, groups * tile), lambda r, s: (0, 0, 0)),
                pl.BlockSpec((groups, strip, row_devices * tile), lambda r, s: (0, 0, 0)),
            ],
            scratch_shapes=[pltpu.VMEM((groups * row_devices, tile, strip), jnp.float32)],
        ),
        out_shape=[
            jax.ShapeDtypeStruct((row_devices, strip, groups * tile), jnp.bfloat16),
            jax.ShapeDtypeStruct((groups, strip, row_devices * tile), jnp.bfloat16),
        ],
        compiler_params=pltpu.CompilerParams(vmem_limit_bytes=56 << 20),
        name="alpha_products",
    )(rows_all, alpha_all, x_strip)


def final_kernel(block, own_ref, mirror_ref, gaps_ref, out_ref, own, mirror, gaps, out, in_sem, out_sem):
    steps = out.shape[1] // block

    def fetch(i):
        span = pl.ds(i * block, block)
        pairs = (
            (gaps_ref.at[:, span], gaps.at[:, span]), (own_ref.at[span, :], own.at[span, :]),
            (mirror_ref.at[:, span], mirror.at[:, span]),
        )
        return [pltpu.make_async_copy(*pair, in_sem.at[n, i]) for n, pair in enumerate(pairs)]

    def store(i):
        span = pl.ds(i * block, block)
        return pltpu.make_async_copy(out.at[:, span], out_ref.at[:, span], out_sem.at[i])

    for i in range(steps):
        for copy in fetch(i):
            copy.start()
    for i in range(steps):
        for copy in fetch(i):
            copy.wait()
        span = slice(i * block, (i + 1) * block)
        turned = own[span, :].T.astype(jnp.float32)
        out[:, span] = (turned + mirror[:, span].astype(jnp.float32)) / gaps[:, span]
        store(i).start()
    for i in range(steps):
        store(i).wait()


def final(own, mirror, gaps):
    rows, columns = gaps.shape
    block = next(n for n in (768, 384, 256, 128) if columns % n == 0)
    dma, anywhere = pltpu.SemaphoreType.DMA, pl.BlockSpec(memory_space=pl.ANY)
    return pl.pallas_call(
        functools.partial(final_kernel, block),
        in_specs=[anywhere] * 3,
        out_specs=anywhere,
        out_shape=jax.ShapeDtypeStruct((rows, columns), jnp.float32),
        scratch_shapes=[
            pltpu.VMEM(own.shape, own.dtype), pltpu.VMEM(mirror.shape, mirror.dtype),
            pltpu.VMEM(gaps.shape, gaps.dtype), pltpu.VMEM(gaps.shape, gaps.dtype),
            dma((3, columns // block)), dma((columns // block,)),
        ],
        name="final",
    )(own, mirror, gaps)


def knock(axes):
    barrier = pltpu.get_barrier_semaphore()
    for axis in axes:
        size, me = lax.axis_size(axis), lax.axis_index(axis)

        @pl.loop(1, size)
        def _(off):
            pl.semaphore_signal(
                barrier, inc=1, device_id={axis: lax.rem(me + off, size)},
                device_id_type=pl.DeviceIdType.MESH,
            )


def enter(axes):
    total = sum(lax.axis_size(axis) - 1 for axis in axes)
    pl.semaphore_wait(pltpu.get_barrier_semaphore(), total)


def remote(src, dst, send_sem, recv_sem, axis, peer):
    return pltpu.make_async_remote_copy(
        src_ref=src, dst_ref=dst, send_sem=send_sem, recv_sem=recv_sem,
        device_id={axis: peer}, device_id_type=pl.DeviceIdType.MESH,
    )


def fused_kernel(chunks, subs, share, rows_ref, lists_ref, c_ref, b_ref, alpha_ref, own_ref, mirror_ref, *scratch):
    held, sent, xt = scratch[:chunks], scratch[chunks : 2 * chunks], scratch[2 * chunks : 2 * chunks + subs]
    (b_own, flat, a_own, a_all, xr, stack, own_out, mirror_out, list_own, list_all, table, picks,
     load_sem, c_own, c_send, c_recv, x_own, x_send, x_recv, l_own, l_send, l_recv, a_sem,
     up_send, up_recv, down_send, down_recv, y_send, y_recv, core_send, core_recv,
     x_side, x_side_recv, core_side, core_side_recv, t_sem,
     o_own, o_send, o_recv, m_own, m_send, m_recv) = scratch[2 * chunks + subs :]
    row_devices, row = lax.axis_size("row"), lax.axis_index("row")
    col_devices, col = lax.axis_size("col"), lax.axis_index("col")
    rows, columns = c_ref.shape
    tiles, depth, width = b_own.shape
    listed_b = depth // width
    slots, tile, _ = flat.shape
    groups = lists_ref.shape[1]
    listed = slots // groups
    chunk, strip = rows // chunks, columns // row_devices
    part = strip // subs
    chips = row_devices // 2
    per = tiles // chips
    stored = a_own.shape[0]
    lines = row_devices // 4
    chip, core = row // 2, lax.rem(row, 2)
    z, y = row // 4, lax.rem(chip, 2)
    units = [(c, 0, strip) for c in range(chunks - 1)]
    units += [(chunks - 1, s * part, part) for s in range(subs)]

    def own_c(c, t):
        return pltpu.make_async_copy(
            c_ref.at[pl.ds(c * chunk, chunk), pl.ds(pl.multiple_of(t * width, width), width)],
            held[c].at[col * tiles + t], c_own.at[c, t],
        )

    def send_c(c, off, t):
        return remote(
            c_ref.at[pl.ds(c * chunk, chunk), pl.ds(pl.multiple_of(t * width, width), width)],
            held[c].at[col * tiles + t], c_send.at[c, off - 1, t], c_recv.at[c, off - 1, t],
            "col", lax.rem(col + off, col_devices),
        )

    def send_x(u, off, peer):
        c, first, size = units[u]
        start = pl.multiple_of(peer * strip + first, 16)
        return remote(
            sent[c].at[pl.ds(start, size), :], xr.at[c, row, pl.ds(first, size), :],
            x_send.at[u, off - 1], x_recv.at[u, off - 1], "row", peer,
        )

    def own_x(u):
        c, first, size = units[u]
        start = pl.multiple_of(row * strip + first, 16)
        return pltpu.make_async_copy(
            sent[c].at[pl.ds(start, size), :], xr.at[c, row, pl.ds(first, size), :], x_own.at[u]
        )

    def send_own(s, off, peer):
        return remote(
            own_out.at[s, peer], own_ref.at[row, pl.ds(s * part, part), :],
            o_send.at[s, off - 1], o_recv.at[s, off - 1], "row", peer,
        )

    def stay_own(s):
        return pltpu.make_async_copy(
            own_out.at[s, row], own_ref.at[row, pl.ds(s * part, part), :], o_own.at[s]
        )

    def send_mirror(s, off):
        peer = lax.rem(col + off, col_devices)
        return remote(
            mirror_out.at[s, peer], mirror_ref.at[col, pl.ds(s * part, part), :],
            m_send.at[s, off - 1], m_recv.at[s, off - 1], "col", peer,
        )

    def stay_mirror(s):
        return pltpu.make_async_copy(
            mirror_out.at[s, col], mirror_ref.at[col, pl.ds(s * part, part), :], m_own.at[s]
        )

    def send_list(off):
        return remote(
            list_own, list_all.at[row], l_send.at[off - 1], l_recv.at[off - 1], "row",
            lax.rem(row + off, row_devices),
        )

    def reach(i):
        odd = lax.rem(i, 2)
        return chips // 2 + (1 - odd) * (i // 2) - odd * ((i + 1) // 2)

    def pair(i):
        return lax.rem(chip + reach(i), chips)

    def send_pair(send, i):
        for e in range(2):
            send(2 * reach(i) + e - core, 2 * pair(i) + e).start()

    partner, partner_off = row + 1 - 2 * core, 1 + core * (row_devices - 2)

    def block(at_z, at_y, at_core):
        return (at_z * 2 + at_y) * 2 + at_core

    def cut(ref, at, first, size):
        return ref.at[pl.ds(at * stored + first, size)]

    def hand(at, first, size, send_sem, recv_sem, peer, axis="row", source=None):
        held_part = cut(a_all, at, first, size)
        if source is not None:
            held_part = source.at[pl.ds(first, size)]
        return remote(held_part, cut(a_all, at, first, size), send_sem, recv_sem, axis, peer)

    main = (col * share, stored - share)
    gives, gets = (col * (stored - share), share), ((1 - col) * (stored - share), share)
    other_core = block(z, y, 1 - core)

    def up(step, source=None):
        at = block(z - step, y, core)
        return hand(at, *main, up_send.at[step], up_recv.at[step], block(z + 1, y, core), source=source)

    def down(step, source=None):
        at = block(z + step, y, core)
        return hand(at, *main, down_send.at[step], down_recv.at[step], block(z - 1, y, core), source=source)

    def over_y(at_z, source=None):
        at = block(at_z, y, core)
        return hand(at, *main, y_send.at[at_z], y_recv.at[at_z], block(z, 1 - y, core), source=source)

    def over_core(at_z, at_y, source=None):
        at, sem = block(at_z, at_y, core), at_z * 2 + at_y
        return hand(at, *main, core_send.at[sem], core_recv.at[sem], other_core, source=source)

    def side_x(at_z, at_y):
        at, sem = block(at_z, at_y, core), at_z * 2 + at_y
        return hand(at, *gives, x_side.at[sem], x_side_recv.at[sem], 1 - col, "col")

    def side_core(at_z, at_y, source=None):
        at, sem = block(at_z, at_y, core), at_z * 2 + at_y
        return hand(at, *gets, core_side.at[sem], core_side_recv.at[sem], other_core, source=source)

    def arrived(at, span, recv_sem, send_sem):
        hand(at, *span, send_sem, recv_sem, other_core).wait_recv()

    def spread(at_z, at_y):
        over_core(at_z, at_y).start()
        if share:
            side_x(at_z, at_y).start()

    def relay(step):
        @pl.when(z - 1 - step >= 0)
        def _():
            arrived(block(z - 1 - step, y, core), main, up_recv.at[step], up_send.at[step])
            if step + 1 < lines - 1:

                @pl.when(z + 1 < lines)
                def _():
                    up(step + 1).start()

            over_y(z - 1 - step).start()
            spread(z - 1 - step, y)

        @pl.when(z + 1 + step < lines)
        def _():
            arrived(block(z + 1 + step, y, core), main, down_recv.at[step], down_send.at[step])
            if step + 1 < lines - 1:

                @pl.when(z >= 1)
                def _():
                    down(step + 1).start()

            over_y(z + 1 + step).start()
            spread(z + 1 + step, y)

    def cross(step):
        at_z = lax.rem(z + step, lines)
        arrived(block(at_z, 1 - y, core), main, y_recv.at[at_z], y_send.at[at_z])
        spread(at_z, 1 - y)

    def others(body):
        for step in range(1, lines):
            body(lax.rem(z + step, lines), y)
        for step in range(lines):
            body(lax.rem(z + step, lines), 1 - y)

    def side_arrived(at_z, at_y):
        sem = at_z * 2 + at_y
        hand(block(at_z, at_y, core), *gets, x_side.at[sem], x_side_recv.at[sem], 1 - col, "col").wait_recv()
        side_core(at_z, at_y).start()

    def multiply(c, group):
        for q in range(per):
            j = group * per + q
            picked = [held[c][rows_ref[s, 0, j]] for s in range(listed_b)]
            product = lax.dot_general(
                b_own[j], jnp.concatenate(picked, axis=1), (((0,), (1,)), ((), ())),
                preferred_element_type=jnp.float32,
            )
            sent[c][pl.ds(pl.multiple_of(j * width, width), width), :] = product.astype(jnp.bfloat16)

    def make_table():
        total = list_all[0]
        for r in range(1, row_devices):
            total = total + list_all[r]
        square = (width, width)
        by_lane = jnp.broadcast_to(total[0:1], square)
        lane = lax.broadcasted_iota(jnp.int32, square, 1)
        sub = lax.broadcasted_iota(jnp.int32, square, 0)
        keys = by_lane * width + lane

        def count(mask):
            return jnp.sum(jnp.where(mask, 1, 0), axis=0, keepdims=True)

        rank = jnp.broadcast_to(count(keys.T < keys), square)
        hit = rank.T == lane
        by_sub = by_lane.T
        order = jnp.sum(jnp.where(hit, sub, 0), axis=0, keepdims=True)
        target = jnp.sum(jnp.where(hit, by_sub, 0), axis=0, keepdims=True)
        began = count(by_sub < target)
        source, slot = order // slots, order % slots
        table[0:1, :] = source * stored + slot
        table[1:2, :] = source * stored + slots + slot % listed
        table[2:3, :] = order // listed
        table[3:4, :] = jnp.where(lane[0:1] > began, 1, 0)
        table[4:5, :] = count(by_sub <= lane) - 1
        table[5:8, :] = jnp.zeros((3, width), jnp.int32)

    def prepare(s):
        lane = lax.broadcasted_iota(jnp.int32, (part, width), 1)
        low = lane < width // 2

        @pl.loop(0, row_devices)
        def _(r):
            cut = pl.ds(s * part, part)
            middle = xr[1, r, cut, :]
            blank = jnp.zeros_like(middle)
            xt[s][r * groups, :, 0:width] = xr[0, r, cut, :]
            xt[s][r * groups, :, width : 2 * width] = jnp.where(low, middle, blank)
            xt[s][r * groups + 1, :, 0:width] = xr[2, r, cut, :]
            xt[s][r * groups + 1, :, width : 2 * width] = jnp.where(low, blank, middle)

    def contract(s):
        def step(p, run):
            weights = jnp.concatenate([a_all[picks[0, p]], a_all[picks[1, p]]], axis=1)
            product = lax.dot_general(
                xt[s][picks[2, p]], weights, CONTRACT_LAST, preferred_element_type=jnp.float32
            )
            run = product + run * picks[3, p].astype(jnp.float32)
            stack[p] = run.astype(stack.dtype)
            return run

        lax.fori_loop(0, width, step, jnp.zeros((part, tile), jnp.float32), unroll=16)

    def assemble(s, k):
        found = [[stack[picks[4, g * row_devices + 2 * k + e]] for e in range(2)] for g in range(groups)]
        for e in range(2):
            own_out[s, 2 * k + e] = jnp.concatenate([found[g][e] for g in range(groups)], axis=1)
        for g in range(groups):
            start = pl.multiple_of(k * 2 * tile, width)
            mirror_out[s, g, :, pl.ds(start, 2 * tile)] = jnp.concatenate(found[g], axis=1)

    load_b = pltpu.make_async_copy(b_ref, b_own, load_sem.at[0])
    load_a = pltpu.make_async_copy(alpha_ref, flat, load_sem.at[1])
    load_a.start()
    knock(("row", "col"))
    lane = lax.broadcasted_iota(jnp.int32, list_own.shape, 1)
    mine = jnp.zeros(list_own.shape, jnp.int32)
    for g in range(groups):
        for s in range(listed):
            mine = jnp.where(lane == row * slots + g * listed + s, lists_ref[0, g, 0, s], mine)
    list_own[...] = mine
    load_a.wait()
    for s in range(listed):
        first, second = flat[s], flat[listed + s]
        a_own[s] = first[:, :width]
        a_own[listed + s] = second[:, tile - width :]
        a_own[slots + s] = jnp.concatenate([first[:, width:], second[:, : tile - width]], axis=1)
    keep_list = pltpu.make_async_copy(list_own, list_all.at[row], l_own)
    keep_a = pltpu.make_async_copy(a_own, cut(a_all, row, 0, stored), a_sem)
    enter(("row", "col"))

    @pl.when(z + 1 < lines)
    def _():
        up(0, a_own).start()

    @pl.when(z >= 1)
    def _():
        down(0, a_own).start()

    over_y(z, a_own).start()
    over_core(z, y, a_own).start()
    if share:
        side_core(z, y, a_own).start()
    for c in range(chunks):
        for off in range(1, col_devices):

            @pl.loop(0, tiles)
            def _(t):
                send_c(c, off, t).start()

        if c == 0:

            @pl.loop(1, row_devices)
            def _(off):
                send_list(off).start()

            keep_list.start()
            keep_a.start()
            load_b.start()

        @pl.loop(0, tiles)
        def _(t):
            own_c(c, t).start()

    load_b.wait()
    move_table = pltpu.make_async_copy(table, picks, t_sem)
    relayed = 0
    for c in range(chunks):
        if relayed < lines - 1:
            relay(relayed)
            relayed += 1

        @pl.loop(0, tiles)
        def _(t):
            own_c(c, t).wait()
            for off in range(1, col_devices):
                send_c(c, off, t).wait_recv()

        @pl.loop(0, chips)
        def _(i):
            multiply(c, pair(i))

            @pl.when(i > 0)
            def _():
                send_pair(functools.partial(send_x, c), i - 1)

        send_x(c, partner_off, partner).start()
        own_x(c).start()
        if c == chunks - 1:
            for s in range(1, subs):

                @pl.loop(0, chips - 1)
                def _(i):
                    send_pair(functools.partial(send_x, c + s), i)

                send_x(c + s, partner_off, partner).start()
                own_x(c + s).start()
        if c == 0:
            keep_list.wait()

            @pl.loop(1, row_devices)
            def _(off):
                send_list(off).wait_recv()

            make_table()
            move_table.start()
            cross(0)

    for step in range(relayed, lines - 1):
        relay(step)
    for step in range(1, lines):
        cross(step)
    if share:
        others(side_arrived)
    keep_a.wait()
    move_table.wait()
    for at_z in range(lines):
        for at_y in range(2):
            at, sem = block(at_z, at_y, 1 - core), at_z * 2 + at_y
            arrived(at, main, core_recv.at[sem], core_send.at[sem])
            if share:
                arrived(at, gets, core_side_recv.at[sem], core_side.at[sem])
    for s in range(subs):
        for u in range(chunks) if s == 0 else [chunks - 1 + s]:
            own_x(u).wait()

            @pl.loop(1, row_devices)
            def _(off):
                send_x(u, off, lax.rem(row + off, row_devices)).wait_recv()

        prepare(s)
        contract(s)

        @pl.loop(0, chips)
        def _(i):
            assemble(s, pair(i))

            @pl.when(i > 0)
            def _():
                send_pair(functools.partial(send_own, s), i - 1)

        send_own(s, partner_off, partner).start()
        for off in range(1, col_devices):
            send_mirror(s, off).start()
        stay_own(s).start()
        stay_mirror(s).start()

    for step in range(lines - 1):

        @pl.when((z - step >= 0) & (z + 1 < lines))
        def _():
            up(step).wait_send()

        @pl.when((z + step < lines) & (z >= 1))
        def _():
            down(step).wait_send()

    for at_z in range(lines):
        over_y(at_z).wait_send()
        for at_y in range(2):
            over_core(at_z, at_y).wait_send()
            if share:
                side_core(at_z, at_y).wait_send()

    if share:
        others(lambda at_z, at_y: side_x(at_z, at_y).wait_send())
    for c in range(chunks):
        for off in range(1, col_devices):

            @pl.loop(0, tiles)
            def _(t):
                send_c(c, off, t).wait_send()

    @pl.loop(1, row_devices)
    def _(off):
        peer = lax.rem(row + off, row_devices)
        send_list(off).wait_send()
        for u in range(len(units)):
            send_x(u, off, peer).wait_send()
        for s in range(subs):
            send_own(s, off, peer).wait()

    for s in range(subs):
        stay_own(s).wait()
        stay_mirror(s).wait()
        for off in range(1, col_devices):
            send_mirror(s, off).wait()


def fused(c_matrix, beta_values, beta_rows, alpha_tiles, alpha_rows, row_devices, col_devices, subs, share):
    rows, columns = c_matrix.shape
    _, tiles, listed, width, _ = beta_values.shape
    slots, tile, _ = alpha_tiles.shape
    groups = alpha_rows.shape[1]
    chunks, strip = rows // width, columns // row_devices
    part, units, lines = strip // subs, rows // width - 1 + subs, row_devices // 4
    stored = slots * tile // width
    row_peers, col_peers = row_devices - 1, col_devices - 1
    dma, half = pltpu.SemaphoreType.DMA, jnp.bfloat16
    anywhere = pl.BlockSpec(memory_space=pl.ANY)
    scalars = pl.BlockSpec(memory_space=pltpu.SMEM)
    return pl.pallas_call(
        functools.partial(fused_kernel, chunks, subs, share),
        in_specs=[scalars, scalars, anywhere, anywhere, anywhere],
        out_specs=[anywhere, anywhere],
        out_shape=[
            jax.ShapeDtypeStruct((row_devices, strip, groups * tile), half),
            jax.ShapeDtypeStruct((col_devices, strip, row_devices * tile), half),
        ],
        scratch_shapes=[pltpu.VMEM((col_devices * tiles, width, width), half)] * chunks
        + [pltpu.VMEM((columns, width), half)] * chunks
        + [pltpu.VMEM((row_devices * groups, part, 2 * width), half)] * subs
        + [
            pltpu.VMEM((tiles, listed * width, width), half),
            pltpu.VMEM((slots, tile, tile), half),
            pltpu.VMEM((stored, tile, width), half),
            pltpu.VMEM((row_devices * stored, tile, width), half),
            pltpu.VMEM((chunks, row_devices, strip, width), half),
            pltpu.VMEM((row_devices * slots, part, tile), half),
            pltpu.VMEM((subs, row_devices, part, groups * tile), half),
            pltpu.VMEM((subs, groups, part, row_devices * tile), half),
            pltpu.VMEM((8, width), jnp.int32),
            pltpu.VMEM((row_devices, 8, width), jnp.int32),
            pltpu.VMEM((8, width), jnp.int32),
            pltpu.SMEM((8, width), jnp.int32),
            dma((2,)),
            dma((chunks, tiles)), dma((chunks, col_peers, tiles)), dma((chunks, col_peers, tiles)),
            dma((units,)), dma((units, row_peers)), dma((units, row_peers)),
            dma, dma((row_peers,)), dma((row_peers,)), dma,
        ]
        + [dma((lines - 1,))] * 4
        + [dma((lines,))] * 2
        + [dma((2 * lines,))] * 6
        + [
            dma,
            dma((subs,)), dma((subs, row_peers)), dma((subs, row_peers)),
            dma((subs,)), dma((subs, col_peers)), dma((subs, col_peers)),
        ],
        compiler_params=pltpu.CompilerParams(
            collective_id=0, has_side_effects=True, vmem_limit_bytes=60 << 20
        ),
        cost_estimate=pl.CostEstimate(flops=1 << 37, bytes_accessed=1 << 28, transcendentals=0),
        name="fused",
    )(
        jnp.transpose(beta_rows, (2, 0, 1)), alpha_rows, c_matrix,
        beta_values.reshape(tiles, listed * width, width), alpha_tiles,
    )


def per_device(c_matrix, beta_values, beta_rows, alpha_values, alpha_rows, gaps):
    row_devices, col_devices = lax.axis_size("row"), lax.axis_size("col")
    groups, stretch, columns = c_matrix.shape
    pairs, _, _, listed, tile, _ = alpha_values.shape
    rows, width = groups * stretch, beta_values.shape[-1]
    c_rows = c_matrix.reshape(rows, columns)
    alpha_tiles = alpha_values.reshape(pairs * groups, listed, tile, tile)
    strip, subs = columns // row_devices, 2
    own_kernels = pairs == 1 and groups == 2 and stretch == tile and 2 * tile == 3 * width
    own_kernels = own_kernels and row_devices % 4 == 0 and row_devices * groups * listed == width
    own_kernels = own_kernels and strip % (16 * subs) == 0 and 2 * strip % width == 0
    if own_kernels:
        own, mirror = fused(
            c_rows, beta_values, beta_rows, alpha_tiles.reshape(-1, tile, tile), alpha_rows,
            row_devices, col_devices, subs, SHARE,
        )
    else:
        rows_all = lax.all_gather(alpha_rows.reshape(pairs * groups, listed), "row")
        alpha_all = lax.all_gather(alpha_tiles, "row")
        xt = beta_products(lax.all_gather(c_rows, "col"), beta_values, beta_rows)
        xt = jnp.moveaxis(xt.reshape(pairs, row_devices, stretch, rows), 1, 0)
        x_strip = lax.all_to_all(xt, "row", 0, 0)[None]
        own, mirror = alpha_products(alpha_all, rows_all, x_strip, groups)
        own = lax.all_to_all(own, "row", 0, 0)
        mirror = lax.all_to_all(mirror, "col", 0, 0)
    out = final(
        own.reshape(columns, groups * stretch),
        mirror.reshape(groups * stretch, columns),
        gaps.reshape(groups * stretch, columns),
    )
    return out.reshape(gaps.shape)


def solution(mesh):
    placed = (
        P(None, "row", "col"),
        P(None, "col", None, None, None),
        P(None, "col", None),
        P(None, None, "row", None, None, None),
        P(None, None, "row", None),
        P(None, "row", "col"),
    )
    return jax.shard_map(
        per_device, mesh=mesh, in_specs=placed, out_specs=P(None, "row", "col"), check_vma=False
    )
```

```python
import functools

import jax
import jax.numpy as jnp
from jax import lax
from jax.experimental import pallas as pl
from jax.experimental.pallas import tpu as pltpu
from jax.sharding import PartitionSpec as P

CONTRACT_LAST = (((1,), (1,)), ((), ()))
SHARE = 2


def beta_kernel(listed, held, rows_ref, c_ref, b_ref, xt_ref):
    k, j = pl.program_id(0), pl.program_id(1)
    width = b_ref.shape[-1]
    picked = []
    for z in range(listed):
        tile = rows_ref[k, j, z]
        owner = tile // held
        start = pl.multiple_of((tile - owner * held) * width, width)
        picked.append(c_ref[owner, :, pl.ds(start, width)])
    lhs = b_ref[0, 0].reshape(listed * width, width)
    product = lax.dot_general(
        lhs, jnp.concatenate(picked, axis=1), (((0,), (1,)), ((), ())),
        preferred_element_type=jnp.float32,
    )
    xt_ref[0] = product.astype(xt_ref.dtype)


def beta_products(gathered, beta_values, beta_rows):
    pairs, tiles, listed, width, _ = beta_values.shape
    owners, rows, columns = gathered.shape
    return pl.pallas_call(
        functools.partial(beta_kernel, listed, columns // width),
        grid_spec=pltpu.PrefetchScalarGridSpec(
            num_scalar_prefetch=1,
            grid=(pairs, tiles),
            in_specs=[
                pl.BlockSpec((owners, rows, columns), lambda k, j, s: (0, 0, 0)),
                pl.BlockSpec((1, 1, listed, width, width), lambda k, j, s: (k, j, 0, 0, 0)),
            ],
            out_specs=pl.BlockSpec((1, width, rows), lambda k, j, s: (k, j, 0)),
        ),
        out_shape=jax.ShapeDtypeStruct((pairs, tiles * width, rows), jnp.bfloat16),
        compiler_params=pltpu.CompilerParams(vmem_limit_bytes=56 << 20),
        name="beta_products",
    )(beta_rows, gathered, beta_values)


def alpha_kernel(groups, rows_ref, a_ref, x_ref, own_ref, mirror_ref, acc_ref):
    r = pl.program_id(0)
    row_devices = pl.num_programs(0)
    pairs = x_ref.shape[2]
    listed, tile = rows_ref.shape[2], acc_ref.shape[1]

    @pl.when(r == 0)
    def _():
        acc_ref[...] = jnp.zeros_like(acc_ref)

    for i in range(x_ref.shape[1]):
        at = r * x_ref.shape[1] + i
        for k in range(pairs):
            parts = [x_ref[c, i, k] for c in range(x_ref.shape[0])]
            merged = jnp.concatenate(parts, axis=1) if len(parts) > 1 else parts[0]
            for g in range(groups):
                x = merged[:, g * tile : (g + 1) * tile]
                slot = k * groups + g

                @pl.loop(0, listed)
                def _(z):
                    acc_ref[rows_ref[at, slot, z]] += lax.dot_general(
                        a_ref[i, slot, z], x, CONTRACT_LAST, preferred_element_type=jnp.float32
                    )

    @pl.when(r == row_devices - 1)
    def _():
        count = acc_ref.shape[0] // groups
        for g in range(groups):
            for to in range(count):
                turned = acc_ref[g * count + to].astype(own_ref.dtype).T
                own_ref[to, :, g * tile : (g + 1) * tile] = turned
                mirror_ref[g, :, to * tile : (to + 1) * tile] = turned


def alpha_products(alpha_all, rows_all, x_strip, groups):
    row_devices, rest = alpha_all.shape[0], alpha_all.shape[1:]
    tile = x_strip.shape[0] * x_strip.shape[-1] // groups
    per = 1
    chunks, _, pairs, strip, chunk = x_strip.shape
    return pl.pallas_call(
        functools.partial(alpha_kernel, groups),
        grid_spec=pltpu.PrefetchScalarGridSpec(
            num_scalar_prefetch=1,
            grid=(row_devices // per,),
            in_specs=[
                pl.BlockSpec((per,) + rest, lambda r, s: (r,) + (0,) * len(rest)),
                pl.BlockSpec((chunks, per, pairs, strip, chunk), lambda r, s: (0, r, 0, 0, 0)),
            ],
            out_specs=[
                pl.BlockSpec((row_devices, strip, groups * tile), lambda r, s: (0, 0, 0)),
                pl.BlockSpec((groups, strip, row_devices * tile), lambda r, s: (0, 0, 0)),
            ],
            scratch_shapes=[pltpu.VMEM((groups * row_devices, tile, strip), jnp.float32)],
        ),
        out_shape=[
            jax.ShapeDtypeStruct((row_devices, strip, groups * tile), jnp.bfloat16),
            jax.ShapeDtypeStruct((groups, strip, row_devices * tile), jnp.bfloat16),
        ],
        compiler_params=pltpu.CompilerParams(vmem_limit_bytes=56 << 20),
        name="alpha_products",
    )(rows_all, alpha_all, x_strip)


def final_kernel(block, own_ref, mirror_ref, gaps_ref, out_ref, own, mirror, gaps, out, in_sem, out_sem):
    steps = out.shape[1] // block

    def fetch(i):
        span = pl.ds(i * block, block)
        pairs = (
            (gaps_ref.at[:, span], gaps.at[:, span]), (own_ref.at[span, :], own.at[span, :]),
            (mirror_ref.at[:, span], mirror.at[:, span]),
        )
        return [pltpu.make_async_copy(*pair, in_sem.at[n, i]) for n, pair in enumerate(pairs)]

    def store(i):
        span = pl.ds(i * block, block)
        return pltpu.make_async_copy(out.at[:, span], out_ref.at[:, span], out_sem.at[i])

    for i in range(steps):
        for copy in fetch(i):
            copy.start()
    for i in range(steps):
        for copy in fetch(i):
            copy.wait()
        span = slice(i * block, (i + 1) * block)
        turned = own[span, :].T.astype(jnp.float32)
        out[:, span] = (turned + mirror[:, span].astype(jnp.float32)) / gaps[:, span]
        store(i).start()
    for i in range(steps):
        store(i).wait()


def final(own, mirror, gaps):
    rows, columns = gaps.shape
    block = next(n for n in (768, 384, 256, 128) if columns % n == 0)
    dma, anywhere = pltpu.SemaphoreType.DMA, pl.BlockSpec(memory_space=pl.ANY)
    return pl.pallas_call(
        functools.partial(final_kernel, block),
        in_specs=[anywhere] * 3,
        out_specs=anywhere,
        out_shape=jax.ShapeDtypeStruct((rows, columns), jnp.float32),
        scratch_shapes=[
            pltpu.VMEM(own.shape, own.dtype), pltpu.VMEM(mirror.shape, mirror.dtype),
            pltpu.VMEM(gaps.shape, gaps.dtype), pltpu.VMEM(gaps.shape, gaps.dtype),
            dma((3, columns // block)), dma((columns // block,)),
        ],
        name="final",
    )(own, mirror, gaps)


def remote(src, dst, send_sem, recv_sem, axis, peer):
    return pltpu.make_async_remote_copy(
        src_ref=src, dst_ref=dst, send_sem=send_sem, recv_sem=recv_sem,
        device_id={axis: peer}, device_id_type=pl.DeviceIdType.MESH,
    )


def fused_kernel(chunks, subs, share, rows_ref, lists_ref, c_ref, b_ref, alpha_ref, own_ref, mirror_ref, *scratch):
    held, sent, xt = scratch[:chunks], scratch[chunks : 2 * chunks], scratch[2 * chunks : 2 * chunks + subs]
    (b_own, flat, a_own, a_all, xr, stack, own_out, mirror_out, list_own, list_all, table, picks,
     load_sem, c_own, c_send, c_recv, x_own, x_send, x_recv, l_own, l_send, l_recv, a_sem,
     up_send, up_recv, down_send, down_recv, y_send, y_recv, core_send, core_recv,
     x_side, x_side_recv, core_side, core_side_recv, t_sem,
     o_own, o_send, o_recv, m_own, m_send, m_recv, rounds) = scratch[2 * chunks + subs :]
    row_devices, row = lax.axis_size("row"), lax.axis_index("row")
    col_devices, col = lax.axis_size("col"), lax.axis_index("col")
    rows, columns = c_ref.shape
    tiles, depth, width = b_own.shape
    listed_b = depth // width
    slots, tile, _ = flat.shape
    groups = lists_ref.shape[1]
    listed = slots // groups
    chunk, strip = rows // chunks, columns // row_devices
    part = strip // subs
    chips = row_devices // 2
    per = tiles // chips
    stored = a_own.shape[0]
    lines = row_devices // 4
    chip, core = row // 2, lax.rem(row, 2)
    z, y = row // 4, lax.rem(chip, 2)
    units = [(c, 0, strip) for c in range(chunks - 1)]
    units += [(chunks - 1, s * part, part) for s in range(subs)]

    def own_c(c, t):
        return pltpu.make_async_copy(
            c_ref.at[pl.ds(c * chunk, chunk), pl.ds(pl.multiple_of(t * width, width), width)],
            held[c].at[col * tiles + t], c_own.at[c, t],
        )

    def send_c(c, off, t):
        return remote(
            c_ref.at[pl.ds(c * chunk, chunk), pl.ds(pl.multiple_of(t * width, width), width)],
            held[c].at[col * tiles + t], c_send.at[c, off - 1, t], c_recv.at[c, off - 1, t],
            "col", lax.rem(col + off, col_devices),
        )

    def send_x(u, off, peer):
        c, first, size = units[u]
        start = pl.multiple_of(peer * strip + first, 16)
        return remote(
            sent[c].at[pl.ds(start, size), :], xr.at[c, row, pl.ds(first, size), :],
            x_send.at[u, off - 1], x_recv.at[u, off - 1], "row", peer,
        )

    def own_x(u):
        c, first, size = units[u]
        start = pl.multiple_of(row * strip + first, 16)
        return pltpu.make_async_copy(
            sent[c].at[pl.ds(start, size), :], xr.at[c, row, pl.ds(first, size), :], x_own.at[u]
        )

    def send_own(s, off, peer):
        return remote(
            own_out.at[s, peer], own_ref.at[row, pl.ds(s * part, part), :],
            o_send.at[s, off - 1], o_recv.at[s, off - 1], "row", peer,
        )

    def stay_own(s):
        return pltpu.make_async_copy(
            own_out.at[s, row], own_ref.at[row, pl.ds(s * part, part), :], o_own.at[s]
        )

    def send_mirror(s, off):
        peer = lax.rem(col + off, col_devices)
        return remote(
            mirror_out.at[s, peer], mirror_ref.at[col, pl.ds(s * part, part), :],
            m_send.at[s, off - 1], m_recv.at[s, off - 1], "col", peer,
        )

    def stay_mirror(s):
        return pltpu.make_async_copy(
            mirror_out.at[s, col], mirror_ref.at[col, pl.ds(s * part, part), :], m_own.at[s]
        )

    def send_list(off):
        return remote(
            list_own, list_all.at[row], l_send.at[off - 1], l_recv.at[off - 1], "row",
            lax.rem(row + off, row_devices),
        )

    def reach(i):
        odd = lax.rem(i, 2)
        return chips // 2 + (1 - odd) * (i // 2) - odd * ((i + 1) // 2)

    def pair(i):
        return lax.rem(chip + reach(i), chips)

    def send_pair(send, i):
        for e in range(2):
            send(2 * reach(i) + e - core, 2 * pair(i) + e).start()

    def block(at_z, at_y, at_core):
        return (at_z * 2 + at_y) * 2 + at_core

    def neighbours(act):
        act("col", 1 - col)
        act("row", block(z, y, 1 - core))
        act("row", block(z, 1 - y, core))

        @pl.when(z >= 1)
        def _():
            act("row", block(z - 1, y, core))

        @pl.when(z + 1 < lines)
        def _():
            act("row", block(z + 1, y, core))

    inner = lax.min(z, 1) + lax.min(lines - 1 - z, 1)

    def signal_near(sem):
        def act(axis, peer):
            pl.semaphore_signal(
                sem, inc=1, device_id={axis: peer}, device_id_type=pl.DeviceIdType.MESH
            )

        neighbours(act)

    def meet(sem):
        signal_near(sem)
        pl.semaphore_wait(sem, 3 + inner)

    partner, partner_off = row + 1 - 2 * core, 1 + core * (row_devices - 2)

    def cut(ref, at, first, size):
        return ref.at[pl.ds(at * stored + first, size)]

    def hand(at, first, size, send_sem, recv_sem, peer, axis="row", source=None):
        held_part = cut(a_all, at, first, size)
        if source is not None:
            held_part = source.at[pl.ds(first, size)]
        return remote(held_part, cut(a_all, at, first, size), send_sem, recv_sem, axis, peer)

    main = (col * share, stored - share)
    gives, gets = (col * (stored - share), share), ((1 - col) * (stored - share), share)
    other_core = block(z, y, 1 - core)

    def up(step, source=None):
        at = block(z - step, y, core)
        return hand(at, *main, up_send.at[step], up_recv.at[step], block(z + 1, y, core), source=source)

    def down(step, source=None):
        at = block(z + step, y, core)
        return hand(at, *main, down_send.at[step], down_recv.at[step], block(z - 1, y, core), source=source)

    def over_y(at_z, source=None):
        at = block(at_z, y, core)
        return hand(at, *main, y_send.at[at_z], y_recv.at[at_z], block(z, 1 - y, core), source=source)

    def over_core(at_z, at_y, source=None):
        at, sem = block(at_z, at_y, core), at_z * 2 + at_y
        return hand(at, *main, core_send.at[sem], core_recv.at[sem], other_core, source=source)

    def side_x(at_z, at_y):
        at, sem = block(at_z, at_y, core), at_z * 2 + at_y
        return hand(at, *gives, x_side.at[sem], x_side_recv.at[sem], 1 - col, "col")

    def side_core(at_z, at_y, source=None):
        at, sem = block(at_z, at_y, core), at_z * 2 + at_y
        return hand(at, *gets, core_side.at[sem], core_side_recv.at[sem], other_core, source=source)

    def arrived(at, span, recv_sem, send_sem):
        hand(at, *span, send_sem, recv_sem, other_core).wait_recv()

    def spread(at_z, at_y):
        over_core(at_z, at_y).start()
        if share:
            side_x(at_z, at_y).start()

    def relay(step):
        @pl.when(z - 1 - step >= 0)
        def _():
            arrived(block(z - 1 - step, y, core), main, up_recv.at[step], up_send.at[step])
            if step + 1 < lines - 1:

                @pl.when(z + 1 < lines)
                def _():
                    up(step + 1).start()

            over_y(z - 1 - step).start()
            spread(z - 1 - step, y)

        @pl.when(z + 1 + step < lines)
        def _():
            arrived(block(z + 1 + step, y, core), main, down_recv.at[step], down_send.at[step])
            if step + 1 < lines - 1:

                @pl.when(z >= 1)
                def _():
                    down(step + 1).start()

            over_y(z + 1 + step).start()
            spread(z + 1 + step, y)

    def cross(step):
        at_z = lax.rem(z + step, lines)
        arrived(block(at_z, 1 - y, core), main, y_recv.at[at_z], y_send.at[at_z])
        spread(at_z, 1 - y)

    def others(body):
        for step in range(1, lines):
            body(lax.rem(z + step, lines), y)
        for step in range(lines):
            body(lax.rem(z + step, lines), 1 - y)

    def side_arrived(at_z, at_y):
        sem = at_z * 2 + at_y
        hand(block(at_z, at_y, core), *gets, x_side.at[sem], x_side_recv.at[sem], 1 - col, "col").wait_recv()
        side_core(at_z, at_y).start()

    def multiply(c, group):
        for q in range(per):
            j = group * per + q
            picked = [held[c][rows_ref[s, 0, j]] for s in range(listed_b)]
            product = lax.dot_general(
                b_own[j], jnp.concatenate(picked, axis=1), (((0,), (1,)), ((), ())),
                preferred_element_type=jnp.float32,
            )
            sent[c][pl.ds(pl.multiple_of(j * width, width), width), :] = product.astype(jnp.bfloat16)

    def make_table():
        total = list_all[0]
        for r in range(1, row_devices):
            total = total + list_all[r]
        square = (width, width)
        by_lane = jnp.broadcast_to(total[0:1], square)
        lane = lax.broadcasted_iota(jnp.int32, square, 1)
        sub = lax.broadcasted_iota(jnp.int32, square, 0)
        keys = by_lane * width + lane

        def count(mask):
            return jnp.sum(jnp.where(mask, 1, 0), axis=0, keepdims=True)

        rank = jnp.broadcast_to(count(keys.T < keys), square)
        hit = rank.T == lane
        by_sub = by_lane.T
        order = jnp.sum(jnp.where(hit, sub, 0), axis=0, keepdims=True)
        target = jnp.sum(jnp.where(hit, by_sub, 0), axis=0, keepdims=True)
        began = count(by_sub < target)
        source, slot = order // slots, order % slots
        table[0:1, :] = source * stored + slot
        table[1:2, :] = source * stored + slots + slot % listed
        table[2:3, :] = order // listed
        table[3:4, :] = jnp.where(lane[0:1] > began, 1, 0)
        table[4:5, :] = count(by_sub <= lane) - 1
        table[5:8, :] = jnp.zeros((3, width), jnp.int32)

    def prepare(s):
        lane = lax.broadcasted_iota(jnp.int32, (part, width), 1)
        low = lane < width // 2

        @pl.loop(0, row_devices)
        def _(r):
            cut = pl.ds(s * part, part)
            middle = xr[1, r, cut, :]
            blank = jnp.zeros_like(middle)
            xt[s][r * groups, :, 0:width] = xr[0, r, cut, :]
            xt[s][r * groups, :, width : 2 * width] = jnp.where(low, middle, blank)
            xt[s][r * groups + 1, :, 0:width] = xr[2, r, cut, :]
            xt[s][r * groups + 1, :, width : 2 * width] = jnp.where(low, blank, middle)

    def contract(s):
        def step(p, run):
            weights = jnp.concatenate([a_all[picks[0, p]], a_all[picks[1, p]]], axis=1)
            product = lax.dot_general(
                xt[s][picks[2, p]], weights, CONTRACT_LAST, preferred_element_type=jnp.float32
            )
            run = product + run * picks[3, p].astype(jnp.float32)
            stack[p] = run.astype(stack.dtype)
            return run

        lax.fori_loop(0, width, step, jnp.zeros((part, tile), jnp.float32), unroll=16)

    def assemble(s, k):
        found = [[stack[picks[4, g * row_devices + 2 * k + e]] for e in range(2)] for g in range(groups)]
        for e in range(2):
            own_out[s, 2 * k + e] = jnp.concatenate([found[g][e] for g in range(groups)], axis=1)
        for g in range(groups):
            start = pl.multiple_of(k * 2 * tile, width)
            mirror_out[s, g, :, pl.ds(start, 2 * tile)] = jnp.concatenate(found[g], axis=1)

    load_b = pltpu.make_async_copy(b_ref, b_own, load_sem.at[0])
    load_a = pltpu.make_async_copy(alpha_ref, flat, load_sem.at[1])
    load_a.start()
    barrier = pltpu.get_barrier_semaphore()
    signal_near(barrier)
    lane = lax.broadcasted_iota(jnp.int32, list_own.shape, 1)
    mine = jnp.zeros(list_own.shape, jnp.int32)
    for g in range(groups):
        for s in range(listed):
            mine = jnp.where(lane == row * slots + g * listed + s, lists_ref[0, g, 0, s], mine)
    list_own[...] = mine
    load_a.wait()
    for s in range(listed):
        first, second = flat[s], flat[listed + s]
        a_own[s] = first[:, :width]
        a_own[listed + s] = second[:, tile - width :]
        a_own[slots + s] = jnp.concatenate([first[:, width:], second[:, : tile - width]], axis=1)
    keep_list = pltpu.make_async_copy(list_own, list_all.at[row], l_own)
    keep_a = pltpu.make_async_copy(a_own, cut(a_all, row, 0, stored), a_sem)
    pl.semaphore_wait(barrier, 3 + inner)

    @pl.when(z + 1 < lines)
    def _():
        up(0, a_own).start()

    @pl.when(z >= 1)
    def _():
        down(0, a_own).start()

    over_y(z, a_own).start()
    over_core(z, y, a_own).start()
    if share:
        side_core(z, y, a_own).start()
    for c in range(chunks):
        for off in range(1, col_devices):

            @pl.loop(0, tiles)
            def _(t):
                send_c(c, off, t).start()

        if c == 0:
            keep_list.start()
            keep_a.start()
            load_b.start()

        @pl.loop(0, tiles)
        def _(t):
            own_c(c, t).start()

    for n in range(lines):
        meet(rounds.at[n])

    @pl.loop(1, row_devices)
    def _(off):
        send_list(off).start()

    load_b.wait()
    move_table = pltpu.make_async_copy(table, picks, t_sem)
    relayed = 0
    for c in range(chunks):
        if relayed < lines - 1:
            relay(relayed)
            relayed += 1

        @pl.loop(0, tiles)
        def _(t):
            own_c(c, t).wait()
            for off in range(1, col_devices):
                send_c(c, off, t).wait_recv()

        @pl.loop(0, chips)
        def _(i):
            multiply(c, pair(i))

            @pl.when(i > 0)
            def _():
                send_pair(functools.partial(send_x, c), i - 1)

        send_x(c, partner_off, partner).start()
        own_x(c).start()
        if c == chunks - 1:
            for s in range(1, subs):

                @pl.loop(0, chips - 1)
                def _(i):
                    send_pair(functools.partial(send_x, c + s), i)

                send_x(c + s, partner_off, partner).start()
                own_x(c + s).start()
        if c == 0:
            keep_list.wait()

            @pl.loop(1, row_devices)
            def _(off):
                send_list(off).wait_recv()

            make_table()
            move_table.start()
            cross(0)

    for step in range(relayed, lines - 1):
        relay(step)
    for step in range(1, lines):
        cross(step)
    if share:
        others(side_arrived)
    keep_a.wait()
    move_table.wait()
    for at_z in range(lines):
        for at_y in range(2):
            at, sem = block(at_z, at_y, 1 - core), at_z * 2 + at_y
            arrived(at, main, core_recv.at[sem], core_send.at[sem])
            if share:
                arrived(at, gets, core_side_recv.at[sem], core_side.at[sem])
    for s in range(subs):
        for u in range(chunks) if s == 0 else [chunks - 1 + s]:
            own_x(u).wait()

            @pl.loop(1, row_devices)
            def _(off):
                send_x(u, off, lax.rem(row + off, row_devices)).wait_recv()

        prepare(s)
        contract(s)

        @pl.loop(0, chips)
        def _(i):
            assemble(s, pair(i))

            @pl.when(i > 0)
            def _():
                send_pair(functools.partial(send_own, s), i - 1)

        send_own(s, partner_off, partner).start()
        for off in range(1, col_devices):
            send_mirror(s, off).start()
        stay_own(s).start()
        stay_mirror(s).start()

    for step in range(lines - 1):

        @pl.when((z - step >= 0) & (z + 1 < lines))
        def _():
            up(step).wait_send()

        @pl.when((z + step < lines) & (z >= 1))
        def _():
            down(step).wait_send()

    for at_z in range(lines):
        over_y(at_z).wait_send()
        for at_y in range(2):
            over_core(at_z, at_y).wait_send()
            if share:
                side_core(at_z, at_y).wait_send()

    if share:
        others(lambda at_z, at_y: side_x(at_z, at_y).wait_send())
    for c in range(chunks):
        for off in range(1, col_devices):

            @pl.loop(0, tiles)
            def _(t):
                send_c(c, off, t).wait_send()

    @pl.loop(1, row_devices)
    def _(off):
        peer = lax.rem(row + off, row_devices)
        send_list(off).wait_send()
        for u in range(len(units)):
            send_x(u, off, peer).wait_send()
        for s in range(subs):
            send_own(s, off, peer).wait()

    for s in range(subs):
        stay_own(s).wait()
        stay_mirror(s).wait()
        for off in range(1, col_devices):
            send_mirror(s, off).wait()


def fused(c_matrix, beta_values, beta_rows, alpha_tiles, alpha_rows, row_devices, col_devices, subs, share):
    rows, columns = c_matrix.shape
    _, tiles, listed, width, _ = beta_values.shape
    slots, tile, _ = alpha_tiles.shape
    groups = alpha_rows.shape[1]
    chunks, strip = rows // width, columns // row_devices
    part, units, lines = strip // subs, rows // width - 1 + subs, row_devices // 4
    stored = slots * tile // width
    row_peers, col_peers = row_devices - 1, col_devices - 1
    dma, half = pltpu.SemaphoreType.DMA, jnp.bfloat16
    anywhere = pl.BlockSpec(memory_space=pl.ANY)
    scalars = pl.BlockSpec(memory_space=pltpu.SMEM)
    return pl.pallas_call(
        functools.partial(fused_kernel, chunks, subs, share),
        in_specs=[scalars, scalars, anywhere, anywhere, anywhere],
        out_specs=[anywhere, anywhere],
        out_shape=[
            jax.ShapeDtypeStruct((row_devices, strip, groups * tile), half),
            jax.ShapeDtypeStruct((col_devices, strip, row_devices * tile), half),
        ],
        scratch_shapes=[pltpu.VMEM((col_devices * tiles, width, width), half)] * chunks
        + [pltpu.VMEM((columns, width), half)] * chunks
        + [pltpu.VMEM((row_devices * groups, part, 2 * width), half)] * subs
        + [
            pltpu.VMEM((tiles, listed * width, width), half),
            pltpu.VMEM((slots, tile, tile), half),
            pltpu.VMEM((stored, tile, width), half),
            pltpu.VMEM((row_devices * stored, tile, width), half),
            pltpu.VMEM((chunks, row_devices, strip, width), half),
            pltpu.VMEM((row_devices * slots, part, tile), half),
            pltpu.VMEM((subs, row_devices, part, groups * tile), half),
            pltpu.VMEM((subs, groups, part, row_devices * tile), half),
            pltpu.VMEM((8, width), jnp.int32),
            pltpu.VMEM((row_devices, 8, width), jnp.int32),
            pltpu.VMEM((8, width), jnp.int32),
            pltpu.SMEM((8, width), jnp.int32),
            dma((2,)),
            dma((chunks, tiles)), dma((chunks, col_peers, tiles)), dma((chunks, col_peers, tiles)),
            dma((units,)), dma((units, row_peers)), dma((units, row_peers)),
            dma, dma((row_peers,)), dma((row_peers,)), dma,
        ]
        + [dma((lines - 1,))] * 4
        + [dma((lines,))] * 2
        + [dma((2 * lines,))] * 6
        + [
            dma,
            dma((subs,)), dma((subs, row_peers)), dma((subs, row_peers)),
            dma((subs,)), dma((subs, col_peers)), dma((subs, col_peers)),
            pltpu.SemaphoreType.REGULAR((lines,)),
        ],
        compiler_params=pltpu.CompilerParams(
            collective_id=0, has_side_effects=True, vmem_limit_bytes=60 << 20
        ),
        cost_estimate=pl.CostEstimate(flops=1 << 37, bytes_accessed=1 << 28, transcendentals=0),
        name="fused",
    )(
        jnp.transpose(beta_rows, (2, 0, 1)), alpha_rows, c_matrix,
        beta_values.reshape(tiles, listed * width, width), alpha_tiles,
    )


def per_device(c_matrix, beta_values, beta_rows, alpha_values, alpha_rows, gaps):
    row_devices, col_devices = lax.axis_size("row"), lax.axis_size("col")
    groups, stretch, columns = c_matrix.shape
    pairs, _, _, listed, tile, _ = alpha_values.shape
    rows, width = groups * stretch, beta_values.shape[-1]
    c_rows = c_matrix.reshape(rows, columns)
    alpha_tiles = alpha_values.reshape(pairs * groups, listed, tile, tile)
    strip, subs = columns // row_devices, 2
    own_kernels = pairs == 1 and groups == 2 and stretch == tile and 2 * tile == 3 * width
    own_kernels = own_kernels and row_devices % 4 == 0 and row_devices * groups * listed == width
    own_kernels = own_kernels and strip % (16 * subs) == 0 and 2 * strip % width == 0
    if own_kernels:
        own, mirror = fused(
            c_rows, beta_values, beta_rows, alpha_tiles.reshape(-1, tile, tile), alpha_rows,
            row_devices, col_devices, subs, SHARE,
        )
    else:
        rows_all = lax.all_gather(alpha_rows.reshape(pairs * groups, listed), "row")
        alpha_all = lax.all_gather(alpha_tiles, "row")
        xt = beta_products(lax.all_gather(c_rows, "col"), beta_values, beta_rows)
        xt = jnp.moveaxis(xt.reshape(pairs, row_devices, stretch, rows), 1, 0)
        x_strip = lax.all_to_all(xt, "row", 0, 0)[None]
        own, mirror = alpha_products(alpha_all, rows_all, x_strip, groups)
        own = lax.all_to_all(own, "row", 0, 0)
        mirror = lax.all_to_all(mirror, "col", 0, 0)
    out = final(
        own.reshape(columns, groups * stretch),
        mirror.reshape(groups * stretch, columns),
        gaps.reshape(groups * stretch, columns),
    )
    return out.reshape(gaps.shape)


def solution(mesh):
    placed = (
        P(None, "row", "col"),
        P(None, "col", None, None, None),
        P(None, "col", None),
        P(None, None, "row", None, None, None),
        P(None, None, "row", None),
        P(None, "row", "col"),
    )
    return jax.shard_map(
        per_device, mesh=mesh, in_specs=placed, out_specs=P(None, "row", "col"), check_vma=False
    )
```

```python
import functools

import jax
import jax.numpy as jnp
from jax import lax
from jax.experimental import pallas as pl
from jax.experimental.pallas import tpu as pltpu
from jax.sharding import PartitionSpec as P

CONTRACT_LAST = (((1,), (1,)), ((), ()))
SHARE = (2, 2)


def beta_kernel(listed, held, rows_ref, c_ref, b_ref, xt_ref):
    k, j = pl.program_id(0), pl.program_id(1)
    width = b_ref.shape[-1]
    picked = []
    for z in range(listed):
        tile = rows_ref[k, j, z]
        owner = tile // held
        start = pl.multiple_of((tile - owner * held) * width, width)
        picked.append(c_ref[owner, :, pl.ds(start, width)])
    lhs = b_ref[0, 0].reshape(listed * width, width)
    product = lax.dot_general(
        lhs, jnp.concatenate(picked, axis=1), (((0,), (1,)), ((), ())),
        preferred_element_type=jnp.float32,
    )
    xt_ref[0] = product.astype(xt_ref.dtype)


def beta_products(gathered, beta_values, beta_rows):
    pairs, tiles, listed, width, _ = beta_values.shape
    owners, rows, columns = gathered.shape
    return pl.pallas_call(
        functools.partial(beta_kernel, listed, columns // width),
        grid_spec=pltpu.PrefetchScalarGridSpec(
            num_scalar_prefetch=1,
            grid=(pairs, tiles),
            in_specs=[
                pl.BlockSpec((owners, rows, columns), lambda k, j, s: (0, 0, 0)),
                pl.BlockSpec((1, 1, listed, width, width), lambda k, j, s: (k, j, 0, 0, 0)),
            ],
            out_specs=pl.BlockSpec((1, width, rows), lambda k, j, s: (k, j, 0)),
        ),
        out_shape=jax.ShapeDtypeStruct((pairs, tiles * width, rows), jnp.bfloat16),
        compiler_params=pltpu.CompilerParams(vmem_limit_bytes=56 << 20),
        name="beta_products",
    )(beta_rows, gathered, beta_values)


def alpha_kernel(groups, rows_ref, a_ref, x_ref, own_ref, mirror_ref, acc_ref):
    r = pl.program_id(0)
    row_devices = pl.num_programs(0)
    pairs = x_ref.shape[2]
    listed, tile = rows_ref.shape[2], acc_ref.shape[1]

    @pl.when(r == 0)
    def _():
        acc_ref[...] = jnp.zeros_like(acc_ref)

    for i in range(x_ref.shape[1]):
        at = r * x_ref.shape[1] + i
        for k in range(pairs):
            parts = [x_ref[c, i, k] for c in range(x_ref.shape[0])]
            merged = jnp.concatenate(parts, axis=1) if len(parts) > 1 else parts[0]
            for g in range(groups):
                x = merged[:, g * tile : (g + 1) * tile]
                slot = k * groups + g

                @pl.loop(0, listed)
                def _(z):
                    acc_ref[rows_ref[at, slot, z]] += lax.dot_general(
                        a_ref[i, slot, z], x, CONTRACT_LAST, preferred_element_type=jnp.float32
                    )

    @pl.when(r == row_devices - 1)
    def _():
        count = acc_ref.shape[0] // groups
        for g in range(groups):
            for to in range(count):
                turned = acc_ref[g * count + to].astype(own_ref.dtype).T
                own_ref[to, :, g * tile : (g + 1) * tile] = turned
                mirror_ref[g, :, to * tile : (to + 1) * tile] = turned


def alpha_products(alpha_all, rows_all, x_strip, groups):
    row_devices, rest = alpha_all.shape[0], alpha_all.shape[1:]
    tile = x_strip.shape[0] * x_strip.shape[-1] // groups
    per = 1
    chunks, _, pairs, strip, chunk = x_strip.shape
    return pl.pallas_call(
        functools.partial(alpha_kernel, groups),
        grid_spec=pltpu.PrefetchScalarGridSpec(
            num_scalar_prefetch=1,
            grid=(row_devices // per,),
            in_specs=[
                pl.BlockSpec((per,) + rest, lambda r, s: (r,) + (0,) * len(rest)),
                pl.BlockSpec((chunks, per, pairs, strip, chunk), lambda r, s: (0, r, 0, 0, 0)),
            ],
            out_specs=[
                pl.BlockSpec((row_devices, strip, groups * tile), lambda r, s: (0, 0, 0)),
                pl.BlockSpec((groups, strip, row_devices * tile), lambda r, s: (0, 0, 0)),
            ],
            scratch_shapes=[pltpu.VMEM((groups * row_devices, tile, strip), jnp.float32)],
        ),
        out_shape=[
            jax.ShapeDtypeStruct((row_devices, strip, groups * tile), jnp.bfloat16),
            jax.ShapeDtypeStruct((groups, strip, row_devices * tile), jnp.bfloat16),
        ],
        compiler_params=pltpu.CompilerParams(vmem_limit_bytes=56 << 20),
        name="alpha_products",
    )(rows_all, alpha_all, x_strip)


def final_kernel(block, own, mirror, gaps, out_ref, out, out_sem):
    steps = out.shape[1] // block

    def store(i):
        span = pl.ds(i * block, block)
        return pltpu.make_async_copy(out.at[:, span], out_ref.at[:, span], out_sem.at[i])

    for i in range(steps):
        span = slice(i * block, (i + 1) * block)
        turned = own[span, :].T.astype(jnp.float32)
        out[:, span] = (turned + mirror[:, span].astype(jnp.float32)) / gaps[:, span]
        store(i).start()
    for i in range(steps):
        store(i).wait()


def final(own, mirror, gaps):
    rows, columns = gaps.shape
    block = next(n for n in (384, 256, 128) if columns % n == 0)
    whole = pl.BlockSpec(memory_space=pltpu.VMEM)
    return pl.pallas_call(
        functools.partial(final_kernel, block),
        in_specs=[whole] * 3,
        out_specs=pl.BlockSpec(memory_space=pl.ANY),
        out_shape=jax.ShapeDtypeStruct((rows, columns), jnp.float32),
        scratch_shapes=[
            pltpu.VMEM(gaps.shape, gaps.dtype), pltpu.SemaphoreType.DMA((columns // block,)),
        ],
        compiler_params=pltpu.CompilerParams(vmem_limit_bytes=20 << 20),
        name="final",
    )(own, mirror, gaps)


def remote(src, dst, send_sem, recv_sem, axis, peer):
    return pltpu.make_async_remote_copy(
        src_ref=src, dst_ref=dst, send_sem=send_sem, recv_sem=recv_sem,
        device_id={axis: peer}, device_id_type=pl.DeviceIdType.MESH,
    )


def fused_kernel(chunks, subs, share, rows_ref, lists_ref, c_ref, b_ref, alpha_ref, own_ref, mirror_ref, *scratch):
    held, sent, xt = scratch[:chunks], scratch[chunks : 2 * chunks], scratch[2 * chunks : 2 * chunks + subs]
    (b_own, flat, a_own, a_all, xr, stack, own_out, mirror_out, list_own, list_all, table, picks,
     load_sem, c_own, c_send, c_recv, x_own, x_send, x_recv, l_own, l_send, l_recv, a_sem,
     up_send, up_recv, down_send, down_recv, y_send, y_recv, core_send, core_recv,
     x_side, x_side_recv, core_side, core_side_recv, t_sem,
     o_own, o_send, o_recv, m_own, m_send, m_recv, rounds) = scratch[2 * chunks + subs :]
    row_devices, row = lax.axis_size("row"), lax.axis_index("row")
    col_devices, col = lax.axis_size("col"), lax.axis_index("col")
    rows, columns = c_ref.shape
    tiles, depth, width = b_own.shape
    listed_b = depth // width
    slots, tile, _ = flat.shape
    groups = lists_ref.shape[1]
    listed = slots // groups
    chunk, strip = rows // chunks, columns // row_devices
    part = strip // subs
    chips = row_devices // 2
    per = tiles // chips
    stored = a_own.shape[0]
    lines = row_devices // 4
    chip, core = row // 2, lax.rem(row, 2)
    z, y = row // 4, lax.rem(chip, 2)
    units = [(c, s * part, part) for s in range(subs) for c in range(chunks)]
    straight, turned = range(2, chips, 2), range(1, chips, 2)

    def own_c(c, t):
        return pltpu.make_async_copy(
            c_ref.at[pl.ds(c * chunk, chunk), pl.ds(pl.multiple_of(t * width, width), width)],
            held[c].at[col * tiles + t], c_own.at[c, t],
        )

    def send_c(c, off, t):
        return remote(
            c_ref.at[pl.ds(c * chunk, chunk), pl.ds(pl.multiple_of(t * width, width), width)],
            held[c].at[col * tiles + t], c_send.at[c, off - 1, t], c_recv.at[c, off - 1, t],
            "col", lax.rem(col + off, col_devices),
        )

    def send_x(u, off, peer):
        c, first, size = units[u]
        start = pl.multiple_of(peer * strip + first, 16)
        return remote(
            sent[c].at[pl.ds(start, size), :], xr.at[c, row, pl.ds(first, size), :],
            x_send.at[u, off - 1], x_recv.at[u, off - 1], "row", peer,
        )

    def own_x(u):
        c, first, size = units[u]
        start = pl.multiple_of(row * strip + first, 16)
        return pltpu.make_async_copy(
            sent[c].at[pl.ds(start, size), :], xr.at[c, row, pl.ds(first, size), :], x_own.at[u]
        )

    def send_own(s, off, peer):
        return remote(
            own_out.at[s, peer], own_ref.at[row, pl.ds(s * part, part), :],
            o_send.at[s, off - 1], o_recv.at[s, off - 1], "row", peer,
        )

    def stay_own(s):
        return pltpu.make_async_copy(
            own_out.at[s, row], own_ref.at[row, pl.ds(s * part, part), :], o_own.at[s]
        )

    def send_mirror(s, off):
        peer = lax.rem(col + off, col_devices)
        return remote(
            mirror_out.at[s, peer], mirror_ref.at[col, pl.ds(s * part, part), :],
            m_send.at[s, off - 1], m_recv.at[s, off - 1], "col", peer,
        )

    def stay_mirror(s):
        return pltpu.make_async_copy(
            mirror_out.at[s, col], mirror_ref.at[col, pl.ds(s * part, part), :], m_own.at[s]
        )

    def send_list(off):
        return remote(
            list_own, list_all.at[row], l_send.at[off - 1], l_recv.at[off - 1], "row",
            lax.rem(row + off, row_devices),
        )

    def reach(i):
        odd = lax.rem(i, 2)
        return chips // 2 + (1 - odd) * (i // 2) - odd * ((i + 1) // 2)

    def pair(i):
        return lax.rem(chip + reach(i), chips)

    def send_pair(send, i):
        for e in range(2):
            send(2 * reach(i) + e - core, 2 * pair(i) + e).start()

    def block(at_z, at_y, at_core):
        return (at_z * 2 + at_y) * 2 + at_core

    def neighbours(act):
        act("col", 1 - col)
        act("row", block(z, y, 1 - core))
        act("row", block(z, 1 - y, core))

        @pl.when(z >= 1)
        def _():
            act("row", block(z - 1, y, core))

        @pl.when(z + 1 < lines)
        def _():
            act("row", block(z + 1, y, core))

    inner = lax.min(z, 1) + lax.min(lines - 1 - z, 1)

    def signal_near(sem):
        def act(axis, peer):
            pl.semaphore_signal(
                sem, inc=1, device_id={axis: peer}, device_id_type=pl.DeviceIdType.MESH
            )

        neighbours(act)

    def meet(sem):
        signal_near(sem)
        pl.semaphore_wait(sem, 3 + inner)

    def send_later(u, steps):
        for o in steps:
            for e in range(2):
                send_x(u, 2 * o + e - core, 2 * lax.rem(chip + o, chips) + e).start()
        if steps == straight:
            send_x(u, partner_off, partner).start()
            own_x(u).start()

    partner, partner_off = row + 1 - 2 * core, 1 + core * (row_devices - 2)

    def cut(ref, at, first, size):
        return ref.at[pl.ds(at * stored + first, size)]

    def hand(at, first, size, send_sem, recv_sem, peer, axis="row", source=None):
        held_part = cut(a_all, at, first, size)
        if source is not None:
            held_part = source.at[pl.ds(first, size)]
        return remote(held_part, cut(a_all, at, first, size), send_sem, recv_sem, axis, peer)

    def main(same):
        part_share = share[0] if same else share[1]
        return col * part_share, stored - part_share

    def gives(same):
        part_share = share[0] if same else share[1]
        return col * (stored - part_share), part_share

    def gets(same):
        part_share = share[0] if same else share[1]
        return (1 - col) * (stored - part_share), part_share

    def place(at_z, same):
        at_y = y if same else 1 - y
        return block(at_z, at_y, core), at_z * 2 + at_y

    other_core = block(z, y, 1 - core)

    def up(step, source=None):
        at = block(z - step, y, core)
        return hand(at, *main(True), up_send.at[step], up_recv.at[step], block(z + 1, y, core), source=source)

    def down(step, source=None):
        at = block(z + step, y, core)
        return hand(at, *main(True), down_send.at[step], down_recv.at[step], block(z - 1, y, core), source=source)

    def over_y(at_z, source=None):
        at = block(at_z, y, core)
        return hand(at, *main(False), y_send.at[at_z], y_recv.at[at_z], block(z, 1 - y, core), source=source)

    def over_core(at_z, same, source=None):
        at, sem = place(at_z, same)
        return hand(at, *main(same), core_send.at[sem], core_recv.at[sem], other_core, source=source)

    def side_x(at_z, same):
        at, sem = place(at_z, same)
        return hand(at, *gives(same), x_side.at[sem], x_side_recv.at[sem], 1 - col, "col")

    def side_core(at_z, same, source=None):
        at, sem = place(at_z, same)
        return hand(at, *gets(same), core_side.at[sem], core_side_recv.at[sem], other_core, source=source)

    def arrived(at, span, recv_sem, send_sem):
        hand(at, *span, send_sem, recv_sem, other_core).wait_recv()

    def spread(at_z, same):
        over_core(at_z, same).start()
        if gives(same)[1]:
            side_x(at_z, same).start()

    def relay(step):
        @pl.when(z - 1 - step >= 0)
        def _():
            arrived(block(z - 1 - step, y, core), main(True), up_recv.at[step], up_send.at[step])
            if step + 1 < lines - 1:

                @pl.when(z + 1 < lines)
                def _():
                    up(step + 1).start()

            over_y(z - 1 - step).start()
            spread(z - 1 - step, True)

        @pl.when(z + 1 + step < lines)
        def _():
            arrived(block(z + 1 + step, y, core), main(True), down_recv.at[step], down_send.at[step])
            if step + 1 < lines - 1:

                @pl.when(z >= 1)
                def _():
                    down(step + 1).start()

            over_y(z + 1 + step).start()
            spread(z + 1 + step, True)

    def cross(step):
        at_z = lax.rem(z + step, lines)
        arrived(block(at_z, 1 - y, core), main(False), y_recv.at[at_z], y_send.at[at_z])
        spread(at_z, False)

    def others(body):
        for same, first in ((True, 1), (False, 0)):
            if gives(same)[1]:
                for step in range(first, lines):
                    body(lax.rem(z + step, lines), same)

    def side_arrived(at_z, same):
        side_x(at_z, same).wait_recv()
        side_core(at_z, same).start()

    def multiply(c, group):
        for q in range(per):
            j = group * per + q
            picked = [held[c][rows_ref[s, 0, j]] for s in range(listed_b)]
            product = lax.dot_general(
                b_own[j], jnp.concatenate(picked, axis=1), (((0,), (1,)), ((), ())),
                preferred_element_type=jnp.float32,
            )
            sent[c][pl.ds(pl.multiple_of(j * width, width), width), :] = product.astype(jnp.bfloat16)

    def make_table():
        total = list_all[0]
        for r in range(1, row_devices):
            total = total + list_all[r]
        square = (width, width)
        by_lane = jnp.broadcast_to(total[0:1], square)
        lane = lax.broadcasted_iota(jnp.int32, square, 1)
        sub = lax.broadcasted_iota(jnp.int32, square, 0)
        keys = by_lane * width + lane

        def count(mask):
            return jnp.sum(jnp.where(mask, 1, 0), axis=0, keepdims=True)

        rank = jnp.broadcast_to(count(keys.T < keys), square)
        hit = rank.T == lane
        by_sub = by_lane.T
        order = jnp.sum(jnp.where(hit, sub, 0), axis=0, keepdims=True)
        target = jnp.sum(jnp.where(hit, by_sub, 0), axis=0, keepdims=True)
        began = count(by_sub < target)
        source, slot = order // slots, order % slots
        table[0:1, :] = source * stored + slot
        table[1:2, :] = source * stored + slots + slot % listed
        table[2:3, :] = order // listed
        table[3:4, :] = jnp.where(lane[0:1] > began, 1, 0)
        table[4:5, :] = count(by_sub <= lane) - 1
        table[5:8, :] = jnp.zeros((3, width), jnp.int32)

    def prepare(s):
        lane = lax.broadcasted_iota(jnp.int32, (part, width), 1)
        low = lane < width // 2

        @pl.loop(0, row_devices)
        def _(r):
            cut = pl.ds(s * part, part)
            middle = xr[1, r, cut, :]
            blank = jnp.zeros_like(middle)
            xt[s][r * groups, :, 0:width] = xr[0, r, cut, :]
            xt[s][r * groups, :, width : 2 * width] = jnp.where(low, middle, blank)
            xt[s][r * groups + 1, :, 0:width] = xr[2, r, cut, :]
            xt[s][r * groups + 1, :, width : 2 * width] = jnp.where(low, blank, middle)

    def contract(s):
        def step(p, run):
            weights = jnp.concatenate([a_all[picks[0, p]], a_all[picks[1, p]]], axis=1)
            product = lax.dot_general(
                xt[s][picks[2, p]], weights, CONTRACT_LAST, preferred_element_type=jnp.float32
            )
            run = product + run * picks[3, p].astype(jnp.float32)
            stack[p] = run.astype(stack.dtype)
            return run

        lax.fori_loop(0, width, step, jnp.zeros((part, tile), jnp.float32), unroll=16)

    def assemble(s, k):
        found = [[stack[picks[4, g * row_devices + 2 * k + e]] for e in range(2)] for g in range(groups)]
        for e in range(2):
            own_out[s, 2 * k + e] = jnp.concatenate([found[g][e] for g in range(groups)], axis=1)
        for g in range(groups):
            start = pl.multiple_of(k * 2 * tile, width)
            mirror_out[s, g, :, pl.ds(start, 2 * tile)] = jnp.concatenate(found[g], axis=1)

    load_b = pltpu.make_async_copy(b_ref, b_own, load_sem.at[0])
    load_a = pltpu.make_async_copy(alpha_ref, flat, load_sem.at[1])
    load_a.start()
    barrier = pltpu.get_barrier_semaphore()
    signal_near(barrier)
    lane = lax.broadcasted_iota(jnp.int32, list_own.shape, 1)
    mine = jnp.zeros(list_own.shape, jnp.int32)
    for g in range(groups):
        for s in range(listed):
            mine = jnp.where(lane == row * slots + g * listed + s, lists_ref[0, g, 0, s], mine)
    list_own[...] = mine
    load_a.wait()
    for s in range(listed):
        first, second = flat[s], flat[listed + s]
        a_own[s] = first[:, :width]
        a_own[listed + s] = second[:, tile - width :]
        a_own[slots + s] = jnp.concatenate([first[:, width:], second[:, : tile - width]], axis=1)
    keep_list = pltpu.make_async_copy(list_own, list_all.at[row], l_own)
    keep_a = pltpu.make_async_copy(a_own, cut(a_all, row, 0, stored), a_sem)
    pl.semaphore_wait(barrier, 3 + inner)

    @pl.when(z + 1 < lines)
    def _():
        up(0, a_own).start()

    @pl.when(z >= 1)
    def _():
        down(0, a_own).start()

    over_y(z, a_own).start()
    over_core(z, True, a_own).start()
    if share[0]:
        side_core(z, True, a_own).start()
    for c in range(chunks):
        for off in range(1, col_devices):

            @pl.loop(0, tiles)
            def _(t):
                send_c(c, off, t).start()

        if c == 0:
            keep_list.start()
            keep_a.start()
            load_b.start()

        @pl.loop(0, tiles)
        def _(t):
            own_c(c, t).start()

    for n in range(lines):
        meet(rounds.at[n])

    @pl.loop(1, row_devices)
    def _(off):
        send_list(off).start()

    load_b.wait()
    move_table = pltpu.make_async_copy(table, picks, t_sem)
    now, later = [[0], [1], [2]], [[(3, straight)], [(3, turned), (4, straight)], [(5, straight), (4, turned), (5, turned)]]
    relayed = 0
    for c in range(chunks):
        if relayed < lines - 1:
            relay(relayed)
            relayed += 1

        @pl.loop(0, tiles)
        def _(t):
            own_c(c, t).wait()
            for off in range(1, col_devices):
                send_c(c, off, t).wait_recv()

        @pl.loop(0, chips)
        def _(i):
            multiply(c, pair(i))

            @pl.when(i > 0)
            def _():
                for u in now[c]:
                    send_pair(functools.partial(send_x, u), i - 1)

        for u in now[c]:
            send_x(u, partner_off, partner).start()
            own_x(u).start()
        for u, steps in later[c]:
            send_later(u, steps)
        if c == 0:
            keep_list.wait()

            @pl.loop(1, row_devices)
            def _(off):
                send_list(off).wait_recv()

            make_table()
            move_table.start()
            cross(0)

    for step in range(relayed, lines - 1):
        relay(step)
    for step in range(1, lines):
        cross(step)
    others(side_arrived)
    keep_a.wait()
    move_table.wait()
    for at_z in range(lines):
        for same in (True, False):
            at, sem = block(at_z, y if same else 1 - y, 1 - core), place(at_z, same)[1]
            arrived(at, main(same), core_recv.at[sem], core_send.at[sem])
            if gets(same)[1]:
                arrived(at, gets(same), core_side_recv.at[sem], core_side.at[sem])
    for s in range(subs):
        for u in range(s * chunks, (s + 1) * chunks):
            own_x(u).wait()

            @pl.loop(1, row_devices)
            def _(off):
                send_x(u, off, lax.rem(row + off, row_devices)).wait_recv()

        prepare(s)
        contract(s)

        @pl.loop(0, chips)
        def _(i):
            assemble(s, pair(i))

            @pl.when(i > 0)
            def _():
                send_pair(functools.partial(send_own, s), i - 1)

        send_own(s, partner_off, partner).start()
        for off in range(1, col_devices):
            send_mirror(s, off).start()
        stay_own(s).start()
        stay_mirror(s).start()

    for step in range(lines - 1):

        @pl.when((z - step >= 0) & (z + 1 < lines))
        def _():
            up(step).wait_send()

        @pl.when((z + step < lines) & (z >= 1))
        def _():
            down(step).wait_send()

    for at_z in range(lines):
        over_y(at_z).wait_send()
        for same in (True, False):
            over_core(at_z, same).wait_send()
            if gets(same)[1]:
                side_core(at_z, same).wait_send()

    others(lambda at_z, same: side_x(at_z, same).wait_send())
    for c in range(chunks):
        for off in range(1, col_devices):

            @pl.loop(0, tiles)
            def _(t):
                send_c(c, off, t).wait_send()

    @pl.loop(1, row_devices)
    def _(off):
        peer = lax.rem(row + off, row_devices)
        send_list(off).wait_send()
        for u in range(len(units)):
            send_x(u, off, peer).wait_send()
        for s in range(subs):
            send_own(s, off, peer).wait()

    for s in range(subs):
        stay_own(s).wait()
        stay_mirror(s).wait()
        for off in range(1, col_devices):
            send_mirror(s, off).wait()


def fused(c_matrix, beta_values, beta_rows, alpha_tiles, alpha_rows, row_devices, col_devices, subs, share):
    rows, columns = c_matrix.shape
    _, tiles, listed, width, _ = beta_values.shape
    slots, tile, _ = alpha_tiles.shape
    groups = alpha_rows.shape[1]
    chunks, strip = rows // width, columns // row_devices
    part, units, lines = strip // subs, rows // width * subs, row_devices // 4
    stored = slots * tile // width
    row_peers, col_peers = row_devices - 1, col_devices - 1
    dma, half = pltpu.SemaphoreType.DMA, jnp.bfloat16
    anywhere = pl.BlockSpec(memory_space=pl.ANY)
    scalars = pl.BlockSpec(memory_space=pltpu.SMEM)
    return pl.pallas_call(
        functools.partial(fused_kernel, chunks, subs, share),
        in_specs=[scalars, scalars, anywhere, anywhere, anywhere],
        out_specs=[anywhere, anywhere],
        out_shape=[
            jax.ShapeDtypeStruct((row_devices, strip, groups * tile), half),
            jax.ShapeDtypeStruct((col_devices, strip, row_devices * tile), half),
        ],
        scratch_shapes=[pltpu.VMEM((col_devices * tiles, width, width), half)] * chunks
        + [pltpu.VMEM((columns, width), half)] * chunks
        + [pltpu.VMEM((row_devices * groups, part, 2 * width), half)] * subs
        + [
            pltpu.VMEM((tiles, listed * width, width), half),
            pltpu.VMEM((slots, tile, tile), half),
            pltpu.VMEM((stored, tile, width), half),
            pltpu.VMEM((row_devices * stored, tile, width), half),
            pltpu.VMEM((chunks, row_devices, strip, width), half),
            pltpu.VMEM((row_devices * slots, part, tile), half),
            pltpu.VMEM((subs, row_devices, part, groups * tile), half),
            pltpu.VMEM((subs, groups, part, row_devices * tile), half),
            pltpu.VMEM((8, width), jnp.int32),
            pltpu.VMEM((row_devices, 8, width), jnp.int32),
            pltpu.VMEM((8, width), jnp.int32),
            pltpu.SMEM((8, width), jnp.int32),
            dma((2,)),
            dma((chunks, tiles)), dma((chunks, col_peers, tiles)), dma((chunks, col_peers, tiles)),
            dma((units,)), dma((units, row_peers)), dma((units, row_peers)),
            dma, dma((row_peers,)), dma((row_peers,)), dma,
        ]
        + [dma((lines - 1,))] * 4
        + [dma((lines,))] * 2
        + [dma((2 * lines,))] * 6
        + [
            dma,
            dma((subs,)), dma((subs, row_peers)), dma((subs, row_peers)),
            dma((subs,)), dma((subs, col_peers)), dma((subs, col_peers)),
            pltpu.SemaphoreType.REGULAR((lines,)),
        ],
        compiler_params=pltpu.CompilerParams(
            collective_id=0, has_side_effects=True, vmem_limit_bytes=48 << 20
        ),
        cost_estimate=pl.CostEstimate(flops=1 << 37, bytes_accessed=1 << 28, transcendentals=0),
        name="fused",
    )(
        jnp.transpose(beta_rows, (2, 0, 1)), alpha_rows, c_matrix,
        beta_values.reshape(tiles, listed * width, width), alpha_tiles,
    )


def per_device(c_matrix, beta_values, beta_rows, alpha_values, alpha_rows, gaps):
    row_devices, col_devices = lax.axis_size("row"), lax.axis_size("col")
    groups, stretch, columns = c_matrix.shape
    pairs, _, _, listed, tile, _ = alpha_values.shape
    rows, width = groups * stretch, beta_values.shape[-1]
    c_rows = c_matrix.reshape(rows, columns)
    alpha_tiles = alpha_values.reshape(pairs * groups, listed, tile, tile)
    strip, subs = columns // row_devices, 2
    own_kernels = pairs == 1 and groups == 2 and stretch == tile and 2 * tile == 3 * width
    own_kernels = own_kernels and row_devices % 4 == 0 and row_devices * groups * listed == width
    own_kernels = own_kernels and strip % (16 * subs) == 0 and 2 * strip % width == 0
    if own_kernels:
        own, mirror = fused(
            c_rows, beta_values, beta_rows, alpha_tiles.reshape(-1, tile, tile), alpha_rows,
            row_devices, col_devices, subs, SHARE,
        )
    else:
        rows_all = lax.all_gather(alpha_rows.reshape(pairs * groups, listed), "row")
        alpha_all = lax.all_gather(alpha_tiles, "row")
        xt = beta_products(lax.all_gather(c_rows, "col"), beta_values, beta_rows)
        xt = jnp.moveaxis(xt.reshape(pairs, row_devices, stretch, rows), 1, 0)
        x_strip = lax.all_to_all(xt, "row", 0, 0)[None]
        own, mirror = alpha_products(alpha_all, rows_all, x_strip, groups)
        own = lax.all_to_all(own, "row", 0, 0)
        mirror = lax.all_to_all(mirror, "col", 0, 0)
    out = final(
        own.reshape(columns, groups * stretch),
        mirror.reshape(groups * stretch, columns),
        gaps.reshape(groups * stretch, columns),
    )
    return out.reshape(gaps.shape)


def solution(mesh):
    placed = (
        P(None, "row", "col"),
        P(None, "col", None, None, None),
        P(None, "col", None),
        P(None, None, "row", None, None, None),
        P(None, None, "row", None),
        P(None, "row", "col"),
    )
    return jax.shard_map(
        per_device, mesh=mesh, in_specs=placed, out_specs=P(None, "row", "col"), check_vma=False
    )
```

```python
import functools

import jax
import jax.numpy as jnp
from jax import lax
from jax.experimental import pallas as pl
from jax.experimental.pallas import tpu as pltpu
from jax.sharding import PartitionSpec as P

CONTRACT_LAST = (((1,), (1,)), ((), ()))
SHARE = (2, 2)


def beta_kernel(listed, held, rows_ref, c_ref, b_ref, xt_ref):
    k, j = pl.program_id(0), pl.program_id(1)
    width = b_ref.shape[-1]
    picked = []
    for z in range(listed):
        tile = rows_ref[k, j, z]
        owner = tile // held
        start = pl.multiple_of((tile - owner * held) * width, width)
        picked.append(c_ref[owner, :, pl.ds(start, width)])
    lhs = b_ref[0, 0].reshape(listed * width, width)
    product = lax.dot_general(
        lhs, jnp.concatenate(picked, axis=1), (((0,), (1,)), ((), ())),
        preferred_element_type=jnp.float32,
    )
    xt_ref[0] = product.astype(xt_ref.dtype)


def beta_products(gathered, beta_values, beta_rows):
    pairs, tiles, listed, width, _ = beta_values.shape
    owners, rows, columns = gathered.shape
    return pl.pallas_call(
        functools.partial(beta_kernel, listed, columns // width),
        grid_spec=pltpu.PrefetchScalarGridSpec(
            num_scalar_prefetch=1,
            grid=(pairs, tiles),
            in_specs=[
                pl.BlockSpec((owners, rows, columns), lambda k, j, s: (0, 0, 0)),
                pl.BlockSpec((1, 1, listed, width, width), lambda k, j, s: (k, j, 0, 0, 0)),
            ],
            out_specs=pl.BlockSpec((1, width, rows), lambda k, j, s: (k, j, 0)),
        ),
        out_shape=jax.ShapeDtypeStruct((pairs, tiles * width, rows), jnp.bfloat16),
        compiler_params=pltpu.CompilerParams(vmem_limit_bytes=56 << 20),
        name="beta_products",
    )(beta_rows, gathered, beta_values)


def alpha_kernel(groups, rows_ref, a_ref, x_ref, own_ref, mirror_ref, acc_ref):
    r = pl.program_id(0)
    row_devices = pl.num_programs(0)
    pairs = x_ref.shape[2]
    listed, tile = rows_ref.shape[2], acc_ref.shape[1]

    @pl.when(r == 0)
    def _():
        acc_ref[...] = jnp.zeros_like(acc_ref)

    for i in range(x_ref.shape[1]):
        at = r * x_ref.shape[1] + i
        for k in range(pairs):
            parts = [x_ref[c, i, k] for c in range(x_ref.shape[0])]
            merged = jnp.concatenate(parts, axis=1) if len(parts) > 1 else parts[0]
            for g in range(groups):
                x = merged[:, g * tile : (g + 1) * tile]
                slot = k * groups + g

                @pl.loop(0, listed)
                def _(z):
                    acc_ref[rows_ref[at, slot, z]] += lax.dot_general(
                        a_ref[i, slot, z], x, CONTRACT_LAST, preferred_element_type=jnp.float32
                    )

    @pl.when(r == row_devices - 1)
    def _():
        count = acc_ref.shape[0] // groups
        for g in range(groups):
            for to in range(count):
                turned = acc_ref[g * count + to].astype(own_ref.dtype).T
                own_ref[to, :, g * tile : (g + 1) * tile] = turned
                mirror_ref[g, :, to * tile : (to + 1) * tile] = turned


def alpha_products(alpha_all, rows_all, x_strip, groups):
    row_devices, rest = alpha_all.shape[0], alpha_all.shape[1:]
    tile = x_strip.shape[0] * x_strip.shape[-1] // groups
    per = 1
    chunks, _, pairs, strip, chunk = x_strip.shape
    return pl.pallas_call(
        functools.partial(alpha_kernel, groups),
        grid_spec=pltpu.PrefetchScalarGridSpec(
            num_scalar_prefetch=1,
            grid=(row_devices // per,),
            in_specs=[
                pl.BlockSpec((per,) + rest, lambda r, s: (r,) + (0,) * len(rest)),
                pl.BlockSpec((chunks, per, pairs, strip, chunk), lambda r, s: (0, r, 0, 0, 0)),
            ],
            out_specs=[
                pl.BlockSpec((row_devices, strip, groups * tile), lambda r, s: (0, 0, 0)),
                pl.BlockSpec((groups, strip, row_devices * tile), lambda r, s: (0, 0, 0)),
            ],
            scratch_shapes=[pltpu.VMEM((groups * row_devices, tile, strip), jnp.float32)],
        ),
        out_shape=[
            jax.ShapeDtypeStruct((row_devices, strip, groups * tile), jnp.bfloat16),
            jax.ShapeDtypeStruct((groups, strip, row_devices * tile), jnp.bfloat16),
        ],
        compiler_params=pltpu.CompilerParams(vmem_limit_bytes=56 << 20),
        name="alpha_products",
    )(rows_all, alpha_all, x_strip)


def final_kernel(block, own, mirror, gaps, out_ref, out, out_sem):
    steps = out.shape[1] // block

    def store(i):
        span = pl.ds(i * block, block)
        return pltpu.make_async_copy(out.at[:, span], out_ref.at[:, span], out_sem.at[i])

    for i in range(steps):
        span = slice(i * block, (i + 1) * block)
        turned = own[span, :].T.astype(jnp.float32)
        out[:, span] = (turned + mirror[:, span].astype(jnp.float32)) / gaps[:, span]
        store(i).start()
    for i in range(steps):
        store(i).wait()


def final(own, mirror, gaps):
    rows, columns = gaps.shape
    block = next(n for n in (384, 256, 128) if columns % n == 0)
    whole = pl.BlockSpec(memory_space=pltpu.VMEM)
    return pl.pallas_call(
        functools.partial(final_kernel, block),
        in_specs=[whole] * 3,
        out_specs=pl.BlockSpec(memory_space=pl.ANY),
        out_shape=jax.ShapeDtypeStruct((rows, columns), jnp.float32),
        scratch_shapes=[
            pltpu.VMEM(gaps.shape, gaps.dtype), pltpu.SemaphoreType.DMA((columns // block,)),
        ],
        compiler_params=pltpu.CompilerParams(vmem_limit_bytes=20 << 20),
        name="final",
    )(own, mirror, gaps)


def remote(src, dst, send_sem, recv_sem, axis, peer):
    return pltpu.make_async_remote_copy(
        src_ref=src, dst_ref=dst, send_sem=send_sem, recv_sem=recv_sem,
        device_id={axis: peer}, device_id_type=pl.DeviceIdType.MESH,
    )


def fused_kernel(chunks, subs, share, rows_ref, lists_ref, c_ref, b_ref, alpha_ref, own_ref, mirror_ref, *scratch):
    held, sent, xt = scratch[:chunks], scratch[chunks : 2 * chunks], scratch[2 * chunks : 2 * chunks + subs]
    (b_own, flat, a_own, a_all, xr, stack, own_out, mirror_out, list_own, list_all, table, picks,
     load_sem, c_own, c_send, c_recv, x_own, x_send, x_recv, l_own, l_send, l_recv, a_sem,
     up_send, up_recv, down_send, down_recv, y_send, y_recv, core_send, core_recv,
     x_side, x_side_recv, core_side, core_side_recv, t_sem,
     o_own, o_send, o_recv, m_own, m_send, m_recv, rounds) = scratch[2 * chunks + subs :]
    row_devices, row = lax.axis_size("row"), lax.axis_index("row")
    col_devices, col = lax.axis_size("col"), lax.axis_index("col")
    rows, columns = c_ref.shape
    tiles, depth, width = b_own.shape
    listed_b = depth // width
    slots, tile, _ = flat.shape
    groups = lists_ref.shape[1]
    listed = slots // groups
    chunk, strip = rows // chunks, columns // row_devices
    part = strip // subs
    chips = row_devices // 2
    per = tiles // chips
    stored = a_own.shape[0]
    lines = row_devices // 4
    chip, core = row // 2, lax.rem(row, 2)
    z, y = row // 4, lax.rem(chip, 2)
    units = [(c, s * part, part) for s in range(subs) for c in range(chunks)]
    straight, turned = range(2, chips, 2), range(1, chips, 2)

    def own_c(c, t):
        return pltpu.make_async_copy(
            c_ref.at[pl.ds(c * chunk, chunk), pl.ds(pl.multiple_of(t * width, width), width)],
            held[c].at[col * tiles + t], c_own.at[c, t],
        )

    def send_c(c, off, t):
        return remote(
            c_ref.at[pl.ds(c * chunk, chunk), pl.ds(pl.multiple_of(t * width, width), width)],
            held[c].at[col * tiles + t], c_send.at[c, off - 1, t], c_recv.at[c, off - 1, t],
            "col", lax.rem(col + off, col_devices),
        )

    def send_x(u, off, peer):
        c, first, size = units[u]
        start = pl.multiple_of(peer * strip + first, 16)
        return remote(
            sent[c].at[pl.ds(start, size), :], xr.at[c, row, pl.ds(first, size), :],
            x_send.at[u, off - 1], x_recv.at[u, off - 1], "row", peer,
        )

    def own_x(u):
        c, first, size = units[u]
        start = pl.multiple_of(row * strip + first, 16)
        return pltpu.make_async_copy(
            sent[c].at[pl.ds(start, size), :], xr.at[c, row, pl.ds(first, size), :], x_own.at[u]
        )

    def send_own(s, off, peer):
        return remote(
            own_out.at[s, peer], own_ref.at[row, pl.ds(s * part, part), :],
            o_send.at[s, off - 1], o_recv.at[s, off - 1], "row", peer,
        )

    def stay_own(s):
        return pltpu.make_async_copy(
            own_out.at[s, row], own_ref.at[row, pl.ds(s * part, part), :], o_own.at[s]
        )

    def send_mirror(s, off):
        peer = lax.rem(col + off, col_devices)
        return remote(
            mirror_out.at[s, peer], mirror_ref.at[col, pl.ds(s * part, part), :],
            m_send.at[s, off - 1], m_recv.at[s, off - 1], "col", peer,
        )

    def stay_mirror(s):
        return pltpu.make_async_copy(
            mirror_out.at[s, col], mirror_ref.at[col, pl.ds(s * part, part), :], m_own.at[s]
        )

    def send_list(off):
        return remote(
            list_own, list_all.at[row], l_send.at[off - 1], l_recv.at[off - 1], "row",
            lax.rem(row + off, row_devices),
        )

    def reach(i):
        odd = lax.rem(i, 2)
        return lax.rem(i + 1, chips)

    def pair(i):
        return lax.rem(chip + reach(i), chips)

    def send_pair(send, i):
        for e in range(2):
            send(2 * reach(i) + e - core, 2 * pair(i) + e).start()

    def block(at_z, at_y, at_core):
        return (at_z * 2 + at_y) * 2 + at_core

    def neighbours(act):
        act("col", 1 - col)
        act("row", block(z, y, 1 - core))
        act("row", block(z, 1 - y, core))

        @pl.when(z >= 1)
        def _():
            act("row", block(z - 1, y, core))

        @pl.when(z + 1 < lines)
        def _():
            act("row", block(z + 1, y, core))

    inner = lax.min(z, 1) + lax.min(lines - 1 - z, 1)

    def signal_near(sem):
        def act(axis, peer):
            pl.semaphore_signal(
                sem, inc=1, device_id={axis: peer}, device_id_type=pl.DeviceIdType.MESH
            )

        neighbours(act)

    def meet(sem):
        signal_near(sem)
        pl.semaphore_wait(sem, 3 + inner)

    def send_later(u, steps):
        for o in steps:
            for e in range(2):
                send_x(u, 2 * o + e - core, 2 * lax.rem(chip + o, chips) + e).start()
        if steps == straight:
            send_x(u, partner_off, partner).start()
            own_x(u).start()

    partner, partner_off = row + 1 - 2 * core, 1 + core * (row_devices - 2)

    def cut(ref, at, first, size):
        return ref.at[pl.ds(at * stored + first, size)]

    def hand(at, first, size, send_sem, recv_sem, peer, axis="row", source=None):
        held_part = cut(a_all, at, first, size)
        if source is not None:
            held_part = source.at[pl.ds(first, size)]
        return remote(held_part, cut(a_all, at, first, size), send_sem, recv_sem, axis, peer)

    def main(same):
        part_share = share[0] if same else share[1]
        return col * part_share, stored - part_share

    def gives(same):
        part_share = share[0] if same else share[1]
        return col * (stored - part_share), part_share

    def gets(same):
        part_share = share[0] if same else share[1]
        return (1 - col) * (stored - part_share), part_share

    def place(at_z, same):
        at_y = y if same else 1 - y
        return block(at_z, at_y, core), at_z * 2 + at_y

    other_core = block(z, y, 1 - core)

    def up(step, source=None):
        at = block(z - step, y, core)
        return hand(at, *main(True), up_send.at[step], up_recv.at[step], block(z + 1, y, core), source=source)

    def down(step, source=None):
        at = block(z + step, y, core)
        return hand(at, *main(True), down_send.at[step], down_recv.at[step], block(z - 1, y, core), source=source)

    def over_y(at_z, source=None):
        at = block(at_z, y, core)
        return hand(at, *main(False), y_send.at[at_z], y_recv.at[at_z], block(z, 1 - y, core), source=source)

    def over_core(at_z, same, source=None):
        at, sem = place(at_z, same)
        return hand(at, *main(same), core_send.at[sem], core_recv.at[sem], other_core, source=source)

    def side_x(at_z, same):
        at, sem = place(at_z, same)
        return hand(at, *gives(same), x_side.at[sem], x_side_recv.at[sem], 1 - col, "col")

    def side_core(at_z, same, source=None):
        at, sem = place(at_z, same)
        return hand(at, *gets(same), core_side.at[sem], core_side_recv.at[sem], other_core, source=source)

    def arrived(at, span, recv_sem, send_sem):
        hand(at, *span, send_sem, recv_sem, other_core).wait_recv()

    def spread(at_z, same):
        over_core(at_z, same).start()
        if gives(same)[1]:
            side_x(at_z, same).start()

    def relay(step):
        @pl.when(z - 1 - step >= 0)
        def _():
            arrived(block(z - 1 - step, y, core), main(True), up_recv.at[step], up_send.at[step])
            if step + 1 < lines - 1:

                @pl.when(z + 1 < lines)
                def _():
                    up(step + 1).start()

            over_y(z - 1 - step).start()
            spread(z - 1 - step, True)

        @pl.when(z + 1 + step < lines)
        def _():
            arrived(block(z + 1 + step, y, core), main(True), down_recv.at[step], down_send.at[step])
            if step + 1 < lines - 1:

                @pl.when(z >= 1)
                def _():
                    down(step + 1).start()

            over_y(z + 1 + step).start()
            spread(z + 1 + step, True)

    def cross(step):
        at_z = lax.rem(z + step, lines)
        arrived(block(at_z, 1 - y, core), main(False), y_recv.at[at_z], y_send.at[at_z])
        spread(at_z, False)

    def others(body):
        for same, first in ((True, 1), (False, 0)):
            if gives(same)[1]:
                for step in range(first, lines):
                    body(lax.rem(z + step, lines), same)

    def side_arrived(at_z, same):
        side_x(at_z, same).wait_recv()
        side_core(at_z, same).start()

    def multiply(c, group):
        for q in range(per):
            j = group * per + q
            picked = [held[c][rows_ref[s, 0, j]] for s in range(listed_b)]
            product = lax.dot_general(
                b_own[j], jnp.concatenate(picked, axis=1), (((0,), (1,)), ((), ())),
                preferred_element_type=jnp.float32,
            )
            sent[c][pl.ds(pl.multiple_of(j * width, width), width), :] = product.astype(jnp.bfloat16)

    def make_table():
        total = list_all[0]
        for r in range(1, row_devices):
            total = total + list_all[r]
        square = (width, width)
        by_lane = jnp.broadcast_to(total[0:1], square)
        lane = lax.broadcasted_iota(jnp.int32, square, 1)
        sub = lax.broadcasted_iota(jnp.int32, square, 0)
        keys = by_lane * width + lane

        def count(mask):
            return jnp.sum(jnp.where(mask, 1, 0), axis=0, keepdims=True)

        rank = jnp.broadcast_to(count(keys.T < keys), square)
        hit = rank.T == lane
        by_sub = by_lane.T
        order = jnp.sum(jnp.where(hit, sub, 0), axis=0, keepdims=True)
        target = jnp.sum(jnp.where(hit, by_sub, 0), axis=0, keepdims=True)
        began = count(by_sub < target)
        source, slot = order // slots, order % slots
        table[0:1, :] = source * stored + slot
        table[1:2, :] = source * stored + slots + slot % listed
        table[2:3, :] = order // listed
        table[3:4, :] = jnp.where(lane[0:1] > began, 1, 0)
        table[4:5, :] = count(by_sub <= lane) - 1
        table[5:8, :] = jnp.zeros((3, width), jnp.int32)

    def prepare(s):
        lane = lax.broadcasted_iota(jnp.int32, (part, width), 1)
        low = lane < width // 2

        @pl.loop(0, row_devices)
        def _(r):
            cut = pl.ds(s * part, part)
            middle = xr[1, r, cut, :]
            blank = jnp.zeros_like(middle)
            xt[s][r * groups, :, 0:width] = xr[0, r, cut, :]
            xt[s][r * groups, :, width : 2 * width] = jnp.where(low, middle, blank)
            xt[s][r * groups + 1, :, 0:width] = xr[2, r, cut, :]
            xt[s][r * groups + 1, :, width : 2 * width] = jnp.where(low, blank, middle)

    def contract(s):
        def step(p, run):
            weights = jnp.concatenate([a_all[picks[0, p]], a_all[picks[1, p]]], axis=1)
            product = lax.dot_general(
                xt[s][picks[2, p]], weights, CONTRACT_LAST, preferred_element_type=jnp.float32
            )
            run = product + run * picks[3, p].astype(jnp.float32)
            stack[p] = run.astype(stack.dtype)
            return run

        lax.fori_loop(0, width, step, jnp.zeros((part, tile), jnp.float32), unroll=16)

    def assemble(s, k):
        found = [[stack[picks[4, g * row_devices + 2 * k + e]] for e in range(2)] for g in range(groups)]
        for e in range(2):
            own_out[s, 2 * k + e] = jnp.concatenate([found[g][e] for g in range(groups)], axis=1)
        for g in range(groups):
            start = pl.multiple_of(k * 2 * tile, width)
            mirror_out[s, g, :, pl.ds(start, 2 * tile)] = jnp.concatenate(found[g], axis=1)

    load_b = pltpu.make_async_copy(b_ref, b_own, load_sem.at[0])
    load_a = pltpu.make_async_copy(alpha_ref, flat, load_sem.at[1])
    load_a.start()
    barrier = pltpu.get_barrier_semaphore()
    signal_near(barrier)
    lane = lax.broadcasted_iota(jnp.int32, list_own.shape, 1)
    mine = jnp.zeros(list_own.shape, jnp.int32)
    for g in range(groups):
        for s in range(listed):
            mine = jnp.where(lane == row * slots + g * listed + s, lists_ref[0, g, 0, s], mine)
    list_own[...] = mine
    load_a.wait()
    for s in range(listed):
        first, second = flat[s], flat[listed + s]
        a_own[s] = first[:, :width]
        a_own[listed + s] = second[:, tile - width :]
        a_own[slots + s] = jnp.concatenate([first[:, width:], second[:, : tile - width]], axis=1)
    keep_list = pltpu.make_async_copy(list_own, list_all.at[row], l_own)
    keep_a = pltpu.make_async_copy(a_own, cut(a_all, row, 0, stored), a_sem)
    pl.semaphore_wait(barrier, 3 + inner)

    @pl.when(z + 1 < lines)
    def _():
        up(0, a_own).start()

    @pl.when(z >= 1)
    def _():
        down(0, a_own).start()

    over_y(z, a_own).start()
    over_core(z, True, a_own).start()
    if share[0]:
        side_core(z, True, a_own).start()
    for c in range(chunks):
        for off in range(1, col_devices):

            @pl.loop(0, tiles)
            def _(t):
                send_c(c, off, t).start()

        if c == 0:
            keep_list.start()
            keep_a.start()
            load_b.start()

        @pl.loop(0, tiles)
        def _(t):
            own_c(c, t).start()

    for n in range(lines):
        meet(rounds.at[n])

    @pl.loop(1, row_devices)
    def _(off):
        send_list(off).start()

    load_b.wait()
    move_table = pltpu.make_async_copy(table, picks, t_sem)
    now, later = [[0], [1], [2]], [[(3, straight), (3, turned)], [(4, straight)], [(5, straight), (4, turned), (5, turned)]]
    relayed = 0
    for c in range(chunks):
        if relayed < lines - 1:
            relay(relayed)
            relayed += 1

        @pl.loop(0, tiles)
        def _(t):
            own_c(c, t).wait()
            for off in range(1, col_devices):
                send_c(c, off, t).wait_recv()

        @pl.loop(0, chips)
        def _(i):
            multiply(c, pair(i))

            @pl.when(i > 0)
            def _():
                for u in now[c]:
                    send_pair(functools.partial(send_x, u), i - 1)

        for u in now[c]:
            send_x(u, partner_off, partner).start()
            own_x(u).start()
        for u, steps in later[c]:
            send_later(u, steps)
        if c == 0:
            keep_list.wait()

            @pl.loop(1, row_devices)
            def _(off):
                send_list(off).wait_recv()

            make_table()
            move_table.start()
            cross(0)

    for step in range(relayed, lines - 1):
        relay(step)
    for step in range(1, lines):
        cross(step)
    others(side_arrived)
    keep_a.wait()
    move_table.wait()
    for at_z in range(lines):
        for same in (True, False):
            at, sem = block(at_z, y if same else 1 - y, 1 - core), place(at_z, same)[1]
            arrived(at, main(same), core_recv.at[sem], core_send.at[sem])
            if gets(same)[1]:
                arrived(at, gets(same), core_side_recv.at[sem], core_side.at[sem])
    for s in range(subs):
        for u in range(s * chunks, (s + 1) * chunks):
            own_x(u).wait()

            @pl.loop(1, row_devices)
            def _(off):
                send_x(u, off, lax.rem(row + off, row_devices)).wait_recv()

        prepare(s)
        contract(s)

        @pl.loop(0, chips)
        def _(i):
            assemble(s, pair(i))

            @pl.when(i > 0)
            def _():
                send_pair(functools.partial(send_own, s), i - 1)

        send_own(s, partner_off, partner).start()
        for off in range(1, col_devices):
            send_mirror(s, off).start()
        stay_own(s).start()
        stay_mirror(s).start()

    for step in range(lines - 1):

        @pl.when((z - step >= 0) & (z + 1 < lines))
        def _():
            up(step).wait_send()

        @pl.when((z + step < lines) & (z >= 1))
        def _():
            down(step).wait_send()

    for at_z in range(lines):
        over_y(at_z).wait_send()
        for same in (True, False):
            over_core(at_z, same).wait_send()
            if gets(same)[1]:
                side_core(at_z, same).wait_send()

    others(lambda at_z, same: side_x(at_z, same).wait_send())
    for c in range(chunks):
        for off in range(1, col_devices):

            @pl.loop(0, tiles)
            def _(t):
                send_c(c, off, t).wait_send()

    @pl.loop(1, row_devices)
    def _(off):
        peer = lax.rem(row + off, row_devices)
        send_list(off).wait_send()
        for u in range(len(units)):
            send_x(u, off, peer).wait_send()
        for s in range(subs):
            send_own(s, off, peer).wait()

    for s in range(subs):
        stay_own(s).wait()
        stay_mirror(s).wait()
        for off in range(1, col_devices):
            send_mirror(s, off).wait()


def fused(c_matrix, beta_values, beta_rows, alpha_tiles, alpha_rows, row_devices, col_devices, subs, share):
    rows, columns = c_matrix.shape
    _, tiles, listed, width, _ = beta_values.shape
    slots, tile, _ = alpha_tiles.shape
    groups = alpha_rows.shape[1]
    chunks, strip = rows // width, columns // row_devices
    part, units, lines = strip // subs, rows // width * subs, row_devices // 4
    stored = slots * tile // width
    row_peers, col_peers = row_devices - 1, col_devices - 1
    dma, half = pltpu.SemaphoreType.DMA, jnp.bfloat16
    anywhere = pl.BlockSpec(memory_space=pl.ANY)
    scalars = pl.BlockSpec(memory_space=pltpu.SMEM)
    return pl.pallas_call(
        functools.partial(fused_kernel, chunks, subs, share),
        in_specs=[scalars, scalars, anywhere, anywhere, anywhere],
        out_specs=[anywhere, anywhere],
        out_shape=[
            jax.ShapeDtypeStruct((row_devices, strip, groups * tile), half),
            jax.ShapeDtypeStruct((col_devices, strip, row_devices * tile), half),
        ],
        scratch_shapes=[pltpu.VMEM((col_devices * tiles, width, width), half)] * chunks
        + [pltpu.VMEM((columns, width), half)] * chunks
        + [pltpu.VMEM((row_devices * groups, part, 2 * width), half)] * subs
        + [
            pltpu.VMEM((tiles, listed * width, width), half),
            pltpu.VMEM((slots, tile, tile), half),
            pltpu.VMEM((stored, tile, width), half),
            pltpu.VMEM((row_devices * stored, tile, width), half),
            pltpu.VMEM((chunks, row_devices, strip, width), half),
            pltpu.VMEM((row_devices * slots, part, tile), half),
            pltpu.VMEM((subs, row_devices, part, groups * tile), half),
            pltpu.VMEM((subs, groups, part, row_devices * tile), half),
            pltpu.VMEM((8, width), jnp.int32),
            pltpu.VMEM((row_devices, 8, width), jnp.int32),
            pltpu.VMEM((8, width), jnp.int32),
            pltpu.SMEM((8, width), jnp.int32),
            dma((2,)),
            dma((chunks, tiles)), dma((chunks, col_peers, tiles)), dma((chunks, col_peers, tiles)),
            dma((units,)), dma((units, row_peers)), dma((units, row_peers)),
            dma, dma((row_peers,)), dma((row_peers,)), dma,
        ]
        + [dma((lines - 1,))] * 4
        + [dma((lines,))] * 2
        + [dma((2 * lines,))] * 6
        + [
            dma,
            dma((subs,)), dma((subs, row_peers)), dma((subs, row_peers)),
            dma((subs,)), dma((subs, col_peers)), dma((subs, col_peers)),
            pltpu.SemaphoreType.REGULAR((lines,)),
        ],
        compiler_params=pltpu.CompilerParams(
            collective_id=0, has_side_effects=True, vmem_limit_bytes=48 << 20
        ),
        cost_estimate=pl.CostEstimate(flops=1 << 37, bytes_accessed=1 << 28, transcendentals=0),
        name="fused",
    )(
        jnp.transpose(beta_rows, (2, 0, 1)), alpha_rows, c_matrix,
        beta_values.reshape(tiles, listed * width, width), alpha_tiles,
    )


def per_device(c_matrix, beta_values, beta_rows, alpha_values, alpha_rows, gaps):
    row_devices, col_devices = lax.axis_size("row"), lax.axis_size("col")
    groups, stretch, columns = c_matrix.shape
    pairs, _, _, listed, tile, _ = alpha_values.shape
    rows, width = groups * stretch, beta_values.shape[-1]
    c_rows = c_matrix.reshape(rows, columns)
    alpha_tiles = alpha_values.reshape(pairs * groups, listed, tile, tile)
    strip, subs = columns // row_devices, 2
    own_kernels = pairs == 1 and groups == 2 and stretch == tile and 2 * tile == 3 * width
    own_kernels = own_kernels and row_devices % 4 == 0 and row_devices * groups * listed == width
    own_kernels = own_kernels and strip % (16 * subs) == 0 and 2 * strip % width == 0
    if own_kernels:
        own, mirror = fused(
            c_rows, beta_values, beta_rows, alpha_tiles.reshape(-1, tile, tile), alpha_rows,
            row_devices, col_devices, subs, SHARE,
        )
    else:
        rows_all = lax.all_gather(alpha_rows.reshape(pairs * groups, listed), "row")
        alpha_all = lax.all_gather(alpha_tiles, "row")
        xt = beta_products(lax.all_gather(c_rows, "col"), beta_values, beta_rows)
        xt = jnp.moveaxis(xt.reshape(pairs, row_devices, stretch, rows), 1, 0)
        x_strip = lax.all_to_all(xt, "row", 0, 0)[None]
        own, mirror = alpha_products(alpha_all, rows_all, x_strip, groups)
        own = lax.all_to_all(own, "row", 0, 0)
        mirror = lax.all_to_all(mirror, "col", 0, 0)
    out = final(
        own.reshape(columns, groups * stretch),
        mirror.reshape(groups * stretch, columns),
        gaps.reshape(groups * stretch, columns),
    )
    return out.reshape(gaps.shape)


def solution(mesh):
    placed = (
        P(None, "row", "col"),
        P(None, "col", None, None, None),
        P(None, "col", None),
        P(None, None, "row", None, None, None),
        P(None, None, "row", None),
        P(None, "row", "col"),
    )
    return jax.shard_map(
        per_device, mesh=mesh, in_specs=placed, out_specs=P(None, "row", "col"), check_vma=False
    )
```

```python
import functools

import jax
import jax.numpy as jnp
from jax import lax
from jax.experimental import pallas as pl
from jax.experimental.pallas import tpu as pltpu
from jax.sharding import PartitionSpec as P

CONTRACT_LAST = (((1,), (1,)), ((), ()))
SHARE = (2, 2)


def beta_kernel(listed, held, rows_ref, c_ref, b_ref, xt_ref):
    k, j = pl.program_id(0), pl.program_id(1)
    width = b_ref.shape[-1]
    picked = []
    for z in range(listed):
        tile = rows_ref[k, j, z]
        owner = tile // held
        start = pl.multiple_of((tile - owner * held) * width, width)
        picked.append(c_ref[owner, :, pl.ds(start, width)])
    lhs = b_ref[0, 0].reshape(listed * width, width)
    product = lax.dot_general(
        lhs, jnp.concatenate(picked, axis=1), (((0,), (1,)), ((), ())),
        preferred_element_type=jnp.float32,
    )
    xt_ref[0] = product.astype(xt_ref.dtype)


def beta_products(gathered, beta_values, beta_rows):
    pairs, tiles, listed, width, _ = beta_values.shape
    owners, rows, columns = gathered.shape
    return pl.pallas_call(
        functools.partial(beta_kernel, listed, columns // width),
        grid_spec=pltpu.PrefetchScalarGridSpec(
            num_scalar_prefetch=1,
            grid=(pairs, tiles),
            in_specs=[
                pl.BlockSpec((owners, rows, columns), lambda k, j, s: (0, 0, 0)),
                pl.BlockSpec((1, 1, listed, width, width), lambda k, j, s: (k, j, 0, 0, 0)),
            ],
            out_specs=pl.BlockSpec((1, width, rows), lambda k, j, s: (k, j, 0)),
        ),
        out_shape=jax.ShapeDtypeStruct((pairs, tiles * width, rows), jnp.bfloat16),
        compiler_params=pltpu.CompilerParams(vmem_limit_bytes=56 << 20),
        name="beta_products",
    )(beta_rows, gathered, beta_values)


def alpha_kernel(groups, rows_ref, a_ref, x_ref, own_ref, mirror_ref, acc_ref):
    r = pl.program_id(0)
    row_devices = pl.num_programs(0)
    pairs = x_ref.shape[2]
    listed, tile = rows_ref.shape[2], acc_ref.shape[1]

    @pl.when(r == 0)
    def _():
        acc_ref[...] = jnp.zeros_like(acc_ref)

    for i in range(x_ref.shape[1]):
        at = r * x_ref.shape[1] + i
        for k in range(pairs):
            parts = [x_ref[c, i, k] for c in range(x_ref.shape[0])]
            merged = jnp.concatenate(parts, axis=1) if len(parts) > 1 else parts[0]
            for g in range(groups):
                x = merged[:, g * tile : (g + 1) * tile]
                slot = k * groups + g

                @pl.loop(0, listed)
                def _(z):
                    acc_ref[rows_ref[at, slot, z]] += lax.dot_general(
                        a_ref[i, slot, z], x, CONTRACT_LAST, preferred_element_type=jnp.float32
                    )

    @pl.when(r == row_devices - 1)
    def _():
        count = acc_ref.shape[0] // groups
        for g in range(groups):
            for to in range(count):
                turned = acc_ref[g * count + to].astype(own_ref.dtype).T
                own_ref[to, :, g * tile : (g + 1) * tile] = turned
                mirror_ref[g, :, to * tile : (to + 1) * tile] = turned


def alpha_products(alpha_all, rows_all, x_strip, groups):
    row_devices, rest = alpha_all.shape[0], alpha_all.shape[1:]
    tile = x_strip.shape[0] * x_strip.shape[-1] // groups
    per = 1
    chunks, _, pairs, strip, chunk = x_strip.shape
    return pl.pallas_call(
        functools.partial(alpha_kernel, groups),
        grid_spec=pltpu.PrefetchScalarGridSpec(
            num_scalar_prefetch=1,
            grid=(row_devices // per,),
            in_specs=[
                pl.BlockSpec((per,) + rest, lambda r, s: (r,) + (0,) * len(rest)),
                pl.BlockSpec((chunks, per, pairs, strip, chunk), lambda r, s: (0, r, 0, 0, 0)),
            ],
            out_specs=[
                pl.BlockSpec((row_devices, strip, groups * tile), lambda r, s: (0, 0, 0)),
                pl.BlockSpec((groups, strip, row_devices * tile), lambda r, s: (0, 0, 0)),
            ],
            scratch_shapes=[pltpu.VMEM((groups * row_devices, tile, strip), jnp.float32)],
        ),
        out_shape=[
            jax.ShapeDtypeStruct((row_devices, strip, groups * tile), jnp.bfloat16),
            jax.ShapeDtypeStruct((groups, strip, row_devices * tile), jnp.bfloat16),
        ],
        compiler_params=pltpu.CompilerParams(vmem_limit_bytes=56 << 20),
        name="alpha_products",
    )(rows_all, alpha_all, x_strip)


def final_kernel(block, own, mirror, gaps, out_ref, out, out_sem):
    steps = out.shape[1] // block

    def store(i):
        span = pl.ds(i * block, block)
        return pltpu.make_async_copy(out.at[:, span], out_ref.at[:, span], out_sem.at[i])

    for i in range(steps):
        span = slice(i * block, (i + 1) * block)
        turned = own[span, :].T.astype(jnp.float32)
        out[:, span] = (turned + mirror[:, span].astype(jnp.float32)) / gaps[:, span]
        store(i).start()
    for i in range(steps):
        store(i).wait()


def final(own, mirror, gaps):
    rows, columns = gaps.shape
    block = next(n for n in (384, 256, 128) if columns % n == 0)
    whole = pl.BlockSpec(memory_space=pltpu.VMEM)
    return pl.pallas_call(
        functools.partial(final_kernel, block),
        in_specs=[whole] * 3,
        out_specs=pl.BlockSpec(memory_space=pl.ANY),
        out_shape=jax.ShapeDtypeStruct((rows, columns), jnp.float32),
        scratch_shapes=[
            pltpu.VMEM(gaps.shape, gaps.dtype), pltpu.SemaphoreType.DMA((columns // block,)),
        ],
        compiler_params=pltpu.CompilerParams(vmem_limit_bytes=20 << 20),
        name="final",
    )(own, mirror, gaps)


def remote(src, dst, send_sem, recv_sem, axis, peer):
    return pltpu.make_async_remote_copy(
        src_ref=src, dst_ref=dst, send_sem=send_sem, recv_sem=recv_sem,
        device_id={axis: peer}, device_id_type=pl.DeviceIdType.MESH,
    )


def fused_kernel(chunks, subs, share, rows_ref, lists_ref, c_ref, b_ref, alpha_ref, own_ref, mirror_ref, *scratch):
    held, sent, xt = scratch[:chunks], scratch[chunks : 2 * chunks], scratch[2 * chunks : 2 * chunks + subs]
    (b_own, flat, a_own, a_all, xr, stack, own_out, mirror_out, list_own, list_all, table, picks,
     load_sem, c_own, c_send, c_recv, x_own, x_send, x_recv, l_own, l_send, l_recv, a_sem,
     up_send, up_recv, down_send, down_recv, y_send, y_recv, core_send, core_recv,
     x_side, x_side_recv, core_side, core_side_recv, t_sem,
     o_own, o_send, o_recv, m_own, m_send, m_recv, rounds) = scratch[2 * chunks + subs :]
    row_devices, row = lax.axis_size("row"), lax.axis_index("row")
    col_devices, col = lax.axis_size("col"), lax.axis_index("col")
    rows, columns = c_ref.shape
    tiles, depth, width = b_own.shape
    listed_b = depth // width
    slots, tile, _ = flat.shape
    groups = lists_ref.shape[1]
    listed = slots // groups
    chunk, strip = rows // chunks, columns // row_devices
    part = strip // subs
    chips = row_devices // 2
    per = tiles // chips
    stored = a_own.shape[0]
    lines = row_devices // 4
    chip, core = row // 2, lax.rem(row, 2)
    z, y = row // 4, lax.rem(chip, 2)
    units = [(c, s * part, part) for s in range(subs) for c in range(chunks)]
    straight, turned = range(2, chips, 2), range(1, chips, 2)

    def own_c(c, t):
        return pltpu.make_async_copy(
            c_ref.at[pl.ds(c * chunk, chunk), pl.ds(pl.multiple_of(t * width, width), width)],
            held[c].at[col * tiles + t], c_own.at[c, t],
        )

    def send_c(c, off, t):
        return remote(
            c_ref.at[pl.ds(c * chunk, chunk), pl.ds(pl.multiple_of(t * width, width), width)],
            held[c].at[col * tiles + t], c_send.at[c, off - 1, t], c_recv.at[c, off - 1, t],
            "col", lax.rem(col + off, col_devices),
        )

    def send_x(u, off, peer):
        c, first, size = units[u]
        start = pl.multiple_of(peer * strip + first, 16)
        return remote(
            sent[c].at[pl.ds(start, size), :], xr.at[c, row, pl.ds(first, size), :],
            x_send.at[u, off - 1], x_recv.at[u, off - 1], "row", peer,
        )

    def own_x(u):
        c, first, size = units[u]
        start = pl.multiple_of(row * strip + first, 16)
        return pltpu.make_async_copy(
            sent[c].at[pl.ds(start, size), :], xr.at[c, row, pl.ds(first, size), :], x_own.at[u]
        )

    def send_own(s, off, peer):
        return remote(
            own_out.at[s, peer], own_ref.at[row, pl.ds(s * part, part), :],
            o_send.at[s, off - 1], o_recv.at[s, off - 1], "row", peer,
        )

    def stay_own(s):
        return pltpu.make_async_copy(
            own_out.at[s, row], own_ref.at[row, pl.ds(s * part, part), :], o_own.at[s]
        )

    def send_mirror(s, off):
        peer = lax.rem(col + off, col_devices)
        return remote(
            mirror_out.at[s, peer], mirror_ref.at[col, pl.ds(s * part, part), :],
            m_send.at[s, off - 1], m_recv.at[s, off - 1], "col", peer,
        )

    def stay_mirror(s):
        return pltpu.make_async_copy(
            mirror_out.at[s, col], mirror_ref.at[col, pl.ds(s * part, part), :], m_own.at[s]
        )

    def send_list(off):
        return remote(
            list_own, list_all.at[row], l_send.at[off - 1], l_recv.at[off - 1], "row",
            lax.rem(row + off, row_devices),
        )

    def reach(i):
        odd = lax.rem(i, 2)
        return lax.rem(i + 1, chips)

    def pair(i):
        return lax.rem(chip + reach(i), chips)

    def send_pair(send, i):
        for e in range(2):
            send(2 * reach(i) + e - core, 2 * pair(i) + e).start()

    def block(at_z, at_y, at_core):
        return (at_z * 2 + at_y) * 2 + at_core

    def neighbours(act):
        act("col", 1 - col)
        act("row", block(z, y, 1 - core))
        act("row", block(z, 1 - y, core))

        @pl.when(z >= 1)
        def _():
            act("row", block(z - 1, y, core))

        @pl.when(z + 1 < lines)
        def _():
            act("row", block(z + 1, y, core))

    inner = lax.min(z, 1) + lax.min(lines - 1 - z, 1)

    def signal_near(sem):
        def act(axis, peer):
            pl.semaphore_signal(
                sem, inc=1, device_id={axis: peer}, device_id_type=pl.DeviceIdType.MESH
            )

        neighbours(act)

    def meet(sem):
        signal_near(sem)
        pl.semaphore_wait(sem, 3 + inner)

    def send_later(u, steps):
        for o in steps:
            for e in range(2):
                send_x(u, 2 * o + e - core, 2 * lax.rem(chip + o, chips) + e).start()
        if steps == straight:
            send_x(u, partner_off, partner).start()
            own_x(u).start()

    partner, partner_off = row + 1 - 2 * core, 1 + core * (row_devices - 2)

    def cut(ref, at, first, size):
        return ref.at[pl.ds(at * stored + first, size)]

    def hand(at, first, size, send_sem, recv_sem, peer, axis="row", source=None):
        held_part = cut(a_all, at, first, size)
        if source is not None:
            held_part = source.at[pl.ds(first, size)]
        return remote(held_part, cut(a_all, at, first, size), send_sem, recv_sem, axis, peer)

    def main(same):
        part_share = share[0] if same else share[1]
        return col * part_share, stored - part_share

    def gives(same):
        part_share = share[0] if same else share[1]
        return col * (stored - part_share), part_share

    def gets(same):
        part_share = share[0] if same else share[1]
        return (1 - col) * (stored - part_share), part_share

    def place(at_z, same):
        at_y = y if same else 1 - y
        return block(at_z, at_y, core), at_z * 2 + at_y

    other_core = block(z, y, 1 - core)

    def up(step, source=None):
        at = block(z - step, y, core)
        return hand(at, *main(True), up_send.at[step], up_recv.at[step], block(z + 1, y, core), source=source)

    def down(step, source=None):
        at = block(z + step, y, core)
        return hand(at, *main(True), down_send.at[step], down_recv.at[step], block(z - 1, y, core), source=source)

    def over_y(at_z, source=None):
        at = block(at_z, y, core)
        return hand(at, *main(False), y_send.at[at_z], y_recv.at[at_z], block(z, 1 - y, core), source=source)

    def over_core(at_z, same, source=None):
        at, sem = place(at_z, same)
        return hand(at, *main(same), core_send.at[sem], core_recv.at[sem], other_core, source=source)

    def side_x(at_z, same):
        at, sem = place(at_z, same)
        return hand(at, *gives(same), x_side.at[sem], x_side_recv.at[sem], 1 - col, "col")

    def side_core(at_z, same, source=None):
        at, sem = place(at_z, same)
        return hand(at, *gets(same), core_side.at[sem], core_side_recv.at[sem], other_core, source=source)

    def arrived(at, span, recv_sem, send_sem):
        hand(at, *span, send_sem, recv_sem, other_core).wait_recv()

    def spread(at_z, same):
        over_core(at_z, same).start()
        if gives(same)[1]:
            side_x(at_z, same).start()

    def relay(step):
        @pl.when(z - 1 - step >= 0)
        def _():
            arrived(block(z - 1 - step, y, core), main(True), up_recv.at[step], up_send.at[step])
            if step + 1 < lines - 1:

                @pl.when(z + 1 < lines)
                def _():
                    up(step + 1).start()

            over_y(z - 1 - step).start()
            spread(z - 1 - step, True)

        @pl.when(z + 1 + step < lines)
        def _():
            arrived(block(z + 1 + step, y, core), main(True), down_recv.at[step], down_send.at[step])
            if step + 1 < lines - 1:

                @pl.when(z >= 1)
                def _():
                    down(step + 1).start()

            over_y(z + 1 + step).start()
            spread(z + 1 + step, True)

    def at_distance(d, body):
        @pl.when(z + d < lines)
        def _():
            body(z + d)

        @pl.when(z >= d)
        def _():
            body(z - d)

    def cross(at_z):
        arrived(block(at_z, 1 - y, core), main(False), y_recv.at[at_z], y_send.at[at_z])
        spread(at_z, False)

    def others(body):
        for d in range(lines):
            for same in (True, False):
                if gives(same)[1] and d > 0:
                    at_distance(d, functools.partial(body, same=same))
                elif gives(same)[1] and not same:
                    body(z, same)

    def side_arrived(at_z, same):
        side_x(at_z, same).wait_recv()
        side_core(at_z, same).start()

    def multiply(c, group):
        for q in range(per):
            j = group * per + q
            picked = [held[c][rows_ref[s, 0, j]] for s in range(listed_b)]
            product = lax.dot_general(
                b_own[j], jnp.concatenate(picked, axis=1), (((0,), (1,)), ((), ())),
                preferred_element_type=jnp.float32,
            )
            sent[c][pl.ds(pl.multiple_of(j * width, width), width), :] = product.astype(jnp.bfloat16)

    def make_table():
        total = list_all[0]
        for r in range(1, row_devices):
            total = total + list_all[r]
        square = (width, width)
        by_lane = jnp.broadcast_to(total[0:1], square)
        lane = lax.broadcasted_iota(jnp.int32, square, 1)
        sub = lax.broadcasted_iota(jnp.int32, square, 0)
        keys = by_lane * width + lane

        def count(mask):
            return jnp.sum(jnp.where(mask, 1, 0), axis=0, keepdims=True)

        rank = jnp.broadcast_to(count(keys.T < keys), square)
        hit = rank.T == lane
        by_sub = by_lane.T
        order = jnp.sum(jnp.where(hit, sub, 0), axis=0, keepdims=True)
        target = jnp.sum(jnp.where(hit, by_sub, 0), axis=0, keepdims=True)
        began = count(by_sub < target)
        source, slot = order // slots, order % slots
        table[0:1, :] = source * stored + slot
        table[1:2, :] = source * stored + slots + slot % listed
        table[2:3, :] = order // listed
        table[3:4, :] = jnp.where(lane[0:1] > began, 1, 0)
        table[4:5, :] = count(by_sub <= lane) - 1
        table[5:8, :] = jnp.zeros((3, width), jnp.int32)

    def prepare(s):
        lane = lax.broadcasted_iota(jnp.int32, (part, width), 1)
        low = lane < width // 2

        @pl.loop(0, row_devices)
        def _(r):
            cut = pl.ds(s * part, part)
            middle = xr[1, r, cut, :]
            blank = jnp.zeros_like(middle)
            xt[s][r * groups, :, 0:width] = xr[0, r, cut, :]
            xt[s][r * groups, :, width : 2 * width] = jnp.where(low, middle, blank)
            xt[s][r * groups + 1, :, 0:width] = xr[2, r, cut, :]
            xt[s][r * groups + 1, :, width : 2 * width] = jnp.where(low, blank, middle)

    def contract(s):
        def step(p, run):
            weights = jnp.concatenate([a_all[picks[0, p]], a_all[picks[1, p]]], axis=1)
            product = lax.dot_general(
                xt[s][picks[2, p]], weights, CONTRACT_LAST, preferred_element_type=jnp.float32
            )
            run = product + run * picks[3, p].astype(jnp.float32)
            stack[p] = run.astype(stack.dtype)
            return run

        lax.fori_loop(0, width, step, jnp.zeros((part, tile), jnp.float32), unroll=16)

    def assemble(s, k):
        found = [[stack[picks[4, g * row_devices + 2 * k + e]] for e in range(2)] for g in range(groups)]
        for e in range(2):
            own_out[s, 2 * k + e] = jnp.concatenate([found[g][e] for g in range(groups)], axis=1)
        for g in range(groups):
            start = pl.multiple_of(k * 2 * tile, width)
            mirror_out[s, g, :, pl.ds(start, 2 * tile)] = jnp.concatenate(found[g], axis=1)

    load_b = pltpu.make_async_copy(b_ref, b_own, load_sem.at[0])
    load_a = pltpu.make_async_copy(alpha_ref, flat, load_sem.at[1])
    load_a.start()
    barrier = pltpu.get_barrier_semaphore()
    signal_near(barrier)
    lane = lax.broadcasted_iota(jnp.int32, list_own.shape, 1)
    mine = jnp.zeros(list_own.shape, jnp.int32)
    for g in range(groups):
        for s in range(listed):
            mine = jnp.where(lane == row * slots + g * listed + s, lists_ref[0, g, 0, s], mine)
    list_own[...] = mine
    load_a.wait()
    for s in range(listed):
        first, second = flat[s], flat[listed + s]
        a_own[s] = first[:, :width]
        a_own[listed + s] = second[:, tile - width :]
        a_own[slots + s] = jnp.concatenate([first[:, width:], second[:, : tile - width]], axis=1)
    keep_list = pltpu.make_async_copy(list_own, list_all.at[row], l_own)
    keep_a = pltpu.make_async_copy(a_own, cut(a_all, row, 0, stored), a_sem)
    pl.semaphore_wait(barrier, 3 + inner)

    @pl.when(z + 1 < lines)
    def _():
        up(0, a_own).start()

    @pl.when(z >= 1)
    def _():
        down(0, a_own).start()

    over_y(z, a_own).start()
    over_core(z, True, a_own).start()
    if share[0]:
        side_core(z, True, a_own).start()
    for c in range(chunks):
        for off in range(1, col_devices):

            @pl.loop(0, tiles)
            def _(t):
                send_c(c, off, t).start()

        if c == 0:
            keep_list.start()
            keep_a.start()
            load_b.start()

        @pl.loop(0, tiles)
        def _(t):
            own_c(c, t).start()

    for n in range(lines):
        meet(rounds.at[n])

    @pl.loop(1, row_devices)
    def _(off):
        send_list(off).start()

    load_b.wait()
    move_table = pltpu.make_async_copy(table, picks, t_sem)
    now, later = [[0], [1], [2]], [[(3, straight), (3, turned)], [(4, straight)], [(5, straight), (4, turned), (5, turned)]]
    relayed = 0
    for c in range(chunks):
        if relayed < lines - 1:
            relay(relayed)
            relayed += 1

        @pl.loop(0, tiles)
        def _(t):
            own_c(c, t).wait()
            for off in range(1, col_devices):
                send_c(c, off, t).wait_recv()

        @pl.loop(0, chips)
        def _(i):
            multiply(c, pair(i))

            @pl.when(i > 0)
            def _():
                for u in now[c]:
                    send_pair(functools.partial(send_x, u), i - 1)

        for u in now[c]:
            send_x(u, partner_off, partner).start()
            own_x(u).start()
        for u, steps in later[c]:
            send_later(u, steps)
        if c == 0:
            keep_list.wait()

            @pl.loop(1, row_devices)
            def _(off):
                send_list(off).wait_recv()

            make_table()
            move_table.start()
            cross(z)

    for step in range(relayed, lines - 1):
        relay(step)
    for d in range(1, lines):
        at_distance(d, cross)
    others(side_arrived)
    keep_a.wait()
    move_table.wait()
    for at_z in range(lines):
        for same in (True, False):
            at, sem = block(at_z, y if same else 1 - y, 1 - core), place(at_z, same)[1]
            arrived(at, main(same), core_recv.at[sem], core_send.at[sem])
            if gets(same)[1]:
                arrived(at, gets(same), core_side_recv.at[sem], core_side.at[sem])
    for s in range(subs):
        for u in range(s * chunks, (s + 1) * chunks):
            own_x(u).wait()

            @pl.loop(1, row_devices)
            def _(off):
                send_x(u, off, lax.rem(row + off, row_devices)).wait_recv()

        prepare(s)
        contract(s)

        @pl.loop(0, chips)
        def _(i):
            assemble(s, pair(i))

            @pl.when(i > 0)
            def _():
                send_pair(functools.partial(send_own, s), i - 1)

        send_own(s, partner_off, partner).start()
        for off in range(1, col_devices):
            send_mirror(s, off).start()
        stay_own(s).start()
        stay_mirror(s).start()

    for step in range(lines - 1):

        @pl.when((z - step >= 0) & (z + 1 < lines))
        def _():
            up(step).wait_send()

        @pl.when((z + step < lines) & (z >= 1))
        def _():
            down(step).wait_send()

    for at_z in range(lines):
        over_y(at_z).wait_send()
        for same in (True, False):
            over_core(at_z, same).wait_send()
            if gets(same)[1]:
                side_core(at_z, same).wait_send()

    others(lambda at_z, same: side_x(at_z, same).wait_send())
    for c in range(chunks):
        for off in range(1, col_devices):

            @pl.loop(0, tiles)
            def _(t):
                send_c(c, off, t).wait_send()

    @pl.loop(1, row_devices)
    def _(off):
        peer = lax.rem(row + off, row_devices)
        send_list(off).wait_send()
        for u in range(len(units)):
            send_x(u, off, peer).wait_send()

    for s in range(subs):
        stay_own(s).wait()
        stay_mirror(s).wait()
        for off in range(1, col_devices):
            send_mirror(s, off).wait()

        @pl.loop(1, row_devices)
        def _(off):
            send_own(s, off, lax.rem(row + off, row_devices)).wait()


def fused(c_matrix, beta_values, beta_rows, alpha_tiles, alpha_rows, row_devices, col_devices, subs, share):
    rows, columns = c_matrix.shape
    _, tiles, listed, width, _ = beta_values.shape
    slots, tile, _ = alpha_tiles.shape
    groups = alpha_rows.shape[1]
    chunks, strip = rows // width, columns // row_devices
    part, units, lines = strip // subs, rows // width * subs, row_devices // 4
    stored = slots * tile // width
    row_peers, col_peers = row_devices - 1, col_devices - 1
    dma, half = pltpu.SemaphoreType.DMA, jnp.bfloat16
    anywhere = pl.BlockSpec(memory_space=pl.ANY)
    scalars = pl.BlockSpec(memory_space=pltpu.SMEM)
    return pl.pallas_call(
        functools.partial(fused_kernel, chunks, subs, share),
        in_specs=[scalars, scalars, anywhere, anywhere, anywhere],
        out_specs=[anywhere, anywhere],
        out_shape=[
            jax.ShapeDtypeStruct((row_devices, strip, groups * tile), half),
            jax.ShapeDtypeStruct((col_devices, strip, row_devices * tile), half),
        ],
        scratch_shapes=[pltpu.VMEM((col_devices * tiles, width, width), half)] * chunks
        + [pltpu.VMEM((columns, width), half)] * chunks
        + [pltpu.VMEM((row_devices * groups, part, 2 * width), half)] * subs
        + [
            pltpu.VMEM((tiles, listed * width, width), half),
            pltpu.VMEM((slots, tile, tile), half),
            pltpu.VMEM((stored, tile, width), half),
            pltpu.VMEM((row_devices * stored, tile, width), half),
            pltpu.VMEM((chunks, row_devices, strip, width), half),
            pltpu.VMEM((row_devices * slots, part, tile), half),
            pltpu.VMEM((subs, row_devices, part, groups * tile), half),
            pltpu.VMEM((subs, groups, part, row_devices * tile), half),
            pltpu.VMEM((8, width), jnp.int32),
            pltpu.VMEM((row_devices, 8, width), jnp.int32),
            pltpu.VMEM((8, width), jnp.int32),
            pltpu.SMEM((8, width), jnp.int32),
            dma((2,)),
            dma((chunks, tiles)), dma((chunks, col_peers, tiles)), dma((chunks, col_peers, tiles)),
            dma((units,)), dma((units, row_peers)), dma((units, row_peers)),
            dma, dma((row_peers,)), dma((row_peers,)), dma,
        ]
        + [dma((lines - 1,))] * 4
        + [dma((lines,))] * 2
        + [dma((2 * lines,))] * 6
        + [
            dma,
            dma((subs,)), dma((subs, row_peers)), dma((subs, row_peers)),
            dma((subs,)), dma((subs, col_peers)), dma((subs, col_peers)),
            pltpu.SemaphoreType.REGULAR((lines,)),
        ],
        compiler_params=pltpu.CompilerParams(
            collective_id=0, has_side_effects=True, vmem_limit_bytes=48 << 20
        ),
        cost_estimate=pl.CostEstimate(flops=1 << 37, bytes_accessed=1 << 28, transcendentals=0),
        name="fused",
    )(
        jnp.transpose(beta_rows, (2, 0, 1)), alpha_rows, c_matrix,
        beta_values.reshape(tiles, listed * width, width), alpha_tiles,
    )


def per_device(c_matrix, beta_values, beta_rows, alpha_values, alpha_rows, gaps):
    row_devices, col_devices = lax.axis_size("row"), lax.axis_size("col")
    groups, stretch, columns = c_matrix.shape
    pairs, _, _, listed, tile, _ = alpha_values.shape
    rows, width = groups * stretch, beta_values.shape[-1]
    c_rows = c_matrix.reshape(rows, columns)
    alpha_tiles = alpha_values.reshape(pairs * groups, listed, tile, tile)
    strip, subs = columns // row_devices, 2
    own_kernels = pairs == 1 and groups == 2 and stretch == tile and 2 * tile == 3 * width
    own_kernels = own_kernels and row_devices % 4 == 0 and row_devices * groups * listed == width
    own_kernels = own_kernels and strip % (16 * subs) == 0 and 2 * strip % width == 0
    if own_kernels:
        own, mirror = fused(
            c_rows, beta_values, beta_rows, alpha_tiles.reshape(-1, tile, tile), alpha_rows,
            row_devices, col_devices, subs, SHARE,
        )
    else:
        rows_all = lax.all_gather(alpha_rows.reshape(pairs * groups, listed), "row")
        alpha_all = lax.all_gather(alpha_tiles, "row")
        xt = beta_products(lax.all_gather(c_rows, "col"), beta_values, beta_rows)
        xt = jnp.moveaxis(xt.reshape(pairs, row_devices, stretch, rows), 1, 0)
        x_strip = lax.all_to_all(xt, "row", 0, 0)[None]
        own, mirror = alpha_products(alpha_all, rows_all, x_strip, groups)
        own = lax.all_to_all(own, "row", 0, 0)
        mirror = lax.all_to_all(mirror, "col", 0, 0)
    out = final(
        own.reshape(columns, groups * stretch),
        mirror.reshape(groups * stretch, columns),
        gaps.reshape(groups * stretch, columns),
    )
    return out.reshape(gaps.shape)


def solution(mesh):
    placed = (
        P(None, "row", "col"),
        P(None, "col", None, None, None),
        P(None, "col", None),
        P(None, None, "row", None, None, None),
        P(None, None, "row", None),
        P(None, "row", "col"),
    )
    return jax.shard_map(
        per_device, mesh=mesh, in_specs=placed, out_specs=P(None, "row", "col"), check_vma=False
    )
```

```python
import functools

import jax
import jax.numpy as jnp
from jax import lax
from jax.experimental import pallas as pl
from jax.experimental.pallas import tpu as pltpu
from jax.sharding import PartitionSpec as P

CONTRACT_LAST = (((1,), (1,)), ((), ()))
SHARE = (2, 2)


def beta_kernel(listed, held, rows_ref, c_ref, b_ref, xt_ref):
    k, j = pl.program_id(0), pl.program_id(1)
    width = b_ref.shape[-1]
    picked = []
    for z in range(listed):
        tile = rows_ref[k, j, z]
        owner = tile // held
        start = pl.multiple_of((tile - owner * held) * width, width)
        picked.append(c_ref[owner, :, pl.ds(start, width)])
    lhs = b_ref[0, 0].reshape(listed * width, width)
    product = lax.dot_general(
        lhs, jnp.concatenate(picked, axis=1), (((0,), (1,)), ((), ())),
        preferred_element_type=jnp.float32,
    )
    xt_ref[0] = product.astype(xt_ref.dtype)


def beta_products(gathered, beta_values, beta_rows):
    pairs, tiles, listed, width, _ = beta_values.shape
    owners, rows, columns = gathered.shape
    return pl.pallas_call(
        functools.partial(beta_kernel, listed, columns // width),
        grid_spec=pltpu.PrefetchScalarGridSpec(
            num_scalar_prefetch=1,
            grid=(pairs, tiles),
            in_specs=[
                pl.BlockSpec((owners, rows, columns), lambda k, j, s: (0, 0, 0)),
                pl.BlockSpec((1, 1, listed, width, width), lambda k, j, s: (k, j, 0, 0, 0)),
            ],
            out_specs=pl.BlockSpec((1, width, rows), lambda k, j, s: (k, j, 0)),
        ),
        out_shape=jax.ShapeDtypeStruct((pairs, tiles * width, rows), jnp.bfloat16),
        compiler_params=pltpu.CompilerParams(vmem_limit_bytes=56 << 20),
        name="beta_products",
    )(beta_rows, gathered, beta_values)


def alpha_kernel(groups, rows_ref, a_ref, x_ref, own_ref, mirror_ref, acc_ref):
    r = pl.program_id(0)
    row_devices = pl.num_programs(0)
    pairs = x_ref.shape[2]
    listed, tile = rows_ref.shape[2], acc_ref.shape[1]

    @pl.when(r == 0)
    def _():
        acc_ref[...] = jnp.zeros_like(acc_ref)

    for i in range(x_ref.shape[1]):
        at = r * x_ref.shape[1] + i
        for k in range(pairs):
            parts = [x_ref[c, i, k] for c in range(x_ref.shape[0])]
            merged = jnp.concatenate(parts, axis=1) if len(parts) > 1 else parts[0]
            for g in range(groups):
                x = merged[:, g * tile : (g + 1) * tile]
                slot = k * groups + g

                @pl.loop(0, listed)
                def _(z):
                    acc_ref[rows_ref[at, slot, z]] += lax.dot_general(
                        a_ref[i, slot, z], x, CONTRACT_LAST, preferred_element_type=jnp.float32
                    )

    @pl.when(r == row_devices - 1)
    def _():
        count = acc_ref.shape[0] // groups
        for g in range(groups):
            for to in range(count):
                turned = acc_ref[g * count + to].astype(own_ref.dtype).T
                own_ref[to, :, g * tile : (g + 1) * tile] = turned
                mirror_ref[g, :, to * tile : (to + 1) * tile] = turned


def alpha_products(alpha_all, rows_all, x_strip, groups):
    row_devices, rest = alpha_all.shape[0], alpha_all.shape[1:]
    tile = x_strip.shape[0] * x_strip.shape[-1] // groups
    per = 1
    chunks, _, pairs, strip, chunk = x_strip.shape
    return pl.pallas_call(
        functools.partial(alpha_kernel, groups),
        grid_spec=pltpu.PrefetchScalarGridSpec(
            num_scalar_prefetch=1,
            grid=(row_devices // per,),
            in_specs=[
                pl.BlockSpec((per,) + rest, lambda r, s: (r,) + (0,) * len(rest)),
                pl.BlockSpec((chunks, per, pairs, strip, chunk), lambda r, s: (0, r, 0, 0, 0)),
            ],
            out_specs=[
                pl.BlockSpec((row_devices, strip, groups * tile), lambda r, s: (0, 0, 0)),
                pl.BlockSpec((groups, strip, row_devices * tile), lambda r, s: (0, 0, 0)),
            ],
            scratch_shapes=[pltpu.VMEM((groups * row_devices, tile, strip), jnp.float32)],
        ),
        out_shape=[
            jax.ShapeDtypeStruct((row_devices, strip, groups * tile), jnp.bfloat16),
            jax.ShapeDtypeStruct((groups, strip, row_devices * tile), jnp.bfloat16),
        ],
        compiler_params=pltpu.CompilerParams(vmem_limit_bytes=56 << 20),
        name="alpha_products",
    )(rows_all, alpha_all, x_strip)


def final_kernel(block, own, mirror, gaps, out_ref, out, out_sem):
    steps = out.shape[1] // block

    def store(i):
        span = pl.ds(i * block, block)
        return pltpu.make_async_copy(out.at[:, span], out_ref.at[:, span], out_sem.at[i])

    for i in range(steps):
        span = slice(i * block, (i + 1) * block)
        turned = own[span, :].T.astype(jnp.float32)
        out[:, span] = (turned + mirror[:, span].astype(jnp.float32)) / gaps[:, span]
        store(i).start()
    for i in range(steps):
        store(i).wait()


def final(own, mirror, gaps):
    rows, columns = gaps.shape
    block = next(n for n in (384, 256, 128) if columns % n == 0)
    whole = pl.BlockSpec(memory_space=pltpu.VMEM)
    return pl.pallas_call(
        functools.partial(final_kernel, block),
        in_specs=[whole] * 3,
        out_specs=pl.BlockSpec(memory_space=pl.ANY),
        out_shape=jax.ShapeDtypeStruct((rows, columns), jnp.float32),
        scratch_shapes=[
            pltpu.VMEM(gaps.shape, gaps.dtype), pltpu.SemaphoreType.DMA((columns // block,)),
        ],
        compiler_params=pltpu.CompilerParams(vmem_limit_bytes=20 << 20),
        name="final",
    )(own, mirror, gaps)


def remote(src, dst, send_sem, recv_sem, axis, peer):
    return pltpu.make_async_remote_copy(
        src_ref=src, dst_ref=dst, send_sem=send_sem, recv_sem=recv_sem,
        device_id={axis: peer}, device_id_type=pl.DeviceIdType.MESH,
    )


def fused_kernel(chunks, subs, share, rows_ref, lists_ref, c_ref, b_ref, alpha_ref, own_ref, mirror_ref, *scratch):
    held, sent, xt = scratch[:chunks], scratch[chunks : 2 * chunks], scratch[2 * chunks : 2 * chunks + subs]
    (b_own, a_own, a_all, xr, stack, own_out, mirror_out, list_own, list_all, table, picks,
     load_sem, c_own, c_send, c_recv, x_own, x_send, x_recv, l_own, l_send, l_recv, a_sem,
     up_send, up_recv, down_send, down_recv, y_send, y_recv, core_send, core_recv,
     x_side, x_side_recv, core_side, core_side_recv, t_sem,
     o_own, o_send, o_recv, m_own, m_send, m_recv, rounds) = scratch[2 * chunks + subs :]
    row_devices, row = lax.axis_size("row"), lax.axis_index("row")
    col_devices, col = lax.axis_size("col"), lax.axis_index("col")
    rows, columns = c_ref.shape
    tiles, depth, width = b_own.shape
    listed_b = depth // width
    slots, tile, _ = alpha_ref.shape
    groups = lists_ref.shape[1]
    listed = slots // groups
    chunk, strip = rows // chunks, columns // row_devices
    part = strip // subs
    chips = row_devices // 2
    per = tiles // chips
    stored = a_own.shape[0]
    lines = row_devices // 4
    chip, core = row // 2, lax.rem(row, 2)
    z, y = row // 4, lax.rem(chip, 2)
    units = [(c, s * part, part) for s in range(subs) for c in range(chunks)]
    straight, turned = range(2, chips, 2), range(1, chips, 2)

    def own_c(c, t):
        return pltpu.make_async_copy(
            c_ref.at[pl.ds(c * chunk, chunk), pl.ds(pl.multiple_of(t * width, width), width)],
            held[c].at[col * tiles + t], c_own.at[c, t],
        )

    def send_c(c, off, t):
        return remote(
            c_ref.at[pl.ds(c * chunk, chunk), pl.ds(pl.multiple_of(t * width, width), width)],
            held[c].at[col * tiles + t], c_send.at[c, off - 1, t], c_recv.at[c, off - 1, t],
            "col", lax.rem(col + off, col_devices),
        )

    def send_x(u, off, peer):
        c, first, size = units[u]
        start = pl.multiple_of(peer * strip + first, 16)
        return remote(
            sent[c].at[pl.ds(start, size), :], xr.at[c, row, pl.ds(first, size), :],
            x_send.at[u, off - 1], x_recv.at[u, off - 1], "row", peer,
        )

    def own_x(u):
        c, first, size = units[u]
        start = pl.multiple_of(row * strip + first, 16)
        return pltpu.make_async_copy(
            sent[c].at[pl.ds(start, size), :], xr.at[c, row, pl.ds(first, size), :], x_own.at[u]
        )

    def send_own(s, off, peer):
        return remote(
            own_out.at[s, peer], own_ref.at[row, pl.ds(s * part, part), :],
            o_send.at[s, off - 1], o_recv.at[s, off - 1], "row", peer,
        )

    def stay_own(s):
        return pltpu.make_async_copy(
            own_out.at[s, row], own_ref.at[row, pl.ds(s * part, part), :], o_own.at[s]
        )

    def send_mirror(s, off):
        peer = lax.rem(col + off, col_devices)
        return remote(
            mirror_out.at[s, peer], mirror_ref.at[col, pl.ds(s * part, part), :],
            m_send.at[s, off - 1], m_recv.at[s, off - 1], "col", peer,
        )

    def stay_mirror(s):
        return pltpu.make_async_copy(
            mirror_out.at[s, col], mirror_ref.at[col, pl.ds(s * part, part), :], m_own.at[s]
        )

    def send_list(off):
        return remote(
            list_own, list_all.at[row], l_send.at[off - 1], l_recv.at[off - 1], "row",
            lax.rem(row + off, row_devices),
        )

    def reach(i):
        odd = lax.rem(i, 2)
        return lax.rem(i + 1, chips)

    def pair(i):
        return lax.rem(chip + reach(i), chips)

    def send_pair(send, i):
        for e in range(2):
            send(2 * reach(i) + e - core, 2 * pair(i) + e).start()

    def block(at_z, at_y, at_core):
        return (at_z * 2 + at_y) * 2 + at_core

    def neighbours(act):
        act("col", 1 - col)
        act("row", block(z, y, 1 - core))
        act("row", block(z, 1 - y, core))

        @pl.when(z >= 1)
        def _():
            act("row", block(z - 1, y, core))

        @pl.when(z + 1 < lines)
        def _():
            act("row", block(z + 1, y, core))

    inner = lax.min(z, 1) + lax.min(lines - 1 - z, 1)

    def signal_near(sem):
        def act(axis, peer):
            pl.semaphore_signal(
                sem, inc=1, device_id={axis: peer}, device_id_type=pl.DeviceIdType.MESH
            )

        neighbours(act)

    def meet(sem):
        signal_near(sem)
        pl.semaphore_wait(sem, 3 + inner)

    def send_later(u, steps):
        for o in steps:
            for e in range(2):
                send_x(u, 2 * o + e - core, 2 * lax.rem(chip + o, chips) + e).start()
        if steps == straight:
            send_x(u, partner_off, partner).start()
            own_x(u).start()

    partner, partner_off = row + 1 - 2 * core, 1 + core * (row_devices - 2)

    def cut(ref, at, first, size):
        return ref.at[pl.ds(at * stored + first, size)]

    def hand(at, first, size, send_sem, recv_sem, peer, axis="row", source=None):
        held_part = cut(a_all, at, first, size)
        if source is not None:
            held_part = source.at[pl.ds(first, size)]
        return remote(held_part, cut(a_all, at, first, size), send_sem, recv_sem, axis, peer)

    def main(same):
        part_share = share[0] if same else share[1]
        return col * part_share, stored - part_share

    def gives(same):
        part_share = share[0] if same else share[1]
        return col * (stored - part_share), part_share

    def gets(same):
        part_share = share[0] if same else share[1]
        return (1 - col) * (stored - part_share), part_share

    def place(at_z, same):
        at_y = y if same else 1 - y
        return block(at_z, at_y, core), at_z * 2 + at_y

    other_core = block(z, y, 1 - core)

    def up(step, source=None):
        at = block(z - step, y, core)
        return hand(at, *main(True), up_send.at[step], up_recv.at[step], block(z + 1, y, core), source=source)

    def down(step, source=None):
        at = block(z + step, y, core)
        return hand(at, *main(True), down_send.at[step], down_recv.at[step], block(z - 1, y, core), source=source)

    def over_y(at_z, source=None):
        at = block(at_z, y, core)
        return hand(at, *main(False), y_send.at[at_z], y_recv.at[at_z], block(z, 1 - y, core), source=source)

    def over_core(at_z, same, source=None):
        at, sem = place(at_z, same)
        return hand(at, *main(same), core_send.at[sem], core_recv.at[sem], other_core, source=source)

    def side_x(at_z, same):
        at, sem = place(at_z, same)
        return hand(at, *gives(same), x_side.at[sem], x_side_recv.at[sem], 1 - col, "col")

    def side_core(at_z, same, source=None):
        at, sem = place(at_z, same)
        return hand(at, *gets(same), core_side.at[sem], core_side_recv.at[sem], other_core, source=source)

    def arrived(at, span, recv_sem, send_sem):
        hand(at, *span, send_sem, recv_sem, other_core).wait_recv()

    def spread(at_z, same):
        over_core(at_z, same).start()
        if gives(same)[1]:
            side_x(at_z, same).start()

    def relay(step):
        @pl.when(z - 1 - step >= 0)
        def _():
            arrived(block(z - 1 - step, y, core), main(True), up_recv.at[step], up_send.at[step])
            if step + 1 < lines - 1:

                @pl.when(z + 1 < lines)
                def _():
                    up(step + 1).start()

            over_y(z - 1 - step).start()
            spread(z - 1 - step, True)

        @pl.when(z + 1 + step < lines)
        def _():
            arrived(block(z + 1 + step, y, core), main(True), down_recv.at[step], down_send.at[step])
            if step + 1 < lines - 1:

                @pl.when(z >= 1)
                def _():
                    down(step + 1).start()

            over_y(z + 1 + step).start()
            spread(z + 1 + step, True)

    def at_distance(d, body):
        @pl.when(z + d < lines)
        def _():
            body(z + d)

        @pl.when(z >= d)
        def _():
            body(z - d)

    def cross(at_z):
        arrived(block(at_z, 1 - y, core), main(False), y_recv.at[at_z], y_send.at[at_z])
        spread(at_z, False)

    def others(body):
        for d in range(lines):
            for same in (True, False):
                if gives(same)[1] and d > 0:
                    at_distance(d, functools.partial(body, same=same))
                elif gives(same)[1] and not same:
                    body(z, same)

    def side_arrived(at_z, same):
        side_x(at_z, same).wait_recv()
        side_core(at_z, same).start()

    def multiply(c, group):
        for q in range(per):
            j = group * per + q
            picked = [held[c][rows_ref[s, 0, j]] for s in range(listed_b)]
            product = lax.dot_general(
                b_own[j], jnp.concatenate(picked, axis=1), (((0,), (1,)), ((), ())),
                preferred_element_type=jnp.float32,
            )
            sent[c][pl.ds(pl.multiple_of(j * width, width), width), :] = product.astype(jnp.bfloat16)

    def make_table():
        total = list_all[0]
        for r in range(1, row_devices):
            total = total + list_all[r]
        square = (width, width)
        by_lane = jnp.broadcast_to(total[0:1], square)
        lane = lax.broadcasted_iota(jnp.int32, square, 1)
        sub = lax.broadcasted_iota(jnp.int32, square, 0)
        keys = by_lane * width + lane

        def count(mask):
            return jnp.sum(jnp.where(mask, 1, 0), axis=0, keepdims=True)

        rank = jnp.broadcast_to(count(keys.T < keys), square)
        hit = rank.T == lane
        by_sub = by_lane.T
        order = jnp.sum(jnp.where(hit, sub, 0), axis=0, keepdims=True)
        target = jnp.sum(jnp.where(hit, by_sub, 0), axis=0, keepdims=True)
        began = count(by_sub < target)
        source, slot = order // slots, order % slots
        table[0:1, :] = source * stored + slot
        table[1:2, :] = source * stored + slots + slot % listed
        table[2:3, :] = order // listed
        table[3:4, :] = jnp.where(lane[0:1] > began, 1, 0)
        table[4:5, :] = count(by_sub <= lane) - 1
        table[5:8, :] = jnp.zeros((3, width), jnp.int32)

    def prepare(s):
        lane = lax.broadcasted_iota(jnp.int32, (part, width), 1)
        low = lane < width // 2

        @pl.loop(0, row_devices)
        def _(r):
            cut = pl.ds(s * part, part)
            middle = xr[1, r, cut, :]
            blank = jnp.zeros_like(middle)
            xt[s][r * groups, :, 0:width] = xr[0, r, cut, :]
            xt[s][r * groups, :, width : 2 * width] = jnp.where(low, middle, blank)
            xt[s][r * groups + 1, :, 0:width] = xr[2, r, cut, :]
            xt[s][r * groups + 1, :, width : 2 * width] = jnp.where(low, blank, middle)

    def contract(s):
        def step(p, run):
            weights = jnp.concatenate([a_all[picks[0, p]], a_all[picks[1, p]]], axis=1)
            product = lax.dot_general(
                xt[s][picks[2, p]], weights, CONTRACT_LAST, preferred_element_type=jnp.float32
            )
            run = product + run * picks[3, p].astype(jnp.float32)
            stack[p] = run.astype(stack.dtype)
            return run

        lax.fori_loop(0, width, step, jnp.zeros((part, tile), jnp.float32), unroll=16)

    def assemble(s, k):
        found = [[stack[picks[4, g * row_devices + 2 * k + e]] for e in range(2)] for g in range(groups)]
        for e in range(2):
            own_out[s, 2 * k + e] = jnp.concatenate([found[g][e] for g in range(groups)], axis=1)
        for g in range(groups):
            start = pl.multiple_of(k * 2 * tile, width)
            mirror_out[s, g, :, pl.ds(start, 2 * tile)] = jnp.concatenate(found[g], axis=1)

    load_b = pltpu.make_async_copy(b_ref, b_own, load_sem.at[0])
    barrier = pltpu.get_barrier_semaphore()
    signal_near(barrier)
    lane = lax.broadcasted_iota(jnp.int32, list_own.shape, 1)
    mine = jnp.zeros(list_own.shape, jnp.int32)
    for g in range(groups):
        for s in range(listed):
            mine = jnp.where(lane == row * slots + g * listed + s, lists_ref[0, g, 0, s], mine)
    list_own[...] = mine
    for s in range(listed):
        first, second = alpha_ref[s], alpha_ref[listed + s]
        a_own[s] = first[:, :width]
        a_own[listed + s] = second[:, tile - width :]
        a_own[slots + s] = jnp.concatenate([first[:, width:], second[:, : tile - width]], axis=1)
    keep_list = pltpu.make_async_copy(list_own, list_all.at[row], l_own)
    keep_a = pltpu.make_async_copy(a_own, cut(a_all, row, 0, stored), a_sem)
    pl.semaphore_wait(barrier, 3 + inner)

    @pl.when(z + 1 < lines)
    def _():
        up(0, a_own).start()

    @pl.when(z >= 1)
    def _():
        down(0, a_own).start()

    over_y(z, a_own).start()
    over_core(z, True, a_own).start()
    if share[0]:
        side_core(z, True, a_own).start()
    for c in range(chunks):
        for off in range(1, col_devices):

            @pl.loop(0, tiles)
            def _(t):
                send_c(c, off, t).start()

        if c == 0:
            keep_list.start()
            keep_a.start()
            load_b.start()

        @pl.loop(0, tiles)
        def _(t):
            own_c(c, t).start()

    for n in range(lines):
        meet(rounds.at[n])

    @pl.loop(1, row_devices)
    def _(off):
        send_list(off).start()

    load_b.wait()
    move_table = pltpu.make_async_copy(table, picks, t_sem)
    now, later = [[0], [1], [2]], [[(3, straight), (3, turned)], [(4, straight)], [(5, straight), (4, turned), (5, turned)]]
    relayed = 0
    for c in range(chunks):
        if relayed < lines - 1:
            relay(relayed)
            relayed += 1

        @pl.loop(0, tiles)
        def _(t):
            own_c(c, t).wait()
            for off in range(1, col_devices):
                send_c(c, off, t).wait_recv()

        @pl.loop(0, chips)
        def _(i):
            multiply(c, pair(i))

            @pl.when(i > 0)
            def _():
                for u in now[c]:
                    send_pair(functools.partial(send_x, u), i - 1)

        for u in now[c]:
            send_x(u, partner_off, partner).start()
            own_x(u).start()
        for u, steps in later[c]:
            send_later(u, steps)
        if c == 0:
            keep_list.wait()

            @pl.loop(1, row_devices)
            def _(off):
                send_list(off).wait_recv()

            make_table()
            move_table.start()
            cross(z)

    for step in range(relayed, lines - 1):
        relay(step)
    for d in range(1, lines):
        at_distance(d, cross)
    others(side_arrived)
    keep_a.wait()
    move_table.wait()
    for at_z in range(lines):
        for same in (True, False):
            at, sem = block(at_z, y if same else 1 - y, 1 - core), place(at_z, same)[1]
            arrived(at, main(same), core_recv.at[sem], core_send.at[sem])
            if gets(same)[1]:
                arrived(at, gets(same), core_side_recv.at[sem], core_side.at[sem])
    for s in range(subs):
        for u in range(s * chunks, (s + 1) * chunks):
            own_x(u).wait()

            @pl.loop(1, row_devices)
            def _(off):
                send_x(u, off, lax.rem(row + off, row_devices)).wait_recv()

        prepare(s)
        contract(s)

        @pl.loop(0, chips)
        def _(i):
            assemble(s, pair(i))

            @pl.when(i > 0)
            def _():
                send_pair(functools.partial(send_own, s), i - 1)

        send_own(s, partner_off, partner).start()
        for off in range(1, col_devices):
            send_mirror(s, off).start()
        stay_own(s).start()
        stay_mirror(s).start()

    for step in range(lines - 1):

        @pl.when((z - step >= 0) & (z + 1 < lines))
        def _():
            up(step).wait_send()

        @pl.when((z + step < lines) & (z >= 1))
        def _():
            down(step).wait_send()

    for at_z in range(lines):
        over_y(at_z).wait_send()
        for same in (True, False):
            over_core(at_z, same).wait_send()
            if gets(same)[1]:
                side_core(at_z, same).wait_send()

    others(lambda at_z, same: side_x(at_z, same).wait_send())
    for c in range(chunks):
        for off in range(1, col_devices):

            @pl.loop(0, tiles)
            def _(t):
                send_c(c, off, t).wait_send()

    @pl.loop(1, row_devices)
    def _(off):
        peer = lax.rem(row + off, row_devices)
        send_list(off).wait_send()
        for u in range(len(units)):
            send_x(u, off, peer).wait_send()

    for s in range(subs):
        stay_own(s).wait()
        stay_mirror(s).wait()
        for off in range(1, col_devices):
            send_mirror(s, off).wait()

        @pl.loop(1, row_devices)
        def _(off):
            send_own(s, off, lax.rem(row + off, row_devices)).wait()


def fused(c_matrix, beta_values, beta_rows, alpha_tiles, alpha_rows, row_devices, col_devices, subs, share):
    rows, columns = c_matrix.shape
    _, tiles, listed, width, _ = beta_values.shape
    slots, tile, _ = alpha_tiles.shape
    groups = alpha_rows.shape[1]
    chunks, strip = rows // width, columns // row_devices
    part, units, lines = strip // subs, rows // width * subs, row_devices // 4
    stored = slots * tile // width
    row_peers, col_peers = row_devices - 1, col_devices - 1
    dma, half = pltpu.SemaphoreType.DMA, jnp.bfloat16
    anywhere = pl.BlockSpec(memory_space=pl.ANY)
    scalars = pl.BlockSpec(memory_space=pltpu.SMEM)
    return pl.pallas_call(
        functools.partial(fused_kernel, chunks, subs, share),
        in_specs=[scalars, scalars, anywhere, anywhere, pl.BlockSpec(memory_space=pltpu.VMEM)],
        out_specs=[anywhere, anywhere],
        out_shape=[
            jax.ShapeDtypeStruct((row_devices, strip, groups * tile), half),
            jax.ShapeDtypeStruct((col_devices, strip, row_devices * tile), half),
        ],
        scratch_shapes=[pltpu.VMEM((col_devices * tiles, width, width), half)] * chunks
        + [pltpu.VMEM((columns, width), half)] * chunks
        + [pltpu.VMEM((row_devices * groups, part, 2 * width), half)] * subs
        + [
            pltpu.VMEM((tiles, listed * width, width), half),
            pltpu.VMEM((stored, tile, width), half),
            pltpu.VMEM((row_devices * stored, tile, width), half),
            pltpu.VMEM((chunks, row_devices, strip, width), half),
            pltpu.VMEM((row_devices * slots, part, tile), half),
            pltpu.VMEM((subs, row_devices, part, groups * tile), half),
            pltpu.VMEM((subs, groups, part, row_devices * tile), half),
            pltpu.VMEM((8, width), jnp.int32),
            pltpu.VMEM((row_devices, 8, width), jnp.int32),
            pltpu.VMEM((8, width), jnp.int32),
            pltpu.SMEM((8, width), jnp.int32),
            dma((1,)),
            dma((chunks, tiles)), dma((chunks, col_peers, tiles)), dma((chunks, col_peers, tiles)),
            dma((units,)), dma((units, row_peers)), dma((units, row_peers)),
            dma, dma((row_peers,)), dma((row_peers,)), dma,
        ]
        + [dma((lines - 1,))] * 4
        + [dma((lines,))] * 2
        + [dma((2 * lines,))] * 6
        + [
            dma,
            dma((subs,)), dma((subs, row_peers)), dma((subs, row_peers)),
            dma((subs,)), dma((subs, col_peers)), dma((subs, col_peers)),
            pltpu.SemaphoreType.REGULAR((lines,)),
        ],
        compiler_params=pltpu.CompilerParams(
            collective_id=0, has_side_effects=True, vmem_limit_bytes=48 << 20
        ),
        cost_estimate=pl.CostEstimate(flops=1 << 37, bytes_accessed=1 << 28, transcendentals=0),
        name="fused",
    )(
        jnp.transpose(beta_rows, (2, 0, 1)), alpha_rows, c_matrix,
        beta_values.reshape(tiles, listed * width, width), alpha_tiles,
    )


def per_device(c_matrix, beta_values, beta_rows, alpha_values, alpha_rows, gaps):
    row_devices, col_devices = lax.axis_size("row"), lax.axis_size("col")
    groups, stretch, columns = c_matrix.shape
    pairs, _, _, listed, tile, _ = alpha_values.shape
    rows, width = groups * stretch, beta_values.shape[-1]
    c_rows = c_matrix.reshape(rows, columns)
    alpha_tiles = alpha_values.reshape(pairs * groups, listed, tile, tile)
    strip, subs = columns // row_devices, 2
    own_kernels = pairs == 1 and groups == 2 and stretch == tile and 2 * tile == 3 * width
    own_kernels = own_kernels and row_devices % 4 == 0 and row_devices * groups * listed == width
    own_kernels = own_kernels and strip % (16 * subs) == 0 and 2 * strip % width == 0
    if own_kernels:
        own, mirror = fused(
            c_rows, beta_values, beta_rows, alpha_tiles.reshape(-1, tile, tile), alpha_rows,
            row_devices, col_devices, subs, SHARE,
        )
    else:
        rows_all = lax.all_gather(alpha_rows.reshape(pairs * groups, listed), "row")
        alpha_all = lax.all_gather(alpha_tiles, "row")
        xt = beta_products(lax.all_gather(c_rows, "col"), beta_values, beta_rows)
        xt = jnp.moveaxis(xt.reshape(pairs, row_devices, stretch, rows), 1, 0)
        x_strip = lax.all_to_all(xt, "row", 0, 0)[None]
        own, mirror = alpha_products(alpha_all, rows_all, x_strip, groups)
        own = lax.all_to_all(own, "row", 0, 0)
        mirror = lax.all_to_all(mirror, "col", 0, 0)
    out = final(
        own.reshape(columns, groups * stretch),
        mirror.reshape(groups * stretch, columns),
        gaps.reshape(groups * stretch, columns),
    )
    return out.reshape(gaps.shape)


def solution(mesh):
    placed = (
        P(None, "row", "col"),
        P(None, "col", None, None, None),
        P(None, "col", None),
        P(None, None, "row", None, None, None),
        P(None, None, "row", None),
        P(None, "row", "col"),
    )
    return jax.shard_map(
        per_device, mesh=mesh, in_specs=placed, out_specs=P(None, "row", "col"), check_vma=False
    )
```

```python
import functools

import jax
import jax.numpy as jnp
from jax import lax
from jax.experimental import pallas as pl
from jax.experimental.pallas import tpu as pltpu
from jax.sharding import PartitionSpec as P

CONTRACT_LAST = (((1,), (1,)), ((), ()))
SHARE = (2, 2)


def beta_kernel(listed, held, rows_ref, c_ref, b_ref, xt_ref):
    k, j = pl.program_id(0), pl.program_id(1)
    width = b_ref.shape[-1]
    picked = []
    for z in range(listed):
        tile = rows_ref[k, j, z]
        owner = tile // held
        start = pl.multiple_of((tile - owner * held) * width, width)
        picked.append(c_ref[owner, :, pl.ds(start, width)])
    lhs = b_ref[0, 0].reshape(listed * width, width)
    product = lax.dot_general(
        lhs, jnp.concatenate(picked, axis=1), (((0,), (1,)), ((), ())),
        preferred_element_type=jnp.float32,
    )
    xt_ref[0] = product.astype(xt_ref.dtype)


def beta_products(gathered, beta_values, beta_rows):
    pairs, tiles, listed, width, _ = beta_values.shape
    owners, rows, columns = gathered.shape
    return pl.pallas_call(
        functools.partial(beta_kernel, listed, columns // width),
        grid_spec=pltpu.PrefetchScalarGridSpec(
            num_scalar_prefetch=1,
            grid=(pairs, tiles),
            in_specs=[
                pl.BlockSpec((owners, rows, columns), lambda k, j, s: (0, 0, 0)),
                pl.BlockSpec((1, 1, listed, width, width), lambda k, j, s: (k, j, 0, 0, 0)),
            ],
            out_specs=pl.BlockSpec((1, width, rows), lambda k, j, s: (k, j, 0)),
        ),
        out_shape=jax.ShapeDtypeStruct((pairs, tiles * width, rows), jnp.bfloat16),
        compiler_params=pltpu.CompilerParams(vmem_limit_bytes=56 << 20),
        name="beta_products",
    )(beta_rows, gathered, beta_values)


def alpha_kernel(groups, rows_ref, a_ref, x_ref, own_ref, mirror_ref, acc_ref):
    r = pl.program_id(0)
    row_devices = pl.num_programs(0)
    pairs = x_ref.shape[2]
    listed, tile = rows_ref.shape[2], acc_ref.shape[1]

    @pl.when(r == 0)
    def _():
        acc_ref[...] = jnp.zeros_like(acc_ref)

    for i in range(x_ref.shape[1]):
        at = r * x_ref.shape[1] + i
        for k in range(pairs):
            parts = [x_ref[c, i, k] for c in range(x_ref.shape[0])]
            merged = jnp.concatenate(parts, axis=1) if len(parts) > 1 else parts[0]
            for g in range(groups):
                x = merged[:, g * tile : (g + 1) * tile]
                slot = k * groups + g

                @pl.loop(0, listed)
                def _(z):
                    acc_ref[rows_ref[at, slot, z]] += lax.dot_general(
                        a_ref[i, slot, z], x, CONTRACT_LAST, preferred_element_type=jnp.float32
                    )

    @pl.when(r == row_devices - 1)
    def _():
        count = acc_ref.shape[0] // groups
        for g in range(groups):
            for to in range(count):
                turned = acc_ref[g * count + to].astype(own_ref.dtype).T
                own_ref[to, :, g * tile : (g + 1) * tile] = turned
                mirror_ref[g, :, to * tile : (to + 1) * tile] = turned


def alpha_products(alpha_all, rows_all, x_strip, groups):
    row_devices, rest = alpha_all.shape[0], alpha_all.shape[1:]
    tile = x_strip.shape[0] * x_strip.shape[-1] // groups
    per = 1
    chunks, _, pairs, strip, chunk = x_strip.shape
    return pl.pallas_call(
        functools.partial(alpha_kernel, groups),
        grid_spec=pltpu.PrefetchScalarGridSpec(
            num_scalar_prefetch=1,
            grid=(row_devices // per,),
            in_specs=[
                pl.BlockSpec((per,) + rest, lambda r, s: (r,) + (0,) * len(rest)),
                pl.BlockSpec((chunks, per, pairs, strip, chunk), lambda r, s: (0, r, 0, 0, 0)),
            ],
            out_specs=[
                pl.BlockSpec((row_devices, strip, groups * tile), lambda r, s: (0, 0, 0)),
                pl.BlockSpec((groups, strip, row_devices * tile), lambda r, s: (0, 0, 0)),
            ],
            scratch_shapes=[pltpu.VMEM((groups * row_devices, tile, strip), jnp.float32)],
        ),
        out_shape=[
            jax.ShapeDtypeStruct((row_devices, strip, groups * tile), jnp.bfloat16),
            jax.ShapeDtypeStruct((groups, strip, row_devices * tile), jnp.bfloat16),
        ],
        compiler_params=pltpu.CompilerParams(vmem_limit_bytes=56 << 20),
        name="alpha_products",
    )(rows_all, alpha_all, x_strip)


def final_kernel(block, own, mirror, gaps, out_ref, out, out_sem):
    steps = out.shape[1] // block

    def store(i):
        span = pl.ds(i * block, block)
        return pltpu.make_async_copy(out.at[:, span], out_ref.at[:, span], out_sem.at[i])

    for i in range(steps):
        span = slice(i * block, (i + 1) * block)
        turned = own[span, :].T.astype(jnp.float32)
        out[:, span] = (turned + mirror[:, span].astype(jnp.float32)) / gaps[:, span]
        store(i).start()
    for i in range(steps):
        store(i).wait()


def final(own, mirror, gaps):
    rows, columns = gaps.shape
    block = next(n for n in (384, 256, 128) if columns % n == 0)
    whole = pl.BlockSpec(memory_space=pltpu.VMEM)
    return pl.pallas_call(
        functools.partial(final_kernel, block),
        in_specs=[whole] * 3,
        out_specs=pl.BlockSpec(memory_space=pl.ANY),
        out_shape=jax.ShapeDtypeStruct((rows, columns), jnp.float32),
        scratch_shapes=[
            pltpu.VMEM(gaps.shape, gaps.dtype), pltpu.SemaphoreType.DMA((columns // block,)),
        ],
        compiler_params=pltpu.CompilerParams(vmem_limit_bytes=20 << 20),
        name="final",
    )(own, mirror, gaps)


def remote(src, dst, send_sem, recv_sem, axis, peer):
    return pltpu.make_async_remote_copy(
        src_ref=src, dst_ref=dst, send_sem=send_sem, recv_sem=recv_sem,
        device_id={axis: peer}, device_id_type=pl.DeviceIdType.MESH,
    )


def fused_kernel(chunks, subs, share, rows_ref, lists_ref, c_ref, b_ref, alpha_ref, own_ref, mirror_ref, *scratch):
    held, sent, xt = scratch[:chunks], scratch[chunks : 2 * chunks], scratch[2 * chunks : 2 * chunks + subs]
    (b_own, a_own, a_all, xr, stack, own_out, mirror_out, list_own, list_all, table, picks,
     load_sem, c_own, c_send, c_recv, x_own, x_send, x_recv, l_own, l_send, l_recv, a_sem,
     up_send, up_recv, down_send, down_recv, y_send, y_recv, core_send, core_recv,
     x_side, x_side_recv, core_side, core_side_recv, t_sem,
     o_own, o_send, o_recv, m_own, m_send, m_recv, rounds) = scratch[2 * chunks + subs :]
    row_devices, row = lax.axis_size("row"), lax.axis_index("row")
    col_devices, col = lax.axis_size("col"), lax.axis_index("col")
    rows, columns = c_ref.shape
    tiles, depth, width = b_own.shape
    listed_b = depth // width
    slots, tile, _ = alpha_ref.shape
    groups = lists_ref.shape[1]
    listed = slots // groups
    chunk, strip = rows // chunks, columns // row_devices
    part = strip // subs
    chips = row_devices // 2
    per = tiles // chips
    stored = a_own.shape[0]
    lines = row_devices // 4
    chip, core = row // 2, lax.rem(row, 2)
    z, y = row // 4, lax.rem(chip, 2)
    units = [(c, s * part, part) for s in range(subs) for c in range(chunks)]
    straight, turned = range(2, chips, 2), range(1, chips, 2)

    def own_c(c, t):
        return pltpu.make_async_copy(
            c_ref.at[pl.ds(c * chunk, chunk), pl.ds(pl.multiple_of(t * width, width), width)],
            held[c].at[col * tiles + t], c_own.at[c, t],
        )

    def send_c(c, off, t):
        return remote(
            c_ref.at[pl.ds(c * chunk, chunk), pl.ds(pl.multiple_of(t * width, width), width)],
            held[c].at[col * tiles + t], c_send.at[c, off - 1, t], c_recv.at[c, off - 1, t],
            "col", lax.rem(col + off, col_devices),
        )

    def send_x(u, off, peer):
        c, first, size = units[u]
        start = pl.multiple_of(peer * strip + first, 16)
        return remote(
            sent[c].at[pl.ds(start, size), :], xr.at[c, row, pl.ds(first, size), :],
            x_send.at[u, off - 1], x_recv.at[u, off - 1], "row", peer,
        )

    def own_x(u):
        c, first, size = units[u]
        start = pl.multiple_of(row * strip + first, 16)
        return pltpu.make_async_copy(
            sent[c].at[pl.ds(start, size), :], xr.at[c, row, pl.ds(first, size), :], x_own.at[u]
        )

    def send_own(s, off, peer):
        return remote(
            own_out.at[s, peer], own_ref.at[row, pl.ds(s * part, part), :],
            o_send.at[s, off - 1], o_recv.at[s, off - 1], "row", peer,
        )

    def stay_own(s):
        return pltpu.make_async_copy(
            own_out.at[s, row], own_ref.at[row, pl.ds(s * part, part), :], o_own.at[s]
        )

    def send_mirror(s, off):
        peer = lax.rem(col + off, col_devices)
        return remote(
            mirror_out.at[s, peer], mirror_ref.at[col, pl.ds(s * part, part), :],
            m_send.at[s, off - 1], m_recv.at[s, off - 1], "col", peer,
        )

    def stay_mirror(s):
        return pltpu.make_async_copy(
            mirror_out.at[s, col], mirror_ref.at[col, pl.ds(s * part, part), :], m_own.at[s]
        )

    def send_list(off):
        return remote(
            list_own, list_all.at[row], l_send.at[off - 1], l_recv.at[off - 1], "row",
            lax.rem(row + off, row_devices),
        )

    def reach(i):
        odd = lax.rem(i, 2)
        return lax.rem(i + 1, chips)

    def pair(i):
        return lax.rem(chip + reach(i), chips)

    def send_pair(send, i):
        for e in range(2):
            send(2 * reach(i) + e - core, 2 * pair(i) + e).start()

    def block(at_z, at_y, at_core):
        return (at_z * 2 + at_y) * 2 + at_core

    def neighbours(act):
        act("col", 1 - col)
        act("row", block(z, y, 1 - core))
        act("row", block(z, 1 - y, core))

        @pl.when(z >= 1)
        def _():
            act("row", block(z - 1, y, core))

        @pl.when(z + 1 < lines)
        def _():
            act("row", block(z + 1, y, core))

    inner = lax.min(z, 1) + lax.min(lines - 1 - z, 1)

    def signal_near(sem):
        def act(axis, peer):
            pl.semaphore_signal(
                sem, inc=1, device_id={axis: peer}, device_id_type=pl.DeviceIdType.MESH
            )

        neighbours(act)

    def meet(sem):
        signal_near(sem)
        pl.semaphore_wait(sem, 3 + inner)

    def send_later(u, steps):
        for o in steps:
            for e in range(2):
                send_x(u, 2 * o + e - core, 2 * lax.rem(chip + o, chips) + e).start()
        if steps == straight:
            send_x(u, partner_off, partner).start()
            own_x(u).start()

    partner, partner_off = row + 1 - 2 * core, 1 + core * (row_devices - 2)

    def cut(ref, at, first, size):
        return ref.at[pl.ds(at * stored + first, size)]

    def hand(at, first, size, send_sem, recv_sem, peer, axis="row", source=None):
        held_part = cut(a_all, at, first, size)
        if source is not None:
            held_part = source.at[pl.ds(first, size)]
        return remote(held_part, cut(a_all, at, first, size), send_sem, recv_sem, axis, peer)

    def main(same):
        part_share = share[0] if same else share[1]
        return col * part_share, stored - part_share

    def gives(same):
        part_share = share[0] if same else share[1]
        return col * (stored - part_share), part_share

    def gets(same):
        part_share = share[0] if same else share[1]
        return (1 - col) * (stored - part_share), part_share

    def place(at_z, same):
        at_y = y if same else 1 - y
        return block(at_z, at_y, core), at_z * 2 + at_y

    other_core = block(z, y, 1 - core)

    def up(step, source=None):
        at = block(z - step, y, core)
        return hand(at, *main(True), up_send.at[step], up_recv.at[step], block(z + 1, y, core), source=source)

    def down(step, source=None):
        at = block(z + step, y, core)
        return hand(at, *main(True), down_send.at[step], down_recv.at[step], block(z - 1, y, core), source=source)

    def over_y(at_z, source=None):
        at = block(at_z, y, core)
        return hand(at, *main(False), y_send.at[at_z], y_recv.at[at_z], block(z, 1 - y, core), source=source)

    def over_core(at_z, same, source=None):
        at, sem = place(at_z, same)
        return hand(at, *main(same), core_send.at[sem], core_recv.at[sem], other_core, source=source)

    def side_x(at_z, same):
        at, sem = place(at_z, same)
        return hand(at, *gives(same), x_side.at[sem], x_side_recv.at[sem], 1 - col, "col")

    def side_core(at_z, same, source=None):
        at, sem = place(at_z, same)
        return hand(at, *gets(same), core_side.at[sem], core_side_recv.at[sem], other_core, source=source)

    def arrived(at, span, recv_sem, send_sem):
        hand(at, *span, send_sem, recv_sem, other_core).wait_recv()

    def spread(at_z, same):
        over_core(at_z, same).start()
        if gives(same)[1]:
            side_x(at_z, same).start()

    def relay(step):
        @pl.when(z - 1 - step >= 0)
        def _():
            arrived(block(z - 1 - step, y, core), main(True), up_recv.at[step], up_send.at[step])
            if step + 1 < lines - 1:

                @pl.when(z + 1 < lines)
                def _():
                    up(step + 1).start()

            over_y(z - 1 - step).start()
            spread(z - 1 - step, True)

        @pl.when(z + 1 + step < lines)
        def _():
            arrived(block(z + 1 + step, y, core), main(True), down_recv.at[step], down_send.at[step])
            if step + 1 < lines - 1:

                @pl.when(z >= 1)
                def _():
                    down(step + 1).start()

            over_y(z + 1 + step).start()
            spread(z + 1 + step, True)

    def at_distance(d, body):
        @pl.when(z + d < lines)
        def _():
            body(z + d)

        @pl.when(z >= d)
        def _():
            body(z - d)

    def cross(at_z):
        arrived(block(at_z, 1 - y, core), main(False), y_recv.at[at_z], y_send.at[at_z])
        spread(at_z, False)

    def others(body):
        for d in range(lines):
            for same in (True, False):
                if gives(same)[1] and d > 0:
                    at_distance(d, functools.partial(body, same=same))
                elif gives(same)[1] and not same:
                    body(z, same)

    def side_arrived(at_z, same):
        side_x(at_z, same).wait_recv()
        side_core(at_z, same).start()

    def multiply(c, group):
        for q in range(per):
            j = group * per + q
            picked = [held[c][rows_ref[s, 0, j]] for s in range(listed_b)]
            product = lax.dot_general(
                b_own[j], jnp.concatenate(picked, axis=1), (((0,), (1,)), ((), ())),
                preferred_element_type=jnp.float32,
            )
            sent[c][pl.ds(pl.multiple_of(j * width, width), width), :] = product.astype(jnp.bfloat16)

    def make_table():
        total = list_all[0]
        for r in range(1, row_devices):
            total = total + list_all[r]
        square = (width, width)
        by_lane = jnp.broadcast_to(total[0:1], square)
        lane = lax.broadcasted_iota(jnp.int32, square, 1)
        sub = lax.broadcasted_iota(jnp.int32, square, 0)
        keys = by_lane * width + lane

        def count(mask):
            return jnp.sum(jnp.where(mask, 1, 0), axis=0, keepdims=True)

        rank = jnp.broadcast_to(count(keys.T < keys), square)
        hit = rank.T == lane
        by_sub = by_lane.T
        order = jnp.sum(jnp.where(hit, sub, 0), axis=0, keepdims=True)
        target = jnp.sum(jnp.where(hit, by_sub, 0), axis=0, keepdims=True)
        began = count(by_sub < target)
        source, slot = order // slots, order % slots
        table[0:1, :] = source * stored + slot
        table[1:2, :] = source * stored + slots + slot % listed
        table[2:3, :] = order // listed
        table[3:4, :] = jnp.where(lane[0:1] > began, 1, 0)
        table[4:5, :] = count(by_sub <= lane) - 1
        table[5:8, :] = jnp.zeros((3, width), jnp.int32)

    def prepare(s):
        lane = lax.broadcasted_iota(jnp.int32, (part, width), 1)
        low = lane < width // 2

        @pl.loop(0, row_devices)
        def _(r):
            cut = pl.ds(s * part, part)
            middle = xr[1, r, cut, :]
            blank = jnp.zeros_like(middle)
            xt[s][r * groups, :, 0:width] = xr[0, r, cut, :]
            xt[s][r * groups, :, width : 2 * width] = jnp.where(low, middle, blank)
            xt[s][r * groups + 1, :, 0:width] = xr[2, r, cut, :]
            xt[s][r * groups + 1, :, width : 2 * width] = jnp.where(low, blank, middle)

    def contract(s):
        def step(p, run):
            weights = jnp.concatenate([a_all[picks[0, p]], a_all[picks[1, p]]], axis=1)
            product = lax.dot_general(
                xt[s][picks[2, p]], weights, CONTRACT_LAST, preferred_element_type=jnp.float32
            )
            run = product + run * picks[3, p].astype(jnp.float32)
            stack[p] = run.astype(stack.dtype)
            return run

        lax.fori_loop(0, width, step, jnp.zeros((part, tile), jnp.float32), unroll=32)

    def assemble(s, k):
        found = [[stack[picks[4, g * row_devices + 2 * k + e]] for e in range(2)] for g in range(groups)]
        for e in range(2):
            own_out[s, 2 * k + e] = jnp.concatenate([found[g][e] for g in range(groups)], axis=1)
        for g in range(groups):
            start = pl.multiple_of(k * 2 * tile, width)
            mirror_out[s, g, :, pl.ds(start, 2 * tile)] = jnp.concatenate(found[g], axis=1)

    load_b = pltpu.make_async_copy(b_ref, b_own, load_sem.at[0])
    barrier = pltpu.get_barrier_semaphore()
    signal_near(barrier)
    lane = lax.broadcasted_iota(jnp.int32, list_own.shape, 1)
    mine = jnp.zeros(list_own.shape, jnp.int32)
    for g in range(groups):
        for s in range(listed):
            mine = jnp.where(lane == row * slots + g * listed + s, lists_ref[0, g, 0, s], mine)
    list_own[...] = mine
    for s in range(listed):
        first, second = alpha_ref[s], alpha_ref[listed + s]
        a_own[s] = first[:, :width]
        a_own[listed + s] = second[:, tile - width :]
        a_own[slots + s] = jnp.concatenate([first[:, width:], second[:, : tile - width]], axis=1)
    keep_list = pltpu.make_async_copy(list_own, list_all.at[row], l_own)
    keep_a = pltpu.make_async_copy(a_own, cut(a_all, row, 0, stored), a_sem)
    pl.semaphore_wait(barrier, 3 + inner)

    @pl.when(z + 1 < lines)
    def _():
        up(0, a_own).start()

    @pl.when(z >= 1)
    def _():
        down(0, a_own).start()

    over_y(z, a_own).start()
    over_core(z, True, a_own).start()
    if share[0]:
        side_core(z, True, a_own).start()
    for c in range(chunks):
        for off in range(1, col_devices):

            @pl.loop(0, tiles)
            def _(t):
                send_c(c, off, t).start()

        if c == 0:
            keep_list.start()
            keep_a.start()
            load_b.start()

        @pl.loop(0, tiles)
        def _(t):
            own_c(c, t).start()

    for n in range(lines):
        meet(rounds.at[n])

    @pl.loop(1, row_devices)
    def _(off):
        send_list(off).start()

    load_b.wait()
    move_table = pltpu.make_async_copy(table, picks, t_sem)
    now, later = [[0], [1], [2]], [[(3, straight), (3, turned)], [(4, straight)], [(5, straight), (4, turned), (5, turned)]]
    relayed = 0
    for c in range(chunks):
        if relayed < lines - 1:
            relay(relayed)
            relayed += 1

        @pl.loop(0, tiles)
        def _(t):
            own_c(c, t).wait()
            for off in range(1, col_devices):
                send_c(c, off, t).wait_recv()

        @pl.loop(0, chips)
        def _(i):
            multiply(c, pair(i))

            @pl.when(i > 0)
            def _():
                for u in now[c]:
                    send_pair(functools.partial(send_x, u), i - 1)

        for u in now[c]:
            send_x(u, partner_off, partner).start()
            own_x(u).start()
        for u, steps in later[c]:
            send_later(u, steps)
        if c == 0:
            keep_list.wait()

            @pl.loop(1, row_devices)
            def _(off):
                send_list(off).wait_recv()

            make_table()
            move_table.start()
            cross(z)

    for step in range(relayed, lines - 1):
        relay(step)
    for d in range(1, lines):
        at_distance(d, cross)
    others(side_arrived)
    keep_a.wait()
    move_table.wait()
    for at_z in range(lines):
        for same in (True, False):
            at, sem = block(at_z, y if same else 1 - y, 1 - core), place(at_z, same)[1]
            arrived(at, main(same), core_recv.at[sem], core_send.at[sem])
            if gets(same)[1]:
                arrived(at, gets(same), core_side_recv.at[sem], core_side.at[sem])
    for s in range(subs):
        for u in range(s * chunks, (s + 1) * chunks):
            own_x(u).wait()

            @pl.loop(1, row_devices)
            def _(off):
                send_x(u, off, lax.rem(row + off, row_devices)).wait_recv()

        prepare(s)
        contract(s)

        @pl.loop(0, chips)
        def _(i):
            assemble(s, pair(i))

            @pl.when(i > 0)
            def _():
                send_pair(functools.partial(send_own, s), i - 1)

        send_own(s, partner_off, partner).start()
        for off in range(1, col_devices):
            send_mirror(s, off).start()
        stay_own(s).start()
        stay_mirror(s).start()

    for step in range(lines - 1):

        @pl.when((z - step >= 0) & (z + 1 < lines))
        def _():
            up(step).wait_send()

        @pl.when((z + step < lines) & (z >= 1))
        def _():
            down(step).wait_send()

    for at_z in range(lines):
        over_y(at_z).wait_send()
        for same in (True, False):
            over_core(at_z, same).wait_send()
            if gets(same)[1]:
                side_core(at_z, same).wait_send()

    others(lambda at_z, same: side_x(at_z, same).wait_send())
    for c in range(chunks):
        for off in range(1, col_devices):

            @pl.loop(0, tiles)
            def _(t):
                send_c(c, off, t).wait_send()

    @pl.loop(1, row_devices)
    def _(off):
        peer = lax.rem(row + off, row_devices)
        send_list(off).wait_send()
        for u in range(len(units)):
            send_x(u, off, peer).wait_send()

    for s in range(subs):
        stay_own(s).wait()
        stay_mirror(s).wait()
        for off in range(1, col_devices):
            send_mirror(s, off).wait()

        @pl.loop(1, row_devices)
        def _(off):
            send_own(s, off, lax.rem(row + off, row_devices)).wait()


def fused(c_matrix, beta_values, beta_rows, alpha_tiles, alpha_rows, row_devices, col_devices, subs, share):
    rows, columns = c_matrix.shape
    _, tiles, listed, width, _ = beta_values.shape
    slots, tile, _ = alpha_tiles.shape
    groups = alpha_rows.shape[1]
    chunks, strip = rows // width, columns // row_devices
    part, units, lines = strip // subs, rows // width * subs, row_devices // 4
    stored = slots * tile // width
    row_peers, col_peers = row_devices - 1, col_devices - 1
    dma, half = pltpu.SemaphoreType.DMA, jnp.bfloat16
    anywhere = pl.BlockSpec(memory_space=pl.ANY)
    scalars = pl.BlockSpec(memory_space=pltpu.SMEM)
    return pl.pallas_call(
        functools.partial(fused_kernel, chunks, subs, share),
        in_specs=[scalars, scalars, anywhere, anywhere, pl.BlockSpec(memory_space=pltpu.VMEM)],
        out_specs=[anywhere, anywhere],
        out_shape=[
            jax.ShapeDtypeStruct((row_devices, strip, groups * tile), half),
            jax.ShapeDtypeStruct((col_devices, strip, row_devices * tile), half),
        ],
        scratch_shapes=[pltpu.VMEM((col_devices * tiles, width, width), half)] * chunks
        + [pltpu.VMEM((columns, width), half)] * chunks
        + [pltpu.VMEM((row_devices * groups, part, 2 * width), half)] * subs
        + [
            pltpu.VMEM((tiles, listed * width, width), half),
            pltpu.VMEM((stored, tile, width), half),
            pltpu.VMEM((row_devices * stored, tile, width), half),
            pltpu.VMEM((chunks, row_devices, strip, width), half),
            pltpu.VMEM((row_devices * slots, part, tile), half),
            pltpu.VMEM((subs, row_devices, part, groups * tile), half),
            pltpu.VMEM((subs, groups, part, row_devices * tile), half),
            pltpu.VMEM((8, width), jnp.int32),
            pltpu.VMEM((row_devices, 8, width), jnp.int32),
            pltpu.VMEM((8, width), jnp.int32),
            pltpu.SMEM((8, width), jnp.int32),
            dma((1,)),
            dma((chunks, tiles)), dma((chunks, col_peers, tiles)), dma((chunks, col_peers, tiles)),
            dma((units,)), dma((units, row_peers)), dma((units, row_peers)),
            dma, dma((row_peers,)), dma((row_peers,)), dma,
        ]
        + [dma((lines - 1,))] * 4
        + [dma((lines,))] * 2
        + [dma((2 * lines,))] * 6
        + [
            dma,
            dma((subs,)), dma((subs, row_peers)), dma((subs, row_peers)),
            dma((subs,)), dma((subs, col_peers)), dma((subs, col_peers)),
            pltpu.SemaphoreType.REGULAR((lines,)),
        ],
        compiler_params=pltpu.CompilerParams(
            collective_id=0, has_side_effects=True, vmem_limit_bytes=48 << 20
        ),
        cost_estimate=pl.CostEstimate(flops=1 << 37, bytes_accessed=1 << 28, transcendentals=0),
        name="fused",
    )(
        jnp.transpose(beta_rows, (2, 0, 1)), alpha_rows, c_matrix,
        beta_values.reshape(tiles, listed * width, width), alpha_tiles,
    )


def per_device(c_matrix, beta_values, beta_rows, alpha_values, alpha_rows, gaps):
    row_devices, col_devices = lax.axis_size("row"), lax.axis_size("col")
    groups, stretch, columns = c_matrix.shape
    pairs, _, _, listed, tile, _ = alpha_values.shape
    rows, width = groups * stretch, beta_values.shape[-1]
    c_rows = c_matrix.reshape(rows, columns)
    alpha_tiles = alpha_values.reshape(pairs * groups, listed, tile, tile)
    strip, subs = columns // row_devices, 2
    own_kernels = pairs == 1 and groups == 2 and stretch == tile and 2 * tile == 3 * width
    own_kernels = own_kernels and row_devices % 4 == 0 and row_devices * groups * listed == width
    own_kernels = own_kernels and strip % (16 * subs) == 0 and 2 * strip % width == 0
    if own_kernels:
        own, mirror = fused(
            c_rows, beta_values, beta_rows, alpha_tiles.reshape(-1, tile, tile), alpha_rows,
            row_devices, col_devices, subs, SHARE,
        )
    else:
        rows_all = lax.all_gather(alpha_rows.reshape(pairs * groups, listed), "row")
        alpha_all = lax.all_gather(alpha_tiles, "row")
        xt = beta_products(lax.all_gather(c_rows, "col"), beta_values, beta_rows)
        xt = jnp.moveaxis(xt.reshape(pairs, row_devices, stretch, rows), 1, 0)
        x_strip = lax.all_to_all(xt, "row", 0, 0)[None]
        own, mirror = alpha_products(alpha_all, rows_all, x_strip, groups)
        own = lax.all_to_all(own, "row", 0, 0)
        mirror = lax.all_to_all(mirror, "col", 0, 0)
    out = final(
        own.reshape(columns, groups * stretch),
        mirror.reshape(groups * stretch, columns),
        gaps.reshape(groups * stretch, columns),
    )
    return out.reshape(gaps.shape)


def solution(mesh):
    placed = (
        P(None, "row", "col"),
        P(None, "col", None, None, None),
        P(None, "col", None),
        P(None, None, "row", None, None, None),
        P(None, None, "row", None),
        P(None, "row", "col"),
    )
    return jax.shard_map(
        per_device, mesh=mesh, in_specs=placed, out_specs=P(None, "row", "col"), check_vma=False
    )
```
